128 devices in a mesh: blk: 128 (over x, y, z, core).
Axes of the slice: x: 4, y: 4, z: 4, core: 2. Of those that a mesh axis runs over, the one named last changes fastest.
Arguments:
- adjoint: float32 [128, 19, 4096], P('blk'), may hold values from -6 to 6
- velocity: float32 [128, 3, 4096], P('blk'), may hold values from -0.15 to 0.15
- relax: float32 [128, 4096], P('blk'), may hold values from 0.6 to 1.9
- fluid_words: int32 [128, 128], P('blk'), may hold values from -2147483648 to 2147483647, as said below
- neighbours: int32 [128, 18], P('blk'), may hold values from -1 to 127, as said below
- inlet_ids: int32 [16], replicated, may hold values from 0 to 127, as said below
- basis: float32 [8, 16, 256], replicated, may hold values from -0.09375 to 0.09375
Outputs:
- adjoint_prev: float32 [128, 19, 4096], P('blk')
- inlet_grad: float32 [8], replicated
The draws below stay inside these ranges and needn't reach their ends.
Inputs may be any that keep to these rules, and one draw needn't show every extreme that they name: `neighbours`: entry k of a block's row names, as device + slot, the occupied block holding the sites beyond it along the velocity of index k + 1 (entries 0 to 5 faces, 6 to 17 edges), or is -1 where there is none; the named block's device is at most 2 indices from the block's device, and in every draw some block names blocks exactly 2 devices away on both sides. Every device holds one occupied block. `fluid_words`: unoccupied slots have no fluid sites. `inlet_ids`: 16 distinct occupied blocks, as device + slot.
All inputs are finite; a program needn't handle non-finite values.
Results may differ from the reference program's by a relative error of at most 0.0003.
Values sent between devices are 32-bit elements; how exact they have to be, the bound alone decides.
A program may use at most 128 MiB of HBM per device.

```python
import jax
import jax.numpy as jnp
import numpy as np
from jax import lax

SLOTS = 1
EDGE = 16
VELS = 19
NEIGHBOURS = 18
REACH = 2
STEPS = 4
NIN = 16
MODES = 8
SITES = 4096
WORDS = 128
BLOCKS_ALL = 128


def layout_counts(key):
    devices = BLOCKS_ALL // SLOTS
    base = jax.random.fold_in(key, 101)
    counts = jax.random.randint(jax.random.fold_in(base, 1), (devices,), 1, SLOTS + 1, dtype=jnp.int32)
    fullest = jax.random.randint(jax.random.fold_in(base, 2), (), 0, devices, dtype=jnp.int32)
    counts = counts.at[fullest].set(SLOTS)
    counts = counts.at[devices - 1].set(SLOTS)
    block_ids = jnp.arange(BLOCKS_ALL, dtype=jnp.int32)
    occupied = block_ids % SLOTS < counts[block_ids // SLOTS]
    return (counts, occupied)


def draw_neighbours(key, part):
    devices = BLOCKS_ALL // SLOTS
    counts, occupied = layout_counts(key)
    base = jax.random.fold_in(key, 202)
    shape = (BLOCKS_ALL, NEIGHBOURS)
    present = jax.random.randint(jax.random.fold_in(base, 1), shape, 0, 10, dtype=jnp.int32) < 6
    offset = jax.random.randint(jax.random.fold_in(base, 2), shape, -REACH, REACH + 1, dtype=jnp.int32)
    home = (jnp.arange(BLOCKS_ALL, dtype=jnp.int32) // SLOTS)[:, None]
    target = home + offset
    target = jnp.where((target < 0) | (target >= devices), home - offset, target)
    picked = jax.random.randint(jax.random.fold_in(base, 3), shape, 0, 1 << 20, dtype=jnp.int32) % counts[target]
    entry = jnp.where(present & occupied[:, None], target * SLOTS + picked, -1)
    anchor = jax.random.randint(jax.random.fold_in(base, 4), (), REACH, devices - REACH, dtype=jnp.int32)
    entry = entry.at[anchor * SLOTS, 0].set((anchor + REACH) * SLOTS)
    entry = entry.at[anchor * SLOTS, 1].set((anchor - REACH) * SLOTS)
    entry = entry.at[(devices - 1) * SLOTS, 2].set(BLOCKS_ALL - 1)
    entry = entry.at[(devices - 1) * SLOTS, 3].set(-1)
    return entry.astype(jnp.int32)


def draw_fluid_words(key, part):
    counts, occupied = layout_counts(key)
    base = jax.random.fold_in(key, 303)
    first = jax.random.randint(jax.random.fold_in(base, 1), (BLOCKS_ALL, WORDS), -2147483648, 2147483647, dtype=jnp.int32)
    second = jax.random.randint(jax.random.fold_in(base, 2), (BLOCKS_ALL, WORDS), -2147483648, 2147483647, dtype=jnp.int32)
    words = jnp.bitwise_or(first, second)
    words = jnp.where(occupied[:, None], words, 0)
    words = words.at[0, 0].set(2147483647)
    words = words.at[0, 1].set(-2147483648)
    return words.astype(jnp.int32)


def draw_inlet_ids(key, part):
    counts, occupied = layout_counts(key)
    order = jax.random.permutation(jax.random.fold_in(key, 404), BLOCKS_ALL).astype(jnp.int32)
    score = 1 - occupied[order].astype(jnp.int32)
    forced = (order == 0) | (order == BLOCKS_ALL - 1)
    score = jnp.where(forced, -1, score)
    ranked = order[jnp.argsort(score, stable=True)]
    return ranked[:NIN].astype(jnp.int32)


def shard_levels(rng, shape, cuts, low, high):
    factor_of, own = 1.0, jax.random.fold_in(rng, 6)
    for axis_at, shards_of in cuts:
        steps = jnp.exp(jax.random.uniform(jax.random.fold_in(own, axis_at), (shards_of,), jnp.float32, low / len(cuts), high / len(cuts)))
        factor_of = factor_of * jnp.repeat(steps, shape[axis_at] // shards_of).reshape([-1 if axis == axis_at else 1 for axis in range(len(shape))])
    return factor_of


def scatter_about(key, shape, deviation, limit, split=(), held_as=jnp.bfloat16):
    entries = deviation * jax.random.normal(key, shape, jnp.float32)
    if split:
        entries = entries * shard_levels(key, shape, split, -0.22, 0.18)
    return jnp.clip(entries, -limit, limit).astype(held_as)


def setup_inputs(seed: int = 0) -> dict:
    seeds = jax.random.split(jax.random.key(seed), 8)
    adjoint = scatter_about(seeds[0], (BLOCKS_ALL, VELS, SITES), 1.0, 6.0, ((0, 128),), jnp.float32)
    velocity = jnp.clip(jax.random.uniform(seeds[1], (BLOCKS_ALL, 3, SITES), jnp.float32, -0.15, 0.15) * shard_levels(seeds[1], (BLOCKS_ALL, 3, SITES), ((0, 128),), -0.4, 0.0), -0.15, 0.15)
    relax = jnp.clip(0.6 + 1.3 * jax.random.uniform(seeds[2], (BLOCKS_ALL, SITES), jnp.float32) ** shard_levels(seeds[2], (BLOCKS_ALL, SITES), ((0, 128),), -0.2, 0.2), 0.6, 1.9)
    fluid_words = draw_fluid_words(jax.random.fold_in(seeds[7], 71), 0)
    neighbours = draw_neighbours(jax.random.fold_in(seeds[7], 71), 0)
    inlet_ids = draw_inlet_ids(jax.random.fold_in(seeds[7], 71), 0)
    basis = scatter_about(seeds[6], (MODES, NIN, EDGE * EDGE), (NIN * EDGE * EDGE) ** -0.5, 0.09375, (), jnp.float32)
    return dict(adjoint=adjoint, velocity=velocity, relax=relax, fluid_words=fluid_words, neighbours=neighbours, inlet_ids=inlet_ids, basis=basis)


VELOCITIES = np.array([[0, 0, 0], [1, 0, 0], [-1, 0, 0], [0, 1, 0], [0, -1, 0], [0, 0, 1], [0, 0, -1],
                       [1, 1, 0], [-1, -1, 0], [1, -1, 0], [-1, 1, 0], [1, 0, 1], [-1, 0, -1], [1, 0, -1],
                       [-1, 0, 1], [0, 1, 1], [0, -1, -1], [0, 1, -1], [0, -1, 1]], dtype=np.int32)
WEIGHTS = np.array([1.0 / 3.0] + [1.0 / 18.0] * 6 + [1.0 / 36.0] * 12, dtype=np.float32)
OPPOSITE = [0, 2, 1, 4, 3, 6, 5, 8, 7, 10, 9, 12, 11, 14, 13, 16, 15, 18, 17]
PADDING = ((0, 0), (1, 1), (1, 1), (1, 1))


def unpack_flags(words, edge):
    shifts = jnp.arange(32, dtype=jnp.int32)
    bits = jnp.bitwise_and(jnp.right_shift(words[..., None], shifts), 1)
    return bits.reshape(words.shape[:-1] + (edge, edge, edge)).astype(jnp.float32)


def source_cut(direction, edge):
    parts = []
    for component in range(3):
        if direction[component] == 1:
            parts.append(0)
        elif direction[component] == -1:
            parts.append(edge - 1)
        else:
            parts.append(slice(None))
    return tuple(parts)


def ghost_cut(direction, edge):
    parts = []
    for component in range(3):
        if direction[component] == 1:
            parts.append(edge + 1)
        elif direction[component] == -1:
            parts.append(0)
        else:
            parts.append(slice(1, edge + 1))
    return tuple(parts)


def target_cut(direction, edge):
    return tuple(slice(1 + int(direction[component]), edge + 1 + int(direction[component])) for component in range(3))


def needed_regions(population):
    chosen = []
    for neighbour in range(NEIGHBOURS):
        direction = VELOCITIES[neighbour + 1]
        fits = True
        for component in range(3):
            if direction[component] != 0 and direction[component] != VELOCITIES[population][component]:
                fits = False
        if fits:
            chosen.append(neighbour)
    return chosen


def broadcast_rows(values, ndim):
    return values.reshape((-1,) + (1,) * (ndim - 1))


def open_plane(inlet_flag, edge):
    plane = jnp.zeros((inlet_flag.shape[0], edge + 2, edge + 2, edge + 2), jnp.float32)
    return plane.at[:, :, :, 0].set(inlet_flag[:, None, None])


def pull_all(cube, segments, sets_list, fluid_ext, open_ext):
    slots = cube.shape[0]
    results = [cube[:, 0]]
    for population in range(1, VELS):
        field = jnp.pad(cube[:, population], PADDING)
        for neighbour in needed_regions(population):
            position = sets_list[neighbour].index(population)
            field = field.at[(slice(None),) + ghost_cut(VELOCITIES[neighbour + 1], EDGE)].set(segments[neighbour][:, position])
        window = (slice(None),) + target_cut(VELOCITIES[population], EDGE)
        bounced = jnp.where(fluid_ext[window] > 0.5, field[window], cube[:, OPPOSITE[population]])
        results.append(jnp.where(open_ext[window] > 0.5, 0.0, bounced))
    return jnp.stack(results, axis=1).reshape(slots, VELS, -1)


def collide(pulled, velocity, relax, fluid):
    speed_x = velocity[:, 0][:, None, :]
    speed_y = velocity[:, 1][:, None, :]
    speed_z = velocity[:, 2][:, None, :]
    comp_x = VELOCITIES[:, 0].astype(np.float32)[None, :, None]
    comp_y = VELOCITIES[:, 1].astype(np.float32)[None, :, None]
    comp_z = VELOCITIES[:, 2].astype(np.float32)[None, :, None]
    projected = comp_x * speed_x + comp_y * speed_y + comp_z * speed_z
    squared = speed_x * speed_x + speed_y * speed_y + speed_z * speed_z
    equilibrium = 1.0 + 3.0 * projected + 4.5 * projected * projected - 1.5 * squared
    weighted = WEIGHTS[None, :, None] * pulled
    weight_sum = jnp.sum(weighted, axis=1, keepdims=True)
    scalar_part = jnp.sum(weighted * equilibrium, axis=1, keepdims=True)
    factor = weighted * (3.0 + 9.0 * projected)
    vector_x = jnp.sum(factor * comp_x, axis=1, keepdims=True) - 3.0 * speed_x * weight_sum
    vector_y = jnp.sum(factor * comp_y, axis=1, keepdims=True) - 3.0 * speed_y * weight_sum
    vector_z = jnp.sum(factor * comp_z, axis=1, keepdims=True) - 3.0 * speed_z * weight_sum
    offset_part = scalar_part - vector_x * speed_x - vector_y * speed_y - vector_z * speed_z
    rate = relax[:, None, :]
    result = (1.0 - rate) * pulled + rate * (offset_part + vector_x * comp_x + vector_y * comp_y + vector_z * comp_z)
    return result * fluid[:, None, :]


def inlet_layer(cube, fluid_cube):
    layer = jnp.zeros((cube.shape[0], cube.shape[2], cube.shape[3]), jnp.float32)
    for population in range(VELS):
        if VELOCITIES[population][2] == 1:
            layer = layer + 3.0 * float(WEIGHTS[population]) * cube[:, population, :, :, 0]
    return (layer * fluid_cube[:, :, :, 0]).reshape(cube.shape[0], -1)


def reference(adjoint, velocity, relax, fluid_words, neighbours, inlet_ids, basis):
    blocks = adjoint.shape[0]
    fluid_cube = unpack_flags(fluid_words, EDGE)
    fluid_flat = fluid_cube.reshape(blocks, -1)
    present = (neighbours >= 0).astype(jnp.float32)
    clipped = jnp.maximum(neighbours, 0).astype(jnp.int32)
    fluid_ext = jnp.pad(fluid_cube, PADDING)
    for neighbour in range(NEIGHBOURS):
        direction = VELOCITIES[neighbour + 1]
        slab = fluid_cube[(slice(None),) + source_cut(direction, EDGE)][clipped[:, neighbour]]
        fluid_ext = fluid_ext.at[(slice(None),) + ghost_cut(direction, EDGE)].set(slab * broadcast_rows(present[:, neighbour], slab.ndim))
    block_ids = jnp.arange(blocks, dtype=jnp.int32)
    inlet_flag = jnp.any(block_ids[:, None] == inlet_ids[None, :], axis=1).astype(jnp.float32)
    open_ext = open_plane(inlet_flag, EDGE)
    sets_list = [list(range(VELS))] * NEIGHBOURS
    layer_sum = jnp.zeros((blocks, EDGE * EDGE), jnp.float32)
    current = adjoint
    for step_index in range(STEPS):
        cube = current.reshape(blocks, VELS, EDGE, EDGE, EDGE)
        layer_sum = layer_sum + inlet_layer(cube, fluid_cube)
        segments = []
        for neighbour in range(NEIGHBOURS):
            slab = cube[(slice(None), slice(None)) + source_cut(VELOCITIES[neighbour + 1], EDGE)][clipped[:, neighbour]]
            segments.append(slab * broadcast_rows(present[:, neighbour], slab.ndim))
        pulled = pull_all(cube, segments, sets_list, fluid_ext, open_ext)
        current = collide(pulled, velocity, relax, fluid_flat)
    inlet_field = layer_sum[inlet_ids]
    inlet_grad = jnp.einsum("pbn,bn->p", basis, inlet_field, precision=lax.Precision.HIGHEST)
    return current, inlet_grad
```

```python
import jax
import jax.numpy as jnp
import numpy as np
from jax import lax
from jax.experimental import pallas as pl
from jax.experimental.pallas import tpu as pltpu
from jax.sharding import PartitionSpec as P

EDGE = 16
VELS = 19
NEIGHBOURS = 18
REACH = 2
STEPS = 4
LANES = 128
NIN = 16
MODES = 8

C = np.array(
    [
        [0, 0, 0],
        [1, 0, 0],
        [-1, 0, 0],
        [0, 1, 0],
        [0, -1, 0],
        [0, 0, 1],
        [0, 0, -1],
        [1, 1, 0],
        [-1, -1, 0],
        [1, -1, 0],
        [-1, 1, 0],
        [1, 0, 1],
        [-1, 0, -1],
        [1, 0, -1],
        [-1, 0, 1],
        [0, 1, 1],
        [0, -1, -1],
        [0, 1, -1],
        [0, -1, 1],
    ],
    dtype=np.int32,
)
OPP = [0, 2, 1, 4, 3, 6, 5, 8, 7, 10, 9, 12, 11, 14, 13, 16, 15, 18, 17]
DIRECTION = {tuple(int(v) for v in C[k + 1]): k for k in range(NEIGHBOURS)}

FLUID = -1
MEMBERS = {
    (axis, sign): [i for i in range(VELS) if C[i][axis] == sign] + [FLUID]
    for axis in range(3)
    for sign in (1, -1)
}
X_BASE = {1: 0, -1: 12}
Y_BASE = {1: 24, -1: 40}
Z_BASE = 56
ROWS = 88
OWN = REACH


def z_slot(sign, item):
    return MEMBERS[(2, sign)].index(item) + (0 if sign == 1 else 6)


def lane_roll(value, by):
    by = by % LANES
    return value if by == 0 else pltpu.roll(value, LANES - by, 1)


def row_roll(value, by):
    return pltpu.roll(value, (-by) % EDGE, 0)


class Masks:
    def __init__(self):
        self.lane = lax.broadcasted_iota(jnp.int32, (EDGE, LANES), 1)
        self.row = lax.broadcasted_iota(jnp.int32, (EDGE, LANES), 0)
        self.z = self.lane % EDGE
        self.yl = self.lane // EDGE


def pack(package, load, plane_row, items, masks):
    for sign in (1, -1):
        x_at = 0 if sign == 1 else EDGE - 1
        for slot, item in enumerate(MEMBERS[(0, sign)]):
            if item in items:
                for yh in range(2):
                    package[pl.ds(X_BASE[sign] + 2 * slot + yh, 1), :] = plane_row(item, yh, x_at)
    for sign in (1, -1):
        yh, start = (0, 0) if sign == 1 else (1, LANES - EDGE)
        block = None
        for slot, item in enumerate(MEMBERS[(1, sign)]):
            if item in items:
                moved = lane_roll(load(item, yh), start - slot * EDGE)
                block = moved if block is None else jnp.where(masks.yl == slot, moved, block)
        package[pl.ds(Y_BASE[sign], EDGE), :] = block
    for yh in range(2):
        block = None
        for sign in (1, -1):
            start = 0 if sign == 1 else EDGE - 1
            for item in MEMBERS[(2, sign)]:
                if item in items:
                    slot = z_slot(sign, item)
                    moved = lane_roll(load(item, yh), start - slot)
                    block = moved if block is None else jnp.where(masks.z == slot, moved, block)
        package[pl.ds(Z_BASE + yh * EDGE, EDGE), :] = block


def pull(field, item, c, ghost, masks):
    cx, cy, cz = (int(v) for v in c)
    v0, v1 = field
    if cx:
        edge = masks.row == (EDGE - 1 if cx == 1 else 0)
        base = X_BASE[cx] + 2 * MEMBERS[(0, cx)].index(item)
        v0 = jnp.where(edge, ghost((cx, 0, 0), base, 1), row_roll(v0, cx))
        v1 = jnp.where(edge, ghost((cx, 0, 0), base + 1, 1), row_roll(v1, cx))
    if cy:
        slot = MEMBERS[(1, cy)].index(item)
        at = 0 if cy == 1 else LANES - EDGE
        plane = lane_roll(ghost((0, cy, 0), Y_BASE[cy], EDGE), slot * EDGE - at)
        if cx:
            line = ghost((cx, cy, 0), base + (0 if cy == 1 else 1), 1)
            plane = jnp.where(edge, line, row_roll(plane, cx))
        if cy == 1:
            take = masks.lane < EDGE
            v0, v1 = jnp.where(take, v1, v0), jnp.where(take, plane, v1)
        else:
            take = masks.lane >= LANES - EDGE
            v0, v1 = jnp.where(take, plane, v0), jnp.where(take, v0, v1)
        v0, v1 = lane_roll(v0, cy * EDGE), lane_roll(v1, cy * EDGE)
    if cz:
        target = EDGE - 1 if cz == 1 else 0
        slot = z_slot(cz, item)
        g = [lane_roll(ghost((0, 0, cz), Z_BASE + yh * EDGE, EDGE), slot - target) for yh in range(2)]
        source = EDGE - 1 - target
        if cx:
            for yh in range(2):
                line = lane_roll(ghost((cx, 0, cz), base + yh, 1), source - target)
                g[yh] = jnp.where(edge, line, row_roll(g[yh], cx))
        if cy:
            line = lane_roll(
                ghost((0, cy, cz), Y_BASE[cy], EDGE),
                MEMBERS[(1, cy)].index(item) * EDGE + source - (at + target),
            )
            if cy == 1:
                g = [jnp.where(take, g[1], g[0]), jnp.where(take, line, g[1])]
            else:
                g = [jnp.where(take, line, g[0]), jnp.where(take, g[0], g[1])]
            g = [lane_roll(v, cy * EDGE) for v in g]
        here = masks.z == target
        v0 = jnp.where(here, g[0], lane_roll(v0, cz))
        v1 = jnp.where(here, g[1], lane_roll(v1, cz))
    return v0, v1


def collide(b, u, k, g, e):
    ux, uy, uz = u
    pairs = [(i, i + 1) for i in range(1, VELS, 2)]
    s = {i: b[i] + b[j] for i, j in pairs}
    d = {i: b[i] - b[j] for i, j in pairs}
    p, q, r = s[7] + s[9], s[11] + s[13], s[15] + s[17]
    sx, sy, sz = s[1] + s[1], s[3] + s[3], s[5] + s[5]
    mxx, myy, mzz = sx + (p + q), sy + (p + r), sz + (q + r)
    mxy, mxz, myz = s[7] - s[9], s[11] - s[13], s[15] - s[17]
    m0 = 12.0 * b[0] + (sx + sy + sz) + (p + q + r)
    m1x = (d[1] + d[1]) + (d[7] + d[9]) + (d[11] + d[13])
    m1y = (d[3] + d[3]) + (d[7] - d[9]) + (d[15] + d[17])
    m1z = (d[5] + d[5]) + (d[11] - d[13]) + (d[15] - d[17])
    nx = mxx * ux + mxy * uy + mxz * uz
    ny = mxy * ux + myy * uy + myz * uz
    nz = mxz * ux + myz * uy + mzz * uz
    vx = g * (m1x + 3.0 * nx - ux * m0)
    vy = g * (m1y + 3.0 * ny - uy * m0)
    vz = g * (m1z + 3.0 * nz - uz * m0)
    o = g * (m0 * e - 1.5 * (ux * nx + uy * ny + uz * nz))
    v = {1: vx, 3: vy, 5: vz, 7: vx + vy, 9: vx - vy, 11: vx + vz, 13: vx - vz, 15: vy + vz, 17: vy - vz}
    out = [k * b[0] + o]
    for i, j in pairs:
        out.append(k * b[i] + (o + v[i]))
        out.append(k * b[j] + (o - v[i]))
    return out


def body(n, inner, *refs):
    (a_hbm, vel_hbm, relax_hbm, words, nbrs, ids, basis_hbm) = refs[:7]
    (out_hbm, grad) = refs[7:9]
    (a, b, vel, relax, basis, fluid, bits, coef) = refs[9:17]
    bufs = refs[17 : 17 + STEPS]
    (part1, part2, local_sem, send_sem, recv_sem, sum_send1, sum_recv1, sum_send2, sum_recv2) = refs[17 + STEPS :]
    me = lax.axis_index("blk")
    outer = n // inner
    place = me % inner
    group = me // inner
    offsets = (2, -2, 1, -1)
    halo_peers = [(me + d + n) % n for d in offsets]
    inner_peers = [group * inner + (place + j) % inner for j in range(1, inner)]
    outer_peers = [((group + j) % outer) * inner + place for j in range(1, outer)]
    peers = halo_peers + inner_peers + outer_peers

    barrier = pltpu.get_barrier_semaphore()
    for peer in peers:
        pl.semaphore_signal(barrier, inc=1, device_id=(peer,), device_id_type=pl.DeviceIdType.MESH)

    loads = []
    for yh in range(2):
        loads.append(pltpu.make_async_copy(a_hbm.at[:, :, yh, :], a.at[:, yh], local_sem.at[yh]))
        loads.append(pltpu.make_async_copy(vel_hbm.at[:, :, yh, :], vel.at[:, yh], local_sem.at[2 + yh]))
        loads.append(pltpu.make_async_copy(relax_hbm.at[:, yh, :], relax.at[yh], local_sem.at[4 + yh]))
    loads.append(pltpu.make_async_copy(basis_hbm, basis, local_sem.at[6]))
    for load in loads:
        load.start()

    masks = Masks()
    for yh in range(2):
        word = jnp.zeros((EDGE, LANES), jnp.int32)
        for x in range(EDGE):
            at = x * 8 + yh * 4
            w = [words[0, at + j] for j in range(4)]
            line = jnp.where(
                masks.lane < 64,
                jnp.where(masks.lane < 32, w[0], w[1]),
                jnp.where(masks.lane < 96, w[2], w[3]),
            )
            word = jnp.where(masks.row == x, line, word)
        bit = jnp.bitwise_and(jnp.right_shift(word, masks.lane % 32), 1)
        fluid[yh] = bit.astype(jnp.float32)

    is_inlet = jnp.int32(0)
    for r in range(NIN):
        is_inlet = is_inlet + (ids[r] == me).astype(jnp.int32)
    keep = 1.0 - is_inlet.astype(jnp.float32)
    keep_z = jnp.where(masks.z == 0, keep, 1.0)
    slot_of = []
    present = []
    for k in range(NEIGHBOURS):
        entry = nbrs[0, k]
        there = (entry >= 0).astype(jnp.int32)
        slot = jnp.clip(entry - me + OWN, 0, 2 * REACH)
        slot_of.append(slot * there + OWN * (1 - there))
        present.append(there.astype(jnp.float32))

    def send(step):
        copies = []
        for index, d in enumerate(offsets):
            copies.append(
                pltpu.make_async_remote_copy(
                    src_ref=bufs[step].at[OWN],
                    dst_ref=bufs[step].at[OWN - d],
                    send_sem=send_sem.at[step, index],
                    recv_sem=recv_sem.at[step, index],
                    device_id=(halo_peers[index],),
                    device_id_type=pl.DeviceIdType.MESH,
                )
            )
        for copy in copies:
            copy.start()
        return copies

    everything = set(range(1, VELS))
    layer = [jnp.zeros((EDGE, LANES), jnp.float32) for _ in range(2)]

    for load in loads:
        load.wait()
    for step in range(STEPS):
        items = everything | ({FLUID} if step == 0 else set())
        pack(
            bufs[step].at[OWN],
            lambda item, yh: fluid[yh] if item == FLUID else a[item, yh],
            lambda item, yh, x: fluid[yh, pl.ds(x, 1), :] if item == FLUID else a[item, yh, pl.ds(x, 1), :],
            items,
            masks,
        )
        if step == 0:
            pl.semaphore_wait(barrier, len(peers))
        copies = send(step)
        for yh in range(2):
            layer[yh] = layer[yh] + (2.0 * a[5, yh] + ((a[11, yh] + a[14, yh]) + (a[15, yh] + a[18, yh])))
            if step == 0:
                f = fluid[yh]
                squared = vel[0, yh] * vel[0, yh] + vel[1, yh] * vel[1, yh] + vel[2, yh] * vel[2, yh]
                coef[0, yh] = f * (1.0 - relax[yh])
                coef[1, yh] = f * relax[yh] * (1.0 / 12.0)
                coef[2, yh] = (1.0 / 3.0) + 0.5 * squared
        if step == STEPS - 1:
            site = lax.broadcasted_iota(jnp.int32, (LANES, 2 * LANES), 0)
            flat = lax.broadcasted_iota(jnp.int32, (LANES, 2 * LANES), 1)
            spread = jnp.zeros((EDGE, 2 * LANES), jnp.float32)
            for yh in range(2):
                pick = ((site % EDGE == 0) & (site // EDGE + 8 * yh == flat % EDGE)).astype(jnp.float32)
                value = jnp.where(masks.z == 0, layer[yh] * fluid[yh], 0.0) * (1.0 / 12.0)
                spread = spread + jnp.dot(
                    value, pick, precision=lax.Precision.HIGHEST, preferred_element_type=jnp.float32
                )
            row = lax.broadcasted_iota(jnp.int32, (EDGE, 2 * LANES), 0)
            lane = lax.broadcasted_iota(jnp.int32, (EDGE, 2 * LANES), 1)
            line = jnp.sum(jnp.where(lane // EDGE == row, spread, 0.0), axis=0, keepdims=True)
            weight = jnp.zeros((EDGE, 2 * LANES), jnp.float32)
            for r in range(NIN):
                mine = (ids[r] == me).astype(jnp.float32)
                weight = jnp.where(row == r, mine, weight)
            weight = weight * line
            mode = lax.broadcasted_iota(jnp.int32, (MODES, LANES), 0)
            total = jnp.zeros((MODES, LANES), jnp.float32)
            for m in range(MODES):
                product = jnp.sum(basis[m] * weight, axis=0, keepdims=True)
                total = jnp.where(mode == m, product[:, :LANES] + product[:, LANES:], total)
            part1[0] = total
            sums1 = []
            for j in range(1, inner):
                sums1.append(
                    pltpu.make_async_remote_copy(
                        src_ref=part1.at[0],
                        dst_ref=part1.at[j],
                        send_sem=sum_send1.at[j - 1],
                        recv_sem=sum_recv1.at[j - 1],
                        device_id=(inner_peers[j - 1],),
                        device_id_type=pl.DeviceIdType.MESH,
                    )
                )
            for copy in sums1:
                copy.start()
            for copy in sums1:
                copy.wait()
            total = part1[0]
            for j in range(1, inner):
                total = total + part1[j]
            part2[0] = total
            sums2 = []
            for j in range(1, outer):
                sums2.append(
                    pltpu.make_async_remote_copy(
                        src_ref=part2.at[0],
                        dst_ref=part2.at[j],
                        send_sem=sum_send2.at[j - 1],
                        recv_sem=sum_recv2.at[j - 1],
                        device_id=(outer_peers[j - 1],),
                        device_id_type=pl.DeviceIdType.MESH,
                    )
                )
            for copy in sums2:
                copy.start()
        for copy in copies:
            copy.wait()

        buf = bufs[step]

        def ghost(direction, row, rows):
            return buf[slot_of[DIRECTION[direction]], pl.ds(row, rows), :]

        if step == 0:

            def ghost_fluid(direction, row, rows):
                k = DIRECTION[direction]
                return buf[slot_of[k], pl.ds(row, rows), :] * present[k]

            for i in range(1, VELS):
                m0, m1 = pull((fluid[0], fluid[1]), FLUID, C[i], ghost_fluid, masks)
                bits[i - 1, 0] = m0
                bits[i - 1, 1] = m1
        for yh in range(2):
            b[0, yh] = a[0, yh]
        for i in range(1, VELS):
            pulled = pull((a[i, 0], a[i, 1]), i, C[i], ghost, masks)
            for yh in range(2):
                value = jnp.where(bits[i - 1, yh] > 0.5, pulled[yh], a[OPP[i], yh])
                if C[i][2] == -1:
                    value = value * keep_z
                b[i, yh] = value
        for yh in range(2):
            for half in range(2):
                rows = pl.ds(8 * half, 8)
                new = collide(
                    [b[i, yh, rows, :] for i in range(VELS)],
                    [vel[c, yh, rows, :] for c in range(3)],
                    coef[0, yh, rows, :],
                    coef[1, yh, rows, :],
                    coef[2, yh, rows, :],
                )
                for i in range(VELS):
                    a[i, yh, rows, :] = new[i]

    stores = [
        pltpu.make_async_copy(a.at[:, yh], out_hbm.at[:, :, yh, :], local_sem.at[yh]) for yh in range(2)
    ]
    for store in stores:
        store.start()
    for copy in sums2:
        copy.wait()
    total = part2[0]
    for j in range(1, outer):
        total = total + part2[j]
    ones = jnp.ones((8, LANES), jnp.float32)
    result = lax.dot_general(
        ones, total, (((1,), (1,)), ((), ())), precision=lax.Precision.HIGHEST, preferred_element_type=jnp.float32
    )
    grad[...] = result[0:1, :]
    for store in stores:
        store.wait()


def on_device(adjoint, velocity, relax, fluid_words, neighbours, inlet_ids, basis):
    n = lax.axis_size("blk")
    inner = 8 if n % 64 == 0 else 4
    outer = n // inner
    f32 = jnp.float32
    shape = (EDGE, 2, LANES)
    any_space = pl.BlockSpec(memory_space=pl.ANY)
    smem = pl.BlockSpec(memory_space=pltpu.SMEM)
    dma = pltpu.SemaphoreType.DMA
    out, grad = pl.pallas_call(
        lambda *refs: body(n, inner, *refs),
        out_shape=(
            jax.ShapeDtypeStruct((VELS,) + shape, f32),
            jax.ShapeDtypeStruct((1, MODES), f32),
        ),
        in_specs=[any_space, any_space, any_space, smem, smem, smem, any_space],
        out_specs=(any_space, pl.BlockSpec(memory_space=pltpu.VMEM)),
        scratch_shapes=[
            pltpu.VMEM((VELS, 2, EDGE, LANES), f32),
            pltpu.VMEM((VELS, 2, EDGE, LANES), f32),
            pltpu.VMEM((3, 2, EDGE, LANES), f32),
            pltpu.VMEM((2, EDGE, LANES), f32),
            pltpu.VMEM((MODES, NIN, 2 * LANES), f32),
            pltpu.VMEM((2, EDGE, LANES), f32),
            pltpu.VMEM((VELS - 1, 2, EDGE, LANES), f32),
            pltpu.VMEM((3, 2, EDGE, LANES), f32),
        ]
        + [pltpu.VMEM((2 * REACH + 1, ROWS, LANES), f32) for _ in range(STEPS)]
        + [
            pltpu.VMEM((inner, MODES, LANES), f32),
            pltpu.VMEM((outer, MODES, LANES), f32),
            dma((7,)),
            dma((STEPS, 4)),
            dma((STEPS, 4)),
            dma((inner - 1,)),
            dma((inner - 1,)),
            dma((outer - 1,)),
            dma((outer - 1,)),
        ],
        compiler_params=pltpu.CompilerParams(collective_id=0, has_side_effects=True),
        name="adjoint_steps",
    )(
        adjoint.reshape((VELS,) + shape),
        velocity.reshape((3,) + shape),
        relax.reshape(shape),
        fluid_words,
        neighbours,
        inlet_ids,
        basis,
    )
    return (out.reshape(1, VELS, EDGE * EDGE * EDGE), grad.reshape(MODES))


def solution(mesh):
    return jax.shard_map(
        on_device,
        mesh=mesh,
        in_specs=(
            P("blk", None, None),
            P("blk", None, None),
            P("blk", None),
            P("blk", None),
            P("blk", None),
            P(),
            P(),
        ),
        out_specs=(P("blk", None, None), P()),
        check_vma=False,
    )
```

```python
import jax
import jax.numpy as jnp
import numpy as np
from jax import lax
from jax.experimental import pallas as pl
from jax.experimental.pallas import tpu as pltpu
from jax.sharding import PartitionSpec as P

EDGE = 16
VELS = 19
NEIGHBOURS = 18
REACH = 2
STEPS = 4
LANES = 128
NIN = 16
MODES = 8

C = np.array(
    [
        [0, 0, 0],
        [1, 0, 0],
        [-1, 0, 0],
        [0, 1, 0],
        [0, -1, 0],
        [0, 0, 1],
        [0, 0, -1],
        [1, 1, 0],
        [-1, -1, 0],
        [1, -1, 0],
        [-1, 1, 0],
        [1, 0, 1],
        [-1, 0, -1],
        [1, 0, -1],
        [-1, 0, 1],
        [0, 1, 1],
        [0, -1, -1],
        [0, 1, -1],
        [0, -1, 1],
    ],
    dtype=np.int32,
)
OPP = [0, 2, 1, 4, 3, 6, 5, 8, 7, 10, 9, 12, 11, 14, 13, 16, 15, 18, 17]
DIRECTION = {tuple(int(v) for v in C[k + 1]): k for k in range(NEIGHBOURS)}

FLUID = -1


def members(axis, sign):
    found = [i for i in range(VELS) if C[i][axis] == sign]
    return sorted(found, key=lambda i: int(np.abs(C[i]).sum()), reverse=True)


Z_ROWS, Y_ROWS, AXIS_ROWS, X_ROWS, X_FLUID, YZ_FLUID = 0, 16, 32, 48, 68, 72
SENT, ROWS = 68, 88
SIGNS = (1, -1)
Z_NUMBER = {i: n for n, i in enumerate([i for s in SIGNS for i in members(2, s)[:4]])}
Y_NUMBER = {i: n for n, i in enumerate([i for s in SIGNS for i in members(1, s)[:4]])}
X_NUMBER = {i: n for n, i in enumerate([i for s in SIGNS for i in members(0, s)])}
CUT = 12
OWN = REACH


def sign_index(sign):
    return 0 if sign == 1 else 1


def x_row(item, sign, yh):
    if item == FLUID:
        return X_FLUID + 2 * sign_index(sign) + yh
    return X_ROWS + 2 * X_NUMBER[item] + yh


def lane_roll(value, by):
    by = by % LANES
    return value if by == 0 else pltpu.roll(value, LANES - by, 1)


def row_roll(value, by):
    return pltpu.roll(value, (-by) % EDGE, 0)


class Masks:
    def __init__(self):
        self.lane = lax.broadcasted_iota(jnp.int32, (EDGE, LANES), 1)
        self.row = lax.broadcasted_iota(jnp.int32, (EDGE, LANES), 0)
        self.z = self.lane % EDGE
        self.yl = self.lane // EDGE


def put(block, mask, value):
    return value if block is None else jnp.where(mask, value, block)


def pack_axis(load, items, masks):
    block = None
    for sign in SIGNS:
        yh, start = (0, 0) if sign == 1 else (1, LANES - EDGE)
        plane = load(items[(1, sign)], yh)
        at = 4 * sign_index(sign) * EDGE + 4
        first = lane_roll(plane, start - at)
        second = lane_roll(plane, start + CUT - at - EDGE)
        block = put(block, masks.yl == at // EDGE, first)
        block = put(block, masks.yl == at // EDGE + 1, second)
    for sign in SIGNS:
        start = 0 if sign == 1 else EDGE - 1
        for yh in range(2):
            slot = 2 * sign_index(sign) + yh
            block = put(block, masks.z == slot, lane_roll(load(items[(2, sign)], yh), start - slot))
    return block


def pack(package, a, fluid, masks):
    def load(item, yh):
        return fluid[yh] if item == FLUID else a[item, yh]

    block = None
    for sign in SIGNS:
        start = 0 if sign == 1 else EDGE - 1
        for item in members(2, sign)[:4]:
            for yh in range(2):
                slot = 2 * Z_NUMBER[item] + yh
                block = put(block, masks.z == slot, lane_roll(load(item, yh), start - slot))
    package[pl.ds(Z_ROWS, EDGE), :] = block
    block = None
    for sign in SIGNS:
        yh, start = (0, 0) if sign == 1 else (1, LANES - EDGE)
        for item in members(1, sign)[:4]:
            number = Y_NUMBER[item]
            block = put(block, masks.yl == number, lane_roll(load(item, yh), start - number * EDGE))
    package[pl.ds(Y_ROWS, EDGE), :] = block
    axis = {(1, 1): 3, (1, -1): 4, (2, 1): 5, (2, -1): 6}
    package[pl.ds(AXIS_ROWS, EDGE), :] = pack_axis(load, axis, masks)
    for sign in SIGNS:
        x_at = 0 if sign == 1 else EDGE - 1
        for item in members(0, sign):
            for yh in range(2):
                package[pl.ds(x_row(item, sign, yh), 1), :] = a[item, yh, pl.ds(x_at, 1), :]
        if fluid is not None:
            for yh in range(2):
                package[pl.ds(x_row(FLUID, sign, yh), 1), :] = fluid[yh, pl.ds(x_at, 1), :]
    if fluid is not None:
        package[pl.ds(YZ_FLUID, EDGE), :] = pack_axis(load, {key: FLUID for key in axis}, masks)


def y_plane(ghost, direction, item, sign, at, masks, only=None):
    if item in Y_NUMBER:
        return lane_roll(ghost(direction, Y_ROWS, EDGE), Y_NUMBER[item] * EDGE - at)
    block = ghost(direction, YZ_FLUID if item == FLUID else AXIS_ROWS, EDGE)
    start = 4 * sign_index(sign) * EDGE + 4
    first = lane_roll(block, start - at) if only is None or only < CUT else None
    second = lane_roll(block, start + EDGE - CUT - at) if only is None or only >= CUT else None
    if first is None or second is None:
        return second if first is None else first
    return jnp.where((masks.lane + (LANES - at)) % LANES < CUT, first, second)


def z_plane(ghost, direction, item, sign, yh, target):
    if item in Z_NUMBER:
        return lane_roll(ghost(direction, Z_ROWS, EDGE), 2 * Z_NUMBER[item] + yh - target)
    block = ghost(direction, YZ_FLUID if item == FLUID else AXIS_ROWS, EDGE)
    return lane_roll(block, 2 * sign_index(sign) + yh - target)


def pull(field, item, c, ghost, masks):
    cx, cy, cz = (int(v) for v in c)
    v0, v1 = field
    if cx:
        edge = masks.row == (EDGE - 1 if cx == 1 else 0)
        v0 = jnp.where(edge, ghost((cx, 0, 0), x_row(item, cx, 0), 1), row_roll(v0, cx))
        v1 = jnp.where(edge, ghost((cx, 0, 0), x_row(item, cx, 1), 1), row_roll(v1, cx))
    if cy:
        at = 0 if cy == 1 else LANES - EDGE
        plane = y_plane(ghost, (0, cy, 0), item, cy, at, masks)
        if cx:
            line = ghost((cx, cy, 0), x_row(item, cx, 0 if cy == 1 else 1), 1)
            plane = jnp.where(edge, line, row_roll(plane, cx))
        if cy == 1:
            take = masks.lane < EDGE
            v0, v1 = jnp.where(take, v1, v0), jnp.where(take, plane, v1)
        else:
            take = masks.lane >= LANES - EDGE
            v0, v1 = jnp.where(take, plane, v0), jnp.where(take, v0, v1)
        v0, v1 = lane_roll(v0, cy * EDGE), lane_roll(v1, cy * EDGE)
    if cz:
        target = EDGE - 1 if cz == 1 else 0
        source = EDGE - 1 - target
        g = [z_plane(ghost, (0, 0, cz), item, cz, yh, target) for yh in range(2)]
        if cx:
            for yh in range(2):
                line = lane_roll(ghost((cx, 0, cz), x_row(item, cx, yh), 1), source - target)
                g[yh] = jnp.where(edge, line, row_roll(g[yh], cx))
        if cy:
            line = y_plane(ghost, (0, cy, cz), item, cy, at + target - source, masks, source)
            if cy == 1:
                g = [jnp.where(take, g[1], g[0]), jnp.where(take, line, g[1])]
            else:
                g = [jnp.where(take, line, g[0]), jnp.where(take, g[0], g[1])]
            g = [lane_roll(v, cy * EDGE) for v in g]
        here = masks.z == target
        v0 = jnp.where(here, g[0], lane_roll(v0, cz))
        v1 = jnp.where(here, g[1], lane_roll(v1, cz))
    return v0, v1


def collide(b, u, k, g, e):
    ux, uy, uz = u
    pairs = [(i, i + 1) for i in range(1, VELS, 2)]
    s = {i: b[i] + b[j] for i, j in pairs}
    d = {i: b[i] - b[j] for i, j in pairs}
    p, q, r = s[7] + s[9], s[11] + s[13], s[15] + s[17]
    sx, sy, sz = s[1] + s[1], s[3] + s[3], s[5] + s[5]
    mxx, myy, mzz = sx + (p + q), sy + (p + r), sz + (q + r)
    mxy, mxz, myz = s[7] - s[9], s[11] - s[13], s[15] - s[17]
    m0 = 12.0 * b[0] + (sx + sy + sz) + (p + q + r)
    m1x = (d[1] + d[1]) + (d[7] + d[9]) + (d[11] + d[13])
    m1y = (d[3] + d[3]) + (d[7] - d[9]) + (d[15] + d[17])
    m1z = (d[5] + d[5]) + (d[11] - d[13]) + (d[15] - d[17])
    nx = mxx * ux + mxy * uy + mxz * uz
    ny = mxy * ux + myy * uy + myz * uz
    nz = mxz * ux + myz * uy + mzz * uz
    vx = g * (m1x + 3.0 * nx - ux * m0)
    vy = g * (m1y + 3.0 * ny - uy * m0)
    vz = g * (m1z + 3.0 * nz - uz * m0)
    o = g * (m0 * e - 1.5 * (ux * nx + uy * ny + uz * nz))
    v = {1: vx, 3: vy, 5: vz, 7: vx + vy, 9: vx - vy, 11: vx + vz, 13: vx - vz, 15: vy + vz, 17: vy - vz}
    out = [k * b[0] + o]
    for i, j in pairs:
        out.append(k * b[i] + (o + v[i]))
        out.append(k * b[j] + (o - v[i]))
    return out


AHEAD, BEHIND, SIBLING, PASSED = OWN + 2, OWN - 2, OWN + 1, OWN - 1


def body(n, inner, *refs):
    (a_hbm, vel_hbm, relax_hbm, words, nbrs, ids, basis_hbm) = refs[:7]
    (out_hbm, grad) = refs[7:9]
    (a, b, vel, relax, basis, fluid, bits, coef) = refs[9:17]
    bufs = refs[17 : 17 + STEPS]
    (part1, part2, local_sem, send_sem, recv_sem, sum_send1, sum_recv1, sum_send2, sum_recv2) = refs[17 + STEPS :]
    me = lax.axis_index("blk")
    outer = n // inner
    place = me % inner
    group = me // inner
    way = 1 - 2 * (me % 2)
    ahead, behind, sibling = me + 2 * way, me - 2 * way, me + way
    has_ahead = (ahead >= 0) & (ahead < n)
    has_behind = (behind >= 0) & (behind < n)
    inner_peers = [group * inner + (place + j) % inner for j in range(1, inner)]
    outer_peers = [((group + j) % outer) * inner + place for j in range(1, outer)]

    barrier = pltpu.get_barrier_semaphore()

    def greet(peer):
        pl.semaphore_signal(barrier, inc=1, device_id=(peer,), device_id_type=pl.DeviceIdType.MESH)

    pl.when(has_ahead)(lambda: greet(ahead))
    pl.when(has_behind)(lambda: greet(behind))
    for peer in [sibling] + inner_peers + outer_peers:
        greet(peer)
    greetings = inner + outer - 1 + has_ahead.astype(jnp.int32) + has_behind.astype(jnp.int32)

    loads = []
    for yh in range(2):
        loads.append(pltpu.make_async_copy(a_hbm.at[:, :, yh, :], a.at[:, yh], local_sem.at[yh]))
        loads.append(pltpu.make_async_copy(vel_hbm.at[:, :, yh, :], vel.at[:, yh], local_sem.at[2 + yh]))
        loads.append(pltpu.make_async_copy(relax_hbm.at[:, yh, :], relax.at[yh], local_sem.at[4 + yh]))
    loads.append(pltpu.make_async_copy(basis_hbm, basis, local_sem.at[6]))
    for load in loads:
        load.start()

    masks = Masks()
    for yh in range(2):
        word = jnp.zeros((EDGE, LANES), jnp.int32)
        for x in range(EDGE):
            at = x * 8 + yh * 4
            w = [words[0, at + j] for j in range(4)]
            line = jnp.where(
                masks.lane < 64,
                jnp.where(masks.lane < 32, w[0], w[1]),
                jnp.where(masks.lane < 96, w[2], w[3]),
            )
            word = jnp.where(masks.row == x, line, word)
        bit = jnp.bitwise_and(jnp.right_shift(word, masks.lane % 32), 1)
        fluid[yh] = bit.astype(jnp.float32)

    is_inlet = jnp.int32(0)
    for r in range(NIN):
        is_inlet = is_inlet + (ids[r] == me).astype(jnp.int32)
    keep = 1.0 - is_inlet.astype(jnp.float32)
    keep_z = jnp.where(masks.z == 0, keep, 1.0)
    slot_of = []
    present = []
    for k in range(NEIGHBOURS):
        entry = nbrs[0, k]
        there = (entry >= 0).astype(jnp.int32)
        slot = jnp.clip(OWN + (entry - me) * way, 0, 2 * REACH)
        slot_of.append(slot * there + OWN * (1 - there))
        present.append(there.astype(jnp.float32))

    def halo(step, index, source, target, peer):
        rows = pl.ds(0, ROWS if step == 0 else SENT)
        return pltpu.make_async_remote_copy(
            src_ref=bufs[step].at[source, rows],
            dst_ref=bufs[step].at[target, rows],
            send_sem=send_sem.at[step, index],
            recv_sem=recv_sem.at[step, index],
            device_id=(peer,),
            device_id_type=pl.DeviceIdType.MESH,
        )

    def sum_copy(part, send, recv, j, peer):
        return pltpu.make_async_remote_copy(
            src_ref=part.at[pl.ds(0, 1)],
            dst_ref=part.at[pl.ds(j, 1)],
            send_sem=send.at[j - 1],
            recv_sem=recv.at[j - 1],
            device_id=(peer,),
            device_id_type=pl.DeviceIdType.MESH,
        )

    layer = [jnp.zeros((EDGE, LANES), jnp.float32) for _ in range(2)]
    for load in loads:
        load.wait()
    exchanges = []
    for step in range(STEPS):
        buf = bufs[step]
        pack(buf.at[OWN], a, fluid if step == 0 else None, masks)
        if step == 0:
            pl.semaphore_wait(barrier, greetings)
        to_ahead = halo(step, 0, OWN, BEHIND, ahead)
        to_behind = halo(step, 1, OWN, AHEAD, behind)
        to_sibling = halo(step, 2, OWN, SIBLING, sibling)
        passing = halo(step, 3, AHEAD, PASSED, sibling)
        exchanges.append((to_ahead, to_behind, to_sibling, passing))
        pl.when(has_behind)(to_behind.start)
        pl.when(has_ahead)(to_ahead.start)
        to_sibling.start()
        for yh in range(2):
            layer[yh] = layer[yh] + (2.0 * a[5, yh] + ((a[11, yh] + a[14, yh]) + (a[15, yh] + a[18, yh])))
            if step == 0:
                f = fluid[yh]
                squared = vel[0, yh] * vel[0, yh] + vel[1, yh] * vel[1, yh] + vel[2, yh] * vel[2, yh]
                coef[0, yh] = f * (1.0 - relax[yh])
                coef[1, yh] = f * relax[yh] * (1.0 / 12.0)
                coef[2, yh] = (1.0 / 3.0) + 0.5 * squared
        if step == STEPS - 1:
            site = lax.broadcasted_iota(jnp.int32, (LANES, 2 * LANES), 0)
            flat = lax.broadcasted_iota(jnp.int32, (LANES, 2 * LANES), 1)
            spread = jnp.zeros((EDGE, 2 * LANES), jnp.float32)
            for yh in range(2):
                pick = ((site % EDGE == 0) & (site // EDGE + 8 * yh == flat % EDGE)).astype(jnp.float32)
                value = jnp.where(masks.z == 0, layer[yh] * fluid[yh], 0.0) * (1.0 / 12.0)
                spread = spread + jnp.dot(
                    value, pick, precision=lax.Precision.HIGHEST, preferred_element_type=jnp.float32
                )
            row = lax.broadcasted_iota(jnp.int32, (EDGE, 2 * LANES), 0)
            lane = lax.broadcasted_iota(jnp.int32, (EDGE, 2 * LANES), 1)
            line = jnp.sum(jnp.where(lane // EDGE == row, spread, 0.0), axis=0, keepdims=True)
            weight = jnp.zeros((EDGE, 2 * LANES), jnp.float32)
            for r in range(NIN):
                mine = (ids[r] == me).astype(jnp.float32)
                weight = jnp.where(row == r, mine, weight)
            weight = weight * line
            mode = lax.broadcasted_iota(jnp.int32, (MODES, LANES), 0)
            total = jnp.zeros((MODES, LANES), jnp.float32)
            for m in range(MODES):
                product = jnp.sum(basis[m] * weight, axis=0, keepdims=True)
                total = jnp.where(mode == m, product[:, :LANES] + product[:, LANES:], total)
            total = jnp.sum(total, axis=1, keepdims=True)
            at_mode = lax.broadcasted_iota(jnp.int32, (MODES, LANES), 1) == mode
            part1[pl.ds(0, 1), :] = jnp.sum(jnp.where(at_mode, total, 0.0), axis=0, keepdims=True)
            sums1 = [sum_copy(part1, sum_send1, sum_recv1, j, inner_peers[j - 1]) for j in range(1, inner)]
            for copy in sums1:
                copy.start()
            for copy in sums1:
                copy.wait_recv()
            part2[pl.ds(0, 1), :] = jnp.sum(part1[...], axis=0, keepdims=True)
            sums2 = [sum_copy(part2, sum_send2, sum_recv2, j, outer_peers[j - 1]) for j in range(1, outer)]
            for copy in sums2:
                copy.start()

        @pl.when(has_ahead)
        def _():
            to_behind.wait_recv()
            passing.start()

        pl.when(has_behind)(to_ahead.wait_recv)
        to_sibling.wait_recv()
        pl.when(has_behind)(passing.wait_recv)

        def ghost(direction, row, rows):
            return buf[slot_of[DIRECTION[direction]], pl.ds(row, rows), :]

        if step == 0:

            def ghost_fluid(direction, row, rows):
                k = DIRECTION[direction]
                return buf[slot_of[k], pl.ds(row, rows), :] * present[k]

            for i in range(1, VELS):
                m0, m1 = pull((fluid[0], fluid[1]), FLUID, C[i], ghost_fluid, masks)
                bits[i - 1, 0] = m0
                bits[i - 1, 1] = m1
        for yh in range(2):
            b[0, yh] = a[0, yh]
        for i in range(1, VELS):
            pulled = pull((a[i, 0], a[i, 1]), i, C[i], ghost, masks)
            for yh in range(2):
                value = jnp.where(bits[i - 1, yh] > 0.5, pulled[yh], a[OPP[i], yh])
                if C[i][2] == -1:
                    value = value * keep_z
                b[i, yh] = value
        for yh in range(2):
            for half in range(2):
                rows = pl.ds(8 * half, 8)
                new = collide(
                    [b[i, yh, rows, :] for i in range(VELS)],
                    [vel[c, yh, rows, :] for c in range(3)],
                    coef[0, yh, rows, :],
                    coef[1, yh, rows, :],
                    coef[2, yh, rows, :],
                )
                for i in range(VELS):
                    a[i, yh, rows, :] = new[i]

    stores = [
        pltpu.make_async_copy(a.at[:, yh], out_hbm.at[:, :, yh, :], local_sem.at[yh]) for yh in range(2)
    ]
    for store in stores:
        store.start()
    for copy in sums2:
        copy.wait_recv()
    grad[...] = jnp.sum(part2[...], axis=0, keepdims=True)[:, :MODES]
    for to_ahead, to_behind, to_sibling, passing in exchanges:
        pl.when(has_ahead)(to_ahead.wait_send)
        pl.when(has_behind)(to_behind.wait_send)
        to_sibling.wait_send()
        pl.when(has_ahead)(passing.wait_send)
    for copy in sums1 + sums2:
        copy.wait_send()
    for store in stores:
        store.wait()


def on_device(adjoint, velocity, relax, fluid_words, neighbours, inlet_ids, basis):
    n = lax.axis_size("blk")
    inner = 8 if n % 64 == 0 else 4
    outer = n // inner
    f32 = jnp.float32
    shape = (EDGE, 2, LANES)
    any_space = pl.BlockSpec(memory_space=pl.ANY)
    smem = pl.BlockSpec(memory_space=pltpu.SMEM)
    dma = pltpu.SemaphoreType.DMA
    out, grad = pl.pallas_call(
        lambda *refs: body(n, inner, *refs),
        out_shape=(
            jax.ShapeDtypeStruct((VELS,) + shape, f32),
            jax.ShapeDtypeStruct((1, MODES), f32),
        ),
        in_specs=[any_space, any_space, any_space, smem, smem, smem, any_space],
        out_specs=(any_space, pl.BlockSpec(memory_space=pltpu.VMEM)),
        scratch_shapes=[
            pltpu.VMEM((VELS, 2, EDGE, LANES), f32),
            pltpu.VMEM((VELS, 2, EDGE, LANES), f32),
            pltpu.VMEM((3, 2, EDGE, LANES), f32),
            pltpu.VMEM((2, EDGE, LANES), f32),
            pltpu.VMEM((MODES, NIN, 2 * LANES), f32),
            pltpu.VMEM((2, EDGE, LANES), f32),
            pltpu.VMEM((VELS - 1, 2, EDGE, LANES), f32),
            pltpu.VMEM((3, 2, EDGE, LANES), f32),
        ]
        + [pltpu.VMEM((2 * REACH + 1, ROWS, LANES), f32) for _ in range(STEPS)]
        + [
            pltpu.VMEM((inner, LANES), f32),
            pltpu.VMEM((outer, LANES), f32),
            dma((7,)),
            dma((STEPS, 4)),
            dma((STEPS, 4)),
            dma((inner - 1,)),
            dma((inner - 1,)),
            dma((outer - 1,)),
            dma((outer - 1,)),
        ],
        compiler_params=pltpu.CompilerParams(collective_id=0, has_side_effects=True),
        name="adjoint_steps",
    )(
        adjoint.reshape((VELS,) + shape),
        velocity.reshape((3,) + shape),
        relax.reshape(shape),
        fluid_words,
        neighbours,
        inlet_ids,
        basis,
    )
    return (out.reshape(1, VELS, EDGE * EDGE * EDGE), grad.reshape(MODES))


def solution(mesh):
    return jax.shard_map(
        on_device,
        mesh=mesh,
        in_specs=(
            P("blk", None, None),
            P("blk", None, None),
            P("blk", None),
            P("blk", None),
            P("blk", None),
            P(),
            P(),
        ),
        out_specs=(P("blk", None, None), P()),
        check_vma=False,
    )
```

```python
import jax
import jax.numpy as jnp
import numpy as np
from jax import lax
from jax.experimental import pallas as pl
from jax.experimental.pallas import tpu as pltpu
from jax.sharding import PartitionSpec as P

EDGE = 16
VELS = 19
NEIGHBOURS = 18
REACH = 2
STEPS = 4
LANES = 128
NIN = 16
MODES = 8

C = np.array(
    [
        [0, 0, 0],
        [1, 0, 0],
        [-1, 0, 0],
        [0, 1, 0],
        [0, -1, 0],
        [0, 0, 1],
        [0, 0, -1],
        [1, 1, 0],
        [-1, -1, 0],
        [1, -1, 0],
        [-1, 1, 0],
        [1, 0, 1],
        [-1, 0, -1],
        [1, 0, -1],
        [-1, 0, 1],
        [0, 1, 1],
        [0, -1, -1],
        [0, 1, -1],
        [0, -1, 1],
    ],
    dtype=np.int32,
)
OPP = [0, 2, 1, 4, 3, 6, 5, 8, 7, 10, 9, 12, 11, 14, 13, 16, 15, 18, 17]
DIRECTION = {tuple(int(v) for v in C[k + 1]): k for k in range(NEIGHBOURS)}

FLUID = -1


def members(axis, sign):
    found = [i for i in range(VELS) if C[i][axis] == sign]
    return sorted(found, key=lambda i: int(np.abs(C[i]).sum()), reverse=True)


Z_ROWS, Y_ROWS, AXIS_ROWS, X_ROWS, X_FLUID, YZ_FLUID = 0, 16, 32, 48, 68, 72
SENT, ROWS = 68, 88
SIGNS = (1, -1)
Z_NUMBER = {i: n for n, i in enumerate([i for s in SIGNS for i in members(2, s)[:4]])}
Y_NUMBER = {i: n for n, i in enumerate([i for s in SIGNS for i in members(1, s)[:4]])}
X_NUMBER = {i: n for n, i in enumerate([i for s in SIGNS for i in members(0, s)])}
CUT = 12
OWN = REACH


def sign_index(sign):
    return 0 if sign == 1 else 1


def x_row(item, sign, yh):
    if item == FLUID:
        return X_FLUID + 2 * sign_index(sign) + yh
    return X_ROWS + 2 * X_NUMBER[item] + yh


def lane_roll(value, by):
    by = by % LANES
    return value if by == 0 else pltpu.roll(value, LANES - by, 1)


def row_roll(value, by):
    return pltpu.roll(value, (-by) % EDGE, 0)


class Masks:
    def __init__(self):
        self.lane = lax.broadcasted_iota(jnp.int32, (EDGE, LANES), 1)
        self.row = lax.broadcasted_iota(jnp.int32, (EDGE, LANES), 0)
        self.z = self.lane % EDGE
        self.yl = self.lane // EDGE


def put(block, mask, value):
    return value if block is None else jnp.where(mask, value, block)


def pack_axis(load, items, masks):
    block = None
    for sign in SIGNS:
        yh, start = (0, 0) if sign == 1 else (1, LANES - EDGE)
        plane = load(items[(1, sign)], yh)
        at = 4 * sign_index(sign) * EDGE + 4
        first = lane_roll(plane, start - at)
        second = lane_roll(plane, start + CUT - at - EDGE)
        block = put(block, masks.yl == at // EDGE, first)
        block = put(block, masks.yl == at // EDGE + 1, second)
    for sign in SIGNS:
        start = 0 if sign == 1 else EDGE - 1
        for yh in range(2):
            slot = 2 * sign_index(sign) + yh
            block = put(block, masks.z == slot, lane_roll(load(items[(2, sign)], yh), start - slot))
    return block


def pack(package, a, fluid, masks):
    def load(item, yh):
        return fluid[yh] if item == FLUID else a[item, yh]

    block = None
    for sign in SIGNS:
        start = 0 if sign == 1 else EDGE - 1
        for item in members(2, sign)[:4]:
            for yh in range(2):
                slot = 2 * Z_NUMBER[item] + yh
                block = put(block, masks.z == slot, lane_roll(load(item, yh), start - slot))
    package[pl.ds(Z_ROWS, EDGE), :] = block
    block = None
    for sign in SIGNS:
        yh, start = (0, 0) if sign == 1 else (1, LANES - EDGE)
        for item in members(1, sign)[:4]:
            number = Y_NUMBER[item]
            block = put(block, masks.yl == number, lane_roll(load(item, yh), start - number * EDGE))
    package[pl.ds(Y_ROWS, EDGE), :] = block
    axis = {(1, 1): 3, (1, -1): 4, (2, 1): 5, (2, -1): 6}
    package[pl.ds(AXIS_ROWS, EDGE), :] = pack_axis(load, axis, masks)
    for sign in SIGNS:
        x_at = 0 if sign == 1 else EDGE - 1
        for item in members(0, sign):
            for yh in range(2):
                package[pl.ds(x_row(item, sign, yh), 1), :] = a[item, yh, pl.ds(x_at, 1), :]
        if fluid is not None:
            for yh in range(2):
                package[pl.ds(x_row(FLUID, sign, yh), 1), :] = fluid[yh, pl.ds(x_at, 1), :]
    if fluid is not None:
        package[pl.ds(YZ_FLUID, EDGE), :] = pack_axis(load, {key: FLUID for key in axis}, masks)


def y_plane(ghost, direction, item, sign, at, masks, only=None):
    if item in Y_NUMBER:
        return lane_roll(ghost(direction, Y_ROWS, EDGE), Y_NUMBER[item] * EDGE - at)
    block = ghost(direction, YZ_FLUID if item == FLUID else AXIS_ROWS, EDGE)
    start = 4 * sign_index(sign) * EDGE + 4
    first = lane_roll(block, start - at) if only is None or only < CUT else None
    second = lane_roll(block, start + EDGE - CUT - at) if only is None or only >= CUT else None
    if first is None or second is None:
        return second if first is None else first
    return jnp.where((masks.lane + (LANES - at)) % LANES < CUT, first, second)


def z_plane(ghost, direction, item, sign, yh, target):
    if item in Z_NUMBER:
        return lane_roll(ghost(direction, Z_ROWS, EDGE), 2 * Z_NUMBER[item] + yh - target)
    block = ghost(direction, YZ_FLUID if item == FLUID else AXIS_ROWS, EDGE)
    return lane_roll(block, 2 * sign_index(sign) + yh - target)


def inside(field, c, masks):
    cx, cy, cz = (int(v) for v in c)
    v0, v1 = field
    if cx:
        v0, v1 = row_roll(v0, cx), row_roll(v1, cx)
    if cy == 1:
        take = masks.lane < EDGE
        v0, v1 = jnp.where(take, v1, v0), v1
    elif cy == -1:
        take = masks.lane >= LANES - EDGE
        v0, v1 = v0, jnp.where(take, v0, v1)
    by = cy * EDGE + cz
    return lane_roll(v0, by), lane_roll(v1, by)


def beyond(c, yh, masks):
    cx, cy, cz = (int(v) for v in c)
    out = None
    if cx:
        out = masks.row == (EDGE - 1 if cx == 1 else 0)
    if cy and yh == (1 if cy == 1 else 0):
        last = masks.yl == (LANES // EDGE - 1 if cy == 1 else 0)
        out = last if out is None else out | last
    if cz:
        last = masks.z == (EDGE - 1 if cz == 1 else 0)
        out = last if out is None else out | last
    return out


HALF = 8


def outside(item, c, ghost, masks):
    cx, cy, cz = (int(v) for v in c)
    both = [(yh, half) for yh in range(2) for half in range(2)]

    def part(value, half):
        return value[HALF * half : HALF * (half + 1)]

    if cx:
        x_half = 1 if cx == 1 else 0
        x_last = masks.row[:HALF] == (HALF - 1 if cx == 1 else 0)
        x_line = [ghost((cx, 0, 0), x_row(item, cx, yh), 1) for yh in range(2)]
    if cy:
        y_half = 1 if cy == 1 else 0
        at, final = (0, LANES - EDGE) if cy == 1 else (LANES - EDGE, 0)
        plane = y_plane(ghost, (0, cy, 0), item, cy, final - cz, masks)
    if cz:
        target = EDGE - 1 if cz == 1 else 0
        source = EDGE - 1 - target
        g = [z_plane(ghost, (0, 0, cz), item, cz, yh, target) for yh in range(2)]
    if cx and not cy and not cz:
        return {(yh, x_half): jnp.broadcast_to(x_line[yh], (HALF, LANES)) for yh in range(2)}
    if cy and not cx and not cz:
        return {(y_half, half): part(plane, half) for half in range(2)}
    if cz and not cx and not cy:
        return {(yh, half): part(g[yh], half) for yh, half in both}
    if cx and cy:
        plane = row_roll(plane, cx)
        line = ghost((cx, cy, 0), x_row(item, cx, 1 - y_half), 1)
        lane = masks.lane[:1]
        take = lane < EDGE if cy == 1 else lane >= LANES - EDGE
        corner, other = (1, 0) if cy == 1 else (0, 1)
        row = [None, None]
        row[corner] = lane_roll(jnp.where(take, line, x_line[corner]), cy * EDGE)
        row[other] = lane_roll(jnp.where(take, x_line[corner], x_line[other]), cy * EDGE)
        return {
            (other, x_half): jnp.broadcast_to(row[other], (HALF, LANES)),
            (corner, x_half): jnp.where(x_last, row[corner], part(plane, x_half)),
            (corner, 1 - x_half): part(plane, 1 - x_half),
        }
    if cx and cz:
        found = {}
        for yh in range(2):
            line = lane_roll(ghost((cx, 0, cz), x_row(item, cx, yh), 1), source - target)
            row = jnp.where(masks.z[:1] == target, line, lane_roll(x_line[yh], cz))
            rolled = row_roll(g[yh], cx)
            found[(yh, x_half)] = jnp.where(x_last, row, part(rolled, x_half))
            found[(yh, 1 - x_half)] = part(rolled, 1 - x_half)
        return found
    line = y_plane(ghost, (0, cy, cz), item, cy, at + target - source, masks, source)
    if cy == 1:
        take = masks.lane < EDGE
        g = [jnp.where(take, g[1], g[0]), jnp.where(take, line, g[1])]
    else:
        take = masks.lane >= LANES - EDGE
        g = [jnp.where(take, line, g[0]), jnp.where(take, g[0], g[1])]
    g = [lane_roll(v, cy * EDGE) for v in g]
    g[y_half] = jnp.where(masks.z == target, g[y_half], plane)
    return {(yh, half): part(g[yh], half) for yh, half in both}


def collide(b, u, k, g, e):
    ux, uy, uz = u
    pairs = [(i, i + 1) for i in range(1, VELS, 2)]
    s = {i: b[i] + b[j] for i, j in pairs}
    d = {i: b[i] - b[j] for i, j in pairs}
    p, q, r = s[7] + s[9], s[11] + s[13], s[15] + s[17]
    sx, sy, sz = s[1] + s[1], s[3] + s[3], s[5] + s[5]
    mxx, myy, mzz = sx + (p + q), sy + (p + r), sz + (q + r)
    mxy, mxz, myz = s[7] - s[9], s[11] - s[13], s[15] - s[17]
    m0 = 12.0 * b[0] + (sx + sy + sz) + (p + q + r)
    m1x = (d[1] + d[1]) + (d[7] + d[9]) + (d[11] + d[13])
    m1y = (d[3] + d[3]) + (d[7] - d[9]) + (d[15] + d[17])
    m1z = (d[5] + d[5]) + (d[11] - d[13]) + (d[15] - d[17])
    nx = mxx * ux + mxy * uy + mxz * uz
    ny = mxy * ux + myy * uy + myz * uz
    nz = mxz * ux + myz * uy + mzz * uz
    vx = g * (m1x + 3.0 * nx - ux * m0)
    vy = g * (m1y + 3.0 * ny - uy * m0)
    vz = g * (m1z + 3.0 * nz - uz * m0)
    o = g * (m0 * e - 1.5 * (ux * nx + uy * ny + uz * nz))
    v = {1: vx, 3: vy, 5: vz, 7: vx + vy, 9: vx - vy, 11: vx + vz, 13: vx - vz, 15: vy + vz, 17: vy - vz}
    out = [k * b[0] + o]
    for i, j in pairs:
        out.append(k * b[i] + (o + v[i]))
        out.append(k * b[j] + (o - v[i]))
    return out


AHEAD, BEHIND, SIBLING, CROSS = OWN + 2, OWN - 2, OWN + 1, OWN - 1


def body(n, inner, *refs):
    (a_hbm, vel_hbm, relax_hbm, words, nbrs, ids, basis_hbm) = refs[:7]
    (out_hbm, grad) = refs[7:9]
    (a, b, vel, relax, basis, fluid, bits, coef, ghost_bits, spread) = refs[9:19]
    bufs = refs[19 : 19 + STEPS]
    (part1, part2, local_sem, send_sem, recv_sem, sum_send1, sum_recv1, sum_send2, sum_recv2) = refs[19 + STEPS :]
    me = lax.axis_index("blk")
    outer = n // inner
    place = me % inner
    group = me // inner
    way = 1 - 2 * (me % 2)
    ahead, behind, sibling, cross = me + 2 * way, me - 2 * way, me + way, me - way
    has_ahead = (ahead >= 0) & (ahead < n)
    has_behind = (behind >= 0) & (behind < n)
    inner_peers = [group * inner + (place + j) % inner for j in range(1, inner)]
    outer_peers = [((group + j) % outer) * inner + place for j in range(1, outer)]

    barrier = pltpu.get_barrier_semaphore()

    def greet(peer):
        pl.semaphore_signal(barrier, inc=1, device_id=(peer,), device_id_type=pl.DeviceIdType.MESH)

    pl.when(has_ahead)(lambda: greet(ahead))
    pl.when(has_behind)(lambda: greet(behind))
    pl.when(has_behind)(lambda: greet(cross))
    for peer in [sibling] + inner_peers + outer_peers:
        greet(peer)
    greetings = inner + outer - 1 + has_ahead.astype(jnp.int32) + 2 * has_behind.astype(jnp.int32)

    loads = []
    for yh in range(2):
        loads.append(pltpu.make_async_copy(a_hbm.at[:, :, yh, :], a.at[:, yh], local_sem.at[yh]))
        loads.append(pltpu.make_async_copy(vel_hbm.at[:, :, yh, :], vel.at[:, yh], local_sem.at[2 + yh]))
        loads.append(pltpu.make_async_copy(relax_hbm.at[:, yh, :], relax.at[yh], local_sem.at[4 + yh]))
    load_basis = pltpu.make_async_copy(basis_hbm, basis, local_sem.at[6])
    load_basis.start()
    for load in loads:
        load.start()

    masks = Masks()
    for yh in range(2):
        word = jnp.zeros((EDGE, LANES), jnp.int32)
        for x in range(EDGE):
            at = x * 8 + yh * 4
            w = [words[0, at + j] for j in range(4)]
            line = jnp.where(
                masks.lane < 64,
                jnp.where(masks.lane < 32, w[0], w[1]),
                jnp.where(masks.lane < 96, w[2], w[3]),
            )
            word = jnp.where(masks.row == x, line, word)
        bit = jnp.bitwise_and(jnp.right_shift(word, masks.lane % 32), 1)
        fluid[yh] = bit.astype(jnp.float32)

    is_inlet = jnp.int32(0)
    for r in range(NIN):
        is_inlet = is_inlet + (ids[r] == me).astype(jnp.int32)
    keep = 1.0 - is_inlet.astype(jnp.float32)
    keep_z = jnp.where(masks.z == 0, keep, 1.0)
    slot_of = []
    present = []
    for k in range(NEIGHBOURS):
        entry = nbrs[0, k]
        there = (entry >= 0).astype(jnp.int32)
        slot = jnp.clip(OWN + (entry - me) * way, 0, 2 * REACH)
        slot_of.append(slot * there + OWN * (1 - there))
        present.append(there.astype(jnp.float32))

    def halo(step, index, source, target, peer):
        rows = pl.ds(0, ROWS if step == 0 else SENT)
        return pltpu.make_async_remote_copy(
            src_ref=bufs[step].at[source, rows],
            dst_ref=bufs[step].at[target, rows],
            send_sem=send_sem.at[step, index],
            recv_sem=recv_sem.at[step, index],
            device_id=(peer,),
            device_id_type=pl.DeviceIdType.MESH,
        )

    def sum_copy(part, send, recv, j, peer):
        return pltpu.make_async_remote_copy(
            src_ref=part.at[pl.ds(0, 1)],
            dst_ref=part.at[pl.ds(j, 1)],
            send_sem=send.at[j - 1],
            recv_sem=recv.at[j - 1],
            device_id=(peer,),
            device_id_type=pl.DeviceIdType.MESH,
        )

    layer = [jnp.zeros((EDGE, LANES), jnp.float32) for _ in range(2)]
    for load in loads:
        load.wait()
    exchanges = []
    for step in range(STEPS):
        buf = bufs[step]
        pack(buf.at[OWN], a, fluid if step == 0 else None, masks)
        if step == 0:
            pl.semaphore_wait(barrier, greetings)
        to_ahead = halo(step, 0, OWN, BEHIND, ahead)
        to_behind = halo(step, 1, OWN, AHEAD, behind)
        to_sibling = halo(step, 2, OWN, SIBLING, sibling)
        to_cross = halo(step, 3, OWN, CROSS, cross)
        exchanges.append((to_ahead, to_behind, to_sibling, to_cross))
        pl.when(has_behind)(to_behind.start)
        pl.when(has_behind)(to_cross.start)
        pl.when(has_ahead)(to_ahead.start)
        to_sibling.start()
        for yh in range(2):
            layer[yh] = layer[yh] + (2.0 * a[5, yh] + ((a[11, yh] + a[14, yh]) + (a[15, yh] + a[18, yh])))
            if step == 0:
                f = fluid[yh]
                squared = vel[0, yh] * vel[0, yh] + vel[1, yh] * vel[1, yh] + vel[2, yh] * vel[2, yh]
                coef[0, yh] = f * (1.0 - relax[yh])
                coef[1, yh] = f * relax[yh] * (1.0 / 12.0)
                coef[2, yh] = (1.0 / 3.0) + 0.5 * squared
        if step == 0:
            load_basis.wait()
            row = lax.broadcasted_iota(jnp.int32, (EDGE, 2 * LANES), 0)
            flat = lax.broadcasted_iota(jnp.int32, (EDGE, 2 * LANES), 1)
            mine = jnp.zeros((EDGE, 2 * LANES), jnp.float32)
            for r in range(NIN):
                mine = jnp.where(row == r, (ids[r] == me).astype(jnp.float32), mine)
            lines = []
            for m in range(MODES):
                line = jnp.sum(basis[m] * mine, axis=0, keepdims=True)
                lines.append(jnp.where(flat // EDGE == row, line, 0.0))
            lines = jnp.concatenate(lines, axis=0)
            q = lax.broadcasted_iota(jnp.int32, (2 * LANES, LANES), 0)
            site = lax.broadcasted_iota(jnp.int32, (2 * LANES, LANES), 1)
            for yh in range(2):
                pick = ((site % EDGE == 0) & (site // EDGE + 8 * yh == q % EDGE)).astype(jnp.float32)
                placed = jnp.dot(lines, pick, precision=lax.Precision.HIGHEST, preferred_element_type=jnp.float32)
                for m in range(MODES):
                    spread[m, yh] = placed[m * EDGE : (m + 1) * EDGE] * (fluid[yh] * (1.0 / 12.0))
        if step == STEPS - 1:
            mode = lax.broadcasted_iota(jnp.int32, (MODES, LANES), 0)
            total = jnp.zeros((MODES, LANES), jnp.float32)
            for m in range(MODES):
                product = spread[m, 0] * layer[0] + spread[m, 1] * layer[1]
                total = jnp.where(mode == m, jnp.sum(product, axis=0, keepdims=True), total)
            total = jnp.sum(total, axis=1, keepdims=True)
            at_mode = lax.broadcasted_iota(jnp.int32, (MODES, LANES), 1) == mode
            part1[pl.ds(0, 1), :] = jnp.sum(jnp.where(at_mode, total, 0.0), axis=0, keepdims=True)
            sums1 = [sum_copy(part1, sum_send1, sum_recv1, j, inner_peers[j - 1]) for j in range(1, inner)]
            for copy in sums1:
                copy.start()
        for yh in range(2):
            b[0, yh] = a[0, yh]
        for i in range(1, VELS):
            if step == 0:
                moved = inside((fluid[0], fluid[1]), C[i], masks)
                for yh in range(2):
                    out = beyond(C[i], yh, masks)
                    bits[i - 1, yh] = moved[yh] if out is None else jnp.where(out, 0.0, moved[yh])
            moved = inside((a[i, 0], a[i, 1]), C[i], masks)
            for yh in range(2):
                back = a[OPP[i], yh]
                if C[i][2] == -1:
                    back = back * keep_z
                b[i, yh] = jnp.where(bits[i - 1, yh] > 0.5, moved[yh], back)
        if step == STEPS - 1:
            for copy in sums1:
                copy.wait_recv()
            part2[pl.ds(0, 1), :] = jnp.sum(part1[...], axis=0, keepdims=True)
            sums2 = [sum_copy(part2, sum_send2, sum_recv2, j, outer_peers[j - 1]) for j in range(1, outer)]
            for copy in sums2:
                copy.start()
        to_sibling.wait_recv()
        pl.when(has_ahead)(to_behind.wait_recv)

        @pl.when(has_behind)
        def _():
            to_ahead.wait_recv()
            to_cross.wait_recv()


        def ghost(direction, row, rows):
            return buf[slot_of[DIRECTION[direction]], pl.ds(row, rows), :]

        if step == 0:

            def ghost_fluid(direction, row, rows):
                k = DIRECTION[direction]
                return buf[slot_of[k], pl.ds(row, rows), :] * present[k]

            for i in range(1, VELS):
                for (yh, half), value in outside(FLUID, C[i], ghost_fluid, masks).items():
                    rows = slice(HALF * half, HALF * (half + 1))
                    value = jnp.where(beyond(C[i], yh, masks)[rows], value, 0.0)
                    if C[i][2] == -1:
                        value = value * keep_z[rows]
                    ghost_bits[i - 1, yh, pl.ds(HALF * half, HALF), :] = value
        for i in range(1, VELS):
            for (yh, half), value in outside(i, C[i], ghost, masks).items():
                rows = pl.ds(HALF * half, HALF)
                b[i, yh, rows, :] = jnp.where(ghost_bits[i - 1, yh, rows, :] > 0.5, value, b[i, yh, rows, :])
        stores = []
        for yh in range(2):
            for half in range(2):
                rows = pl.ds(HALF * half, HALF)
                new = collide(
                    [b[i, yh, rows, :] for i in range(VELS)],
                    [vel[c, yh, rows, :] for c in range(3)],
                    coef[0, yh, rows, :],
                    coef[1, yh, rows, :],
                    coef[2, yh, rows, :],
                )
                for i in range(VELS):
                    a[i, yh, rows, :] = new[i]
                if step == STEPS - 1:
                    store = pltpu.make_async_copy(
                        a.at[:, yh, rows], out_hbm.at[:, rows, yh, :], local_sem.at[2 * yh + half]
                    )
                    store.start()
                    stores.append(store)

    for copy in sums2:
        copy.wait_recv()
    grad[...] = jnp.sum(part2[...], axis=0, keepdims=True)[:, :MODES]
    for to_ahead, to_behind, to_sibling, to_cross in exchanges:
        pl.when(has_ahead)(to_ahead.wait_send)
        pl.when(has_behind)(to_behind.wait_send)
        to_sibling.wait_send()
        pl.when(has_behind)(to_cross.wait_send)
    for copy in sums1 + sums2:
        copy.wait_send()
    for store in stores:
        store.wait()


def on_device(adjoint, velocity, relax, fluid_words, neighbours, inlet_ids, basis):
    n = lax.axis_size("blk")
    inner = 8 if n % 64 == 0 else 4
    outer = n // inner
    f32 = jnp.float32
    shape = (EDGE, 2, LANES)
    any_space = pl.BlockSpec(memory_space=pl.ANY)
    smem = pl.BlockSpec(memory_space=pltpu.SMEM)
    dma = pltpu.SemaphoreType.DMA
    out, grad = pl.pallas_call(
        lambda *refs: body(n, inner, *refs),
        out_shape=(
            jax.ShapeDtypeStruct((VELS,) + shape, f32),
            jax.ShapeDtypeStruct((1, MODES), f32),
        ),
        in_specs=[any_space, any_space, any_space, smem, smem, smem, any_space],
        out_specs=(any_space, pl.BlockSpec(memory_space=pltpu.VMEM)),
        scratch_shapes=[
            pltpu.VMEM((VELS, 2, EDGE, LANES), f32),
            pltpu.VMEM((VELS, 2, EDGE, LANES), f32),
            pltpu.VMEM((3, 2, EDGE, LANES), f32),
            pltpu.VMEM((2, EDGE, LANES), f32),
            pltpu.VMEM((MODES, NIN, 2 * LANES), f32),
            pltpu.VMEM((2, EDGE, LANES), f32),
            pltpu.VMEM((VELS - 1, 2, EDGE, LANES), f32),
            pltpu.VMEM((3, 2, EDGE, LANES), f32),
            pltpu.VMEM((VELS - 1, 2, EDGE, LANES), f32),
            pltpu.VMEM((MODES, 2, EDGE, LANES), f32),
        ]
        + [pltpu.VMEM((2 * REACH + 1, ROWS, LANES), f32) for _ in range(STEPS)]
        + [
            pltpu.VMEM((inner, LANES), f32),
            pltpu.VMEM((outer, LANES), f32),
            dma((7,)),
            dma((STEPS, 4)),
            dma((STEPS, 4)),
            dma((inner - 1,)),
            dma((inner - 1,)),
            dma((outer - 1,)),
            dma((outer - 1,)),
        ],
        compiler_params=pltpu.CompilerParams(collective_id=0, has_side_effects=True),
        name="adjoint_steps",
    )(
        adjoint.reshape((VELS,) + shape),
        velocity.reshape((3,) + shape),
        relax.reshape(shape),
        fluid_words,
        neighbours,
        inlet_ids,
        basis,
    )
    return (out.reshape(1, VELS, EDGE * EDGE * EDGE), grad.reshape(MODES))


def solution(mesh):
    return jax.shard_map(
        on_device,
        mesh=mesh,
        in_specs=(
            P("blk", None, None),
            P("blk", None, None),
            P("blk", None),
            P("blk", None),
            P("blk", None),
            P(),
            P(),
        ),
        out_specs=(P("blk", None, None), P()),
        check_vma=False,
    )
```

```python
import functools

import jax
import jax.numpy as jnp
import numpy as np
from jax import lax
from jax.experimental import pallas as pl
from jax.experimental.pallas import tpu as pltpu
from jax.sharding import PartitionSpec as P

EDGE = 16
VELS = 19
NEIGHBOURS = 18
REACH = 2
STEPS = 4
LANES = 128
NIN = 16
MODES = 8

C = np.array(
    [
        [0, 0, 0],
        [1, 0, 0],
        [-1, 0, 0],
        [0, 1, 0],
        [0, -1, 0],
        [0, 0, 1],
        [0, 0, -1],
        [1, 1, 0],
        [-1, -1, 0],
        [1, -1, 0],
        [-1, 1, 0],
        [1, 0, 1],
        [-1, 0, -1],
        [1, 0, -1],
        [-1, 0, 1],
        [0, 1, 1],
        [0, -1, -1],
        [0, 1, -1],
        [0, -1, 1],
    ],
    dtype=np.int32,
)
OPP = [0, 2, 1, 4, 3, 6, 5, 8, 7, 10, 9, 12, 11, 14, 13, 16, 15, 18, 17]
DIRECTION = {tuple(int(v) for v in C[k + 1]): k for k in range(NEIGHBOURS)}

FLUID = -1


def members(axis, sign):
    found = [i for i in range(VELS) if C[i][axis] == sign]
    return sorted(found, key=lambda i: int(np.abs(C[i]).sum()), reverse=True)


Z_ROWS, Y_ROWS, AXIS_ROWS, X_ROWS, X_FLUID, YZ_FLUID = 0, 16, 32, 48, 68, 72
SENT, ROWS = 68, 88
SIGNS = (1, -1)
Z_NUMBER = {i: n for n, i in enumerate([i for s in SIGNS for i in members(2, s)[:4]])}
Y_NUMBER = {i: n for n, i in enumerate([i for s in SIGNS for i in members(1, s)[:4]])}
X_NUMBER = {i: n for n, i in enumerate([i for s in SIGNS for i in members(0, s)])}
CUT = 12
OWN = REACH


def sign_index(sign):
    return 0 if sign == 1 else 1


def x_row(item, sign, yh):
    if item == FLUID:
        return X_FLUID + 2 * sign_index(sign) + yh
    return X_ROWS + 2 * X_NUMBER[item] + yh


def lane_roll(value, by):
    by = by % LANES
    return value if by == 0 else pltpu.roll(value, LANES - by, 1)


def row_roll(value, by):
    return pltpu.roll(value, (-by) % EDGE, 0)


class Masks:
    def __init__(self):
        self.lane = lax.broadcasted_iota(jnp.int32, (EDGE, LANES), 1)
        self.row = lax.broadcasted_iota(jnp.int32, (EDGE, LANES), 0)
        self.z = self.lane % EDGE
        self.yl = self.lane // EDGE


def put(block, mask, value):
    return value if block is None else jnp.where(mask, value, block)


def pack_axis(load, items, masks):
    block = None
    for sign in SIGNS:
        yh, start = (0, 0) if sign == 1 else (1, LANES - EDGE)
        plane = load(items[(1, sign)], yh)
        at = 4 * sign_index(sign) * EDGE + 4
        first = lane_roll(plane, start - at)
        second = lane_roll(plane, start + CUT - at - EDGE)
        block = put(block, masks.yl == at // EDGE, first)
        block = put(block, masks.yl == at // EDGE + 1, second)
    for sign in SIGNS:
        start = 0 if sign == 1 else EDGE - 1
        for yh in range(2):
            slot = 2 * sign_index(sign) + yh
            block = put(block, masks.z == slot, lane_roll(load(items[(2, sign)], yh), start - slot))
    return block


def pack(package, a, fluid, masks):
    def load(item, yh):
        return fluid[yh] if item == FLUID else a[item, yh]

    block = None
    for sign in SIGNS:
        start = 0 if sign == 1 else EDGE - 1
        for item in members(2, sign)[:4]:
            for yh in range(2):
                slot = 2 * Z_NUMBER[item] + yh
                block = put(block, masks.z == slot, lane_roll(load(item, yh), start - slot))
    package[pl.ds(Z_ROWS, EDGE), :] = block
    block = None
    for sign in SIGNS:
        yh, start = (0, 0) if sign == 1 else (1, LANES - EDGE)
        for item in members(1, sign)[:4]:
            number = Y_NUMBER[item]
            block = put(block, masks.yl == number, lane_roll(load(item, yh), start - number * EDGE))
    package[pl.ds(Y_ROWS, EDGE), :] = block
    axis = {(1, 1): 3, (1, -1): 4, (2, 1): 5, (2, -1): 6}
    package[pl.ds(AXIS_ROWS, EDGE), :] = pack_axis(load, axis, masks)
    for sign in SIGNS:
        x_at = 0 if sign == 1 else EDGE - 1
        for item in members(0, sign):
            for yh in range(2):
                package[pl.ds(x_row(item, sign, yh), 1), :] = a[item, yh, pl.ds(x_at, 1), :]
        if fluid is not None:
            for yh in range(2):
                package[pl.ds(x_row(FLUID, sign, yh), 1), :] = fluid[yh, pl.ds(x_at, 1), :]
    if fluid is not None:
        package[pl.ds(YZ_FLUID, EDGE), :] = pack_axis(load, {key: FLUID for key in axis}, masks)


def y_plane(ghost, direction, item, sign, at, masks, only=None):
    if item in Y_NUMBER:
        return lane_roll(ghost(direction, Y_ROWS, EDGE), Y_NUMBER[item] * EDGE - at)
    block = ghost(direction, YZ_FLUID if item == FLUID else AXIS_ROWS, EDGE)
    start = 4 * sign_index(sign) * EDGE + 4
    first = lane_roll(block, start - at) if only is None or only < CUT else None
    second = lane_roll(block, start + EDGE - CUT - at) if only is None or only >= CUT else None
    if first is None or second is None:
        return second if first is None else first
    return jnp.where((masks.lane + (LANES - at)) % LANES < CUT, first, second)


def z_plane(ghost, direction, item, sign, yh, target):
    if item in Z_NUMBER:
        return lane_roll(ghost(direction, Z_ROWS, EDGE), 2 * Z_NUMBER[item] + yh - target)
    block = ghost(direction, YZ_FLUID if item == FLUID else AXIS_ROWS, EDGE)
    return lane_roll(block, 2 * sign_index(sign) + yh - target)


def inside(field, c, masks):
    cx, cy, cz = (int(v) for v in c)
    v0, v1 = field
    if cx:
        v0, v1 = row_roll(v0, cx), row_roll(v1, cx)
    if cy == 1:
        take = masks.lane < EDGE
        v0, v1 = jnp.where(take, v1, v0), v1
    elif cy == -1:
        take = masks.lane >= LANES - EDGE
        v0, v1 = v0, jnp.where(take, v0, v1)
    by = cy * EDGE + cz
    return lane_roll(v0, by), lane_roll(v1, by)


def beyond(c, yh, masks):
    cx, cy, cz = (int(v) for v in c)
    out = None
    if cx:
        out = masks.row == (EDGE - 1 if cx == 1 else 0)
    if cy and yh == (1 if cy == 1 else 0):
        last = masks.yl == (LANES // EDGE - 1 if cy == 1 else 0)
        out = last if out is None else out | last
    if cz:
        last = masks.z == (EDGE - 1 if cz == 1 else 0)
        out = last if out is None else out | last
    return out


HALF = 8


def outside(item, c, ghost, masks):
    cx, cy, cz = (int(v) for v in c)
    both = [(yh, half) for yh in range(2) for half in range(2)]

    def part(value, half):
        return value[HALF * half : HALF * (half + 1)]

    if cx:
        x_half = 1 if cx == 1 else 0
        x_last = masks.row[:HALF] == (HALF - 1 if cx == 1 else 0)
        x_line = [ghost((cx, 0, 0), x_row(item, cx, yh), 1) for yh in range(2)]
    if cy:
        y_half = 1 if cy == 1 else 0
        at, final = (0, LANES - EDGE) if cy == 1 else (LANES - EDGE, 0)
        plane = y_plane(ghost, (0, cy, 0), item, cy, final - cz, masks)
    if cz:
        target = EDGE - 1 if cz == 1 else 0
        source = EDGE - 1 - target
        g = [z_plane(ghost, (0, 0, cz), item, cz, yh, target) for yh in range(2)]
    if cx and not cy and not cz:
        return {(yh, x_half): jnp.broadcast_to(x_line[yh], (HALF, LANES)) for yh in range(2)}
    if cy and not cx and not cz:
        return {(y_half, half): part(plane, half) for half in range(2)}
    if cz and not cx and not cy:
        return {(yh, half): part(g[yh], half) for yh, half in both}
    if cx and cy:
        plane = row_roll(plane, cx)
        line = ghost((cx, cy, 0), x_row(item, cx, 1 - y_half), 1)
        lane = masks.lane[:1]
        take = lane < EDGE if cy == 1 else lane >= LANES - EDGE
        corner, other = (1, 0) if cy == 1 else (0, 1)
        row = [None, None]
        row[corner] = lane_roll(jnp.where(take, line, x_line[corner]), cy * EDGE)
        row[other] = lane_roll(jnp.where(take, x_line[corner], x_line[other]), cy * EDGE)
        return {
            (other, x_half): jnp.broadcast_to(row[other], (HALF, LANES)),
            (corner, x_half): jnp.where(x_last, row[corner], part(plane, x_half)),
            (corner, 1 - x_half): part(plane, 1 - x_half),
        }
    if cx and cz:
        found = {}
        for yh in range(2):
            line = lane_roll(ghost((cx, 0, cz), x_row(item, cx, yh), 1), source - target)
            row = jnp.where(masks.z[:1] == target, line, lane_roll(x_line[yh], cz))
            rolled = row_roll(g[yh], cx)
            found[(yh, x_half)] = jnp.where(x_last, row, part(rolled, x_half))
            found[(yh, 1 - x_half)] = part(rolled, 1 - x_half)
        return found
    line = y_plane(ghost, (0, cy, cz), item, cy, at + target - source, masks, source)
    if cy == 1:
        take = masks.lane < EDGE
        g = [jnp.where(take, g[1], g[0]), jnp.where(take, line, g[1])]
    else:
        take = masks.lane >= LANES - EDGE
        g = [jnp.where(take, line, g[0]), jnp.where(take, g[0], g[1])]
    g = [lane_roll(v, cy * EDGE) for v in g]
    g[y_half] = jnp.where(masks.z == target, g[y_half], plane)
    return {(yh, half): part(g[yh], half) for yh, half in both}


def collide(b, u, k, g, e):
    ux, uy, uz = u
    pairs = [(i, i + 1) for i in range(1, VELS, 2)]
    s = {i: b[i] + b[j] for i, j in pairs}
    d = {i: b[i] - b[j] for i, j in pairs}
    p, q, r = s[7] + s[9], s[11] + s[13], s[15] + s[17]
    sx, sy, sz = s[1] + s[1], s[3] + s[3], s[5] + s[5]
    mxx, myy, mzz = sx + (p + q), sy + (p + r), sz + (q + r)
    mxy, mxz, myz = s[7] - s[9], s[11] - s[13], s[15] - s[17]
    m0 = 12.0 * b[0] + (sx + sy + sz) + (p + q + r)
    m1x = (d[1] + d[1]) + (d[7] + d[9]) + (d[11] + d[13])
    m1y = (d[3] + d[3]) + (d[7] - d[9]) + (d[15] + d[17])
    m1z = (d[5] + d[5]) + (d[11] - d[13]) + (d[15] - d[17])
    nx = mxx * ux + mxy * uy + mxz * uz
    ny = mxy * ux + myy * uy + myz * uz
    nz = mxz * ux + myz * uy + mzz * uz
    vx = g * (m1x + 3.0 * nx - ux * m0)
    vy = g * (m1y + 3.0 * ny - uy * m0)
    vz = g * (m1z + 3.0 * nz - uz * m0)
    o = g * (m0 * e - 1.5 * (ux * nx + uy * ny + uz * nz))
    v = {1: vx, 3: vy, 5: vz, 7: vx + vy, 9: vx - vy, 11: vx + vz, 13: vx - vz, 15: vy + vz, 17: vy - vz}
    out = [k * b[0] + o]
    for i, j in pairs:
        out.append(k * b[i] + (o + v[i]))
        out.append(k * b[j] + (o - v[i]))
    return out


AHEAD, BEHIND, SIBLING, CROSS = OWN + 2, OWN - 2, OWN + 1, OWN - 1


def body(n, inner, *refs):
    (a_hbm, vel_hbm, relax_hbm, words, nbrs, ids, basis_hbm) = refs[:7]
    (a, grad) = refs[7:9]
    (b, vel, relax, basis, fluid, bits, coef, ghost_bits, spread) = refs[9:18]
    bufs = refs[18 : 18 + STEPS]
    (part1, part2, local_sem, send_sem, recv_sem, sum_send1, sum_recv1, sum_send2, sum_recv2) = refs[18 + STEPS :]
    me = lax.axis_index("blk")
    outer = n // inner
    place = me % inner
    group = me // inner
    way = 1 - 2 * (me % 2)
    ahead, behind, sibling, cross = me + 2 * way, me - 2 * way, me + way, me - way
    has_ahead = (ahead >= 0) & (ahead < n)
    has_behind = (behind >= 0) & (behind < n)
    inner_peers = [group * inner + (place + j) % inner for j in range(1, inner)]
    outer_peers = [((group + j) % outer) * inner + place for j in range(1, outer)]

    barrier = pltpu.get_barrier_semaphore()

    def greet(peer):
        pl.semaphore_signal(barrier, inc=1, device_id=(peer,), device_id_type=pl.DeviceIdType.MESH)

    pl.when(has_ahead)(lambda: greet(ahead))
    pl.when(has_behind)(lambda: greet(behind))
    pl.when(has_behind)(lambda: greet(cross))
    for peer in [sibling] + inner_peers + outer_peers:
        greet(peer)
    greetings = inner + outer - 1 + has_ahead.astype(jnp.int32) + 2 * has_behind.astype(jnp.int32)

    loads = []
    for yh in range(2):
        loads.append(pltpu.make_async_copy(a_hbm.at[:, :, yh, :], a.at[:, yh], local_sem.at[yh]))
        loads.append(pltpu.make_async_copy(vel_hbm.at[:, :, yh, :], vel.at[:, yh], local_sem.at[2 + yh]))
        loads.append(pltpu.make_async_copy(relax_hbm.at[:, yh, :], relax.at[yh], local_sem.at[4 + yh]))
    load_basis = pltpu.make_async_copy(basis_hbm, basis, local_sem.at[6])
    load_basis.start()
    for load in loads:
        load.start()

    masks = Masks()
    for yh in range(2):
        word = jnp.zeros((EDGE, LANES), jnp.int32)
        for x in range(EDGE):
            at = x * 8 + yh * 4
            w = [words[0, at + j] for j in range(4)]
            line = jnp.where(
                masks.lane < 64,
                jnp.where(masks.lane < 32, w[0], w[1]),
                jnp.where(masks.lane < 96, w[2], w[3]),
            )
            word = jnp.where(masks.row == x, line, word)
        bit = jnp.bitwise_and(jnp.right_shift(word, masks.lane % 32), 1)
        fluid[yh] = bit.astype(jnp.float32)

    is_inlet = jnp.int32(0)
    for r in range(NIN):
        is_inlet = is_inlet + (ids[r] == me).astype(jnp.int32)
    keep = 1.0 - is_inlet.astype(jnp.float32)
    keep_z = jnp.where(masks.z == 0, keep, 1.0)
    slot_of = []
    present = []
    for k in range(NEIGHBOURS):
        entry = nbrs[0, k]
        there = (entry >= 0).astype(jnp.int32)
        slot = jnp.clip(OWN + (entry - me) * way, 0, 2 * REACH)
        slot_of.append(slot * there + OWN * (1 - there))
        present.append(there.astype(jnp.float32))

    def halo(step, index, source, target, peer):
        rows = pl.ds(0, ROWS if step == 0 else SENT)
        return pltpu.make_async_remote_copy(
            src_ref=bufs[step].at[source, rows],
            dst_ref=bufs[step].at[target, rows],
            send_sem=send_sem.at[step, index],
            recv_sem=recv_sem.at[step, index],
            device_id=(peer,),
            device_id_type=pl.DeviceIdType.MESH,
        )

    def sum_copy(part, send, recv, j, peer):
        return pltpu.make_async_remote_copy(
            src_ref=part.at[pl.ds(0, 1)],
            dst_ref=part.at[pl.ds(j, 1)],
            send_sem=send.at[j - 1],
            recv_sem=recv.at[j - 1],
            device_id=(peer,),
            device_id_type=pl.DeviceIdType.MESH,
        )

    layer = [jnp.zeros((EDGE, LANES), jnp.float32) for _ in range(2)]
    for load in loads:
        load.wait()
    exchanges = []
    for step in range(STEPS):
        buf = bufs[step]
        pack(buf.at[OWN], a, fluid if step == 0 else None, masks)
        if step == 0:
            pl.semaphore_wait(barrier, greetings)
        to_ahead = halo(step, 0, OWN, BEHIND, ahead)
        to_behind = halo(step, 1, OWN, AHEAD, behind)
        to_sibling = halo(step, 2, OWN, SIBLING, sibling)
        to_cross = halo(step, 3, OWN, CROSS, cross)
        exchanges.append((to_ahead, to_behind, to_sibling, to_cross))
        pl.when(has_behind)(to_behind.start)
        pl.when(has_behind)(to_cross.start)
        pl.when(has_ahead)(to_ahead.start)
        to_sibling.start()
        for yh in range(2):
            layer[yh] = layer[yh] + (2.0 * a[5, yh] + ((a[11, yh] + a[14, yh]) + (a[15, yh] + a[18, yh])))
            if step == 0:
                f = fluid[yh]
                squared = vel[0, yh] * vel[0, yh] + vel[1, yh] * vel[1, yh] + vel[2, yh] * vel[2, yh]
                coef[0, yh] = f * (1.0 - relax[yh])
                coef[1, yh] = f * relax[yh] * (1.0 / 12.0)
                coef[2, yh] = (1.0 / 3.0) + 0.5 * squared
        if step == 0:
            load_basis.wait()
            row = lax.broadcasted_iota(jnp.int32, (EDGE, 2 * LANES), 0)
            flat = lax.broadcasted_iota(jnp.int32, (EDGE, 2 * LANES), 1)
            mine = jnp.zeros((EDGE, 2 * LANES), jnp.float32)
            for r in range(NIN):
                mine = jnp.where(row == r, (ids[r] == me).astype(jnp.float32), mine)
            lines = []
            for m in range(MODES):
                line = jnp.sum(basis[m] * mine, axis=0, keepdims=True)
                lines.append(jnp.where(flat // EDGE == row, line, 0.0))
            lines = jnp.concatenate(lines, axis=0)
            q = lax.broadcasted_iota(jnp.int32, (2 * LANES, LANES), 0)
            site = lax.broadcasted_iota(jnp.int32, (2 * LANES, LANES), 1)
            for yh in range(2):
                pick = ((site % EDGE == 0) & (site // EDGE + 8 * yh == q % EDGE)).astype(jnp.float32)
                placed = jnp.dot(lines, pick, precision=lax.Precision.HIGHEST, preferred_element_type=jnp.float32)
                for m in range(MODES):
                    spread[m, yh] = placed[m * EDGE : (m + 1) * EDGE] * (fluid[yh] * (1.0 / 12.0))
        if step == STEPS - 1:
            mode = lax.broadcasted_iota(jnp.int32, (MODES, LANES), 0)
            total = jnp.zeros((MODES, LANES), jnp.float32)
            for m in range(MODES):
                product = spread[m, 0] * layer[0] + spread[m, 1] * layer[1]
                total = jnp.where(mode == m, jnp.sum(product, axis=0, keepdims=True), total)
            total = jnp.sum(total, axis=1, keepdims=True)
            at_mode = lax.broadcasted_iota(jnp.int32, (MODES, LANES), 1) == mode
            part1[pl.ds(0, 1), :] = jnp.sum(jnp.where(at_mode, total, 0.0), axis=0, keepdims=True)
            sums1 = [sum_copy(part1, sum_send1, sum_recv1, j, inner_peers[j - 1]) for j in range(1, inner)]
            for copy in sums1:
                copy.start()
        for yh in range(2):
            b[0, yh] = a[0, yh]
        for i in range(1, VELS):
            if step == 0:
                moved = inside((fluid[0], fluid[1]), C[i], masks)
                for yh in range(2):
                    out = beyond(C[i], yh, masks)
                    bits[i - 1, yh] = moved[yh] if out is None else jnp.where(out, 0.0, moved[yh])
            moved = inside((a[i, 0], a[i, 1]), C[i], masks)
            for yh in range(2):
                back = a[OPP[i], yh]
                if C[i][2] == -1:
                    back = back * keep_z
                b[i, yh] = jnp.where(bits[i - 1, yh] > 0.5, moved[yh], back)
        if step == STEPS - 1:
            for copy in sums1:
                copy.wait_recv()
            part2[pl.ds(0, 1), :] = jnp.sum(part1[...], axis=0, keepdims=True)
            sums2 = [sum_copy(part2, sum_send2, sum_recv2, j, outer_peers[j - 1]) for j in range(1, outer)]
            for copy in sums2:
                copy.start()
        to_sibling.wait_recv()
        pl.when(has_ahead)(to_behind.wait_recv)

        @pl.when(has_behind)
        def _():
            to_ahead.wait_recv()
            to_cross.wait_recv()


        def ghost(direction, row, rows):
            return buf[slot_of[DIRECTION[direction]], pl.ds(row, rows), :]

        if step == 0:

            def ghost_fluid(direction, row, rows):
                k = DIRECTION[direction]
                return buf[slot_of[k], pl.ds(row, rows), :] * present[k]

            for i in range(1, VELS):
                for (yh, half), value in outside(FLUID, C[i], ghost_fluid, masks).items():
                    rows = slice(HALF * half, HALF * (half + 1))
                    value = jnp.where(beyond(C[i], yh, masks)[rows], value, 0.0)
                    if C[i][2] == -1:
                        value = value * keep_z[rows]
                    ghost_bits[i - 1, yh, pl.ds(HALF * half, HALF), :] = value
        for i in range(1, VELS):
            for (yh, half), value in outside(i, C[i], ghost, masks).items():
                rows = pl.ds(HALF * half, HALF)
                b[i, yh, rows, :] = jnp.where(ghost_bits[i - 1, yh, rows, :] > 0.5, value, b[i, yh, rows, :])
        for yh in range(2):
            for half in range(2):
                rows = pl.ds(HALF * half, HALF)
                new = collide(
                    [b[i, yh, rows, :] for i in range(VELS)],
                    [vel[c, yh, rows, :] for c in range(3)],
                    coef[0, yh, rows, :],
                    coef[1, yh, rows, :],
                    coef[2, yh, rows, :],
                )
                for i in range(VELS):
                    a[i, yh, rows, :] = new[i]

    for copy in sums2:
        copy.wait_recv()
    grad[...] = jnp.sum(part2[...], axis=0, keepdims=True)[:, :MODES]
    for to_ahead, to_behind, to_sibling, to_cross in exchanges:
        pl.when(has_ahead)(to_ahead.wait_send)
        pl.when(has_behind)(to_behind.wait_send)
        to_sibling.wait_send()
        pl.when(has_behind)(to_cross.wait_send)
    for copy in sums1 + sums2:
        copy.wait_send()


def hand_over(parts, state, grad_in, out, grad, sem):
    stores = [pltpu.make_async_copy(grad_in, grad, sem.at[2 * parts])]
    bounds = [VELS * j // parts for j in range(parts + 1)]
    for j in range(parts):
        for yh in range(2):
            rows = pl.ds(bounds[j], bounds[j + 1] - bounds[j])
            stores.append(pltpu.make_async_copy(state.at[rows, yh], out.at[rows, :, yh], sem.at[2 * j + yh]))
    for store in stores:
        store.start()
    for store in stores:
        store.wait()


def on_device(adjoint, velocity, relax, fluid_words, neighbours, inlet_ids, basis):
    n = lax.axis_size("blk")
    inner = 8 if n % 64 == 0 else 4
    outer = n // inner
    f32 = jnp.float32
    shape = (EDGE, 2, LANES)
    any_space = pl.BlockSpec(memory_space=pl.ANY)
    smem = pl.BlockSpec(memory_space=pltpu.SMEM)
    dma = pltpu.SemaphoreType.DMA
    out, grad = pl.pallas_call(
        lambda *refs: body(n, inner, *refs),
        out_shape=(
            pltpu.VMEM((VELS, 2, EDGE, LANES), f32),
            jax.ShapeDtypeStruct((1, MODES), f32),
        ),
        in_specs=[any_space, any_space, any_space, smem, smem, smem, any_space],
        out_specs=(pl.BlockSpec(memory_space=pltpu.VMEM), pl.BlockSpec(memory_space=pltpu.VMEM)),
        scratch_shapes=[
            pltpu.VMEM((VELS, 2, EDGE, LANES), f32),
            pltpu.VMEM((3, 2, EDGE, LANES), f32),
            pltpu.VMEM((2, EDGE, LANES), f32),
            pltpu.VMEM((MODES, NIN, 2 * LANES), f32),
            pltpu.VMEM((2, EDGE, LANES), f32),
            pltpu.VMEM((VELS - 1, 2, EDGE, LANES), f32),
            pltpu.VMEM((3, 2, EDGE, LANES), f32),
            pltpu.VMEM((VELS - 1, 2, EDGE, LANES), f32),
            pltpu.VMEM((MODES, 2, EDGE, LANES), f32),
        ]
        + [pltpu.VMEM((2 * REACH + 1, ROWS, LANES), f32) for _ in range(STEPS)]
        + [
            pltpu.VMEM((inner, LANES), f32),
            pltpu.VMEM((outer, LANES), f32),
            dma((7,)),
            dma((STEPS, 4)),
            dma((STEPS, 4)),
            dma((inner - 1,)),
            dma((inner - 1,)),
            dma((outer - 1,)),
            dma((outer - 1,)),
        ],
        compiler_params=pltpu.CompilerParams(collective_id=0, has_side_effects=True),
        name="adjoint_steps",
    )(
        adjoint.reshape((VELS,) + shape),
        velocity.reshape((3,) + shape),
        relax.reshape(shape),
        fluid_words,
        neighbours,
        inlet_ids,
        basis,
    )
    parts = 4
    out, grad = pl.pallas_call(
        functools.partial(hand_over, parts),
        out_shape=(
            jax.ShapeDtypeStruct((VELS,) + shape, f32),
            jax.ShapeDtypeStruct((1, MODES), f32),
        ),
        in_specs=[pl.BlockSpec(memory_space=pltpu.VMEM), any_space],
        out_specs=(any_space, any_space),
        scratch_shapes=[dma((2 * parts + 1,))],
        name="hand_over",
    )(pltpu.with_memory_space_constraint(out, pltpu.VMEM), grad)
    return (out.reshape(1, VELS, EDGE * EDGE * EDGE), grad.reshape(MODES))


def solution(mesh):
    return jax.shard_map(
        on_device,
        mesh=mesh,
        in_specs=(
            P("blk", None, None),
            P("blk", None, None),
            P("blk", None),
            P("blk", None),
            P("blk", None),
            P(),
            P(),
        ),
        out_specs=(P("blk", None, None), P()),
        check_vma=False,
    )
```

```python
import functools

import jax
import jax.numpy as jnp
import numpy as np
from jax import lax
from jax.experimental import pallas as pl
from jax.experimental.pallas import tpu as pltpu
from jax.sharding import PartitionSpec as P

EDGE = 16
VELS = 19
NEIGHBOURS = 18
REACH = 2
STEPS = 4
LANES = 128
NIN = 16
MODES = 8

C = np.array(
    [
        [0, 0, 0],
        [1, 0, 0],
        [-1, 0, 0],
        [0, 1, 0],
        [0, -1, 0],
        [0, 0, 1],
        [0, 0, -1],
        [1, 1, 0],
        [-1, -1, 0],
        [1, -1, 0],
        [-1, 1, 0],
        [1, 0, 1],
        [-1, 0, -1],
        [1, 0, -1],
        [-1, 0, 1],
        [0, 1, 1],
        [0, -1, -1],
        [0, 1, -1],
        [0, -1, 1],
    ],
    dtype=np.int32,
)
OPP = [0, 2, 1, 4, 3, 6, 5, 8, 7, 10, 9, 12, 11, 14, 13, 16, 15, 18, 17]
DIRECTION = {tuple(int(v) for v in C[k + 1]): k for k in range(NEIGHBOURS)}

FLUID = -1


def members(axis, sign):
    found = [i for i in range(VELS) if C[i][axis] == sign]
    return sorted(found, key=lambda i: int(np.abs(C[i]).sum()), reverse=True)


Z_ROWS, Y_ROWS, AXIS_ROWS, X_ROWS, X_FLUID, YZ_FLUID = 0, 16, 32, 48, 68, 72
SENT, ROWS = 68, 88
SIGNS = (1, -1)
Z_NUMBER = {i: n for n, i in enumerate([i for s in SIGNS for i in members(2, s)[:4]])}
Y_NUMBER = {i: n for n, i in enumerate([i for s in SIGNS for i in members(1, s)[:4]])}
X_NUMBER = {i: n for n, i in enumerate([i for s in SIGNS for i in members(0, s)])}
CUT = 12
OWN = REACH


def sign_index(sign):
    return 0 if sign == 1 else 1


def x_row(item, sign, yh):
    if item == FLUID:
        return X_FLUID + 2 * sign_index(sign) + yh
    return X_ROWS + 2 * X_NUMBER[item] + yh


def lane_roll(value, by):
    by = by % LANES
    return value if by == 0 else pltpu.roll(value, LANES - by, 1)


def row_roll(value, by):
    return pltpu.roll(value, (-by) % EDGE, 0)


class Masks:
    def __init__(self):
        self.lane = lax.broadcasted_iota(jnp.int32, (EDGE, LANES), 1)
        self.row = lax.broadcasted_iota(jnp.int32, (EDGE, LANES), 0)
        self.z = self.lane % EDGE
        self.yl = self.lane // EDGE


def put(block, mask, value):
    return value if block is None else jnp.where(mask, value, block)


def pack_axis(load, items, masks):
    block = None
    for sign in SIGNS:
        yh, start = (0, 0) if sign == 1 else (1, LANES - EDGE)
        plane = load(items[(1, sign)], yh)
        at = 4 * sign_index(sign) * EDGE + 4
        first = lane_roll(plane, start - at)
        second = lane_roll(plane, start + CUT - at - EDGE)
        block = put(block, masks.yl == at // EDGE, first)
        block = put(block, masks.yl == at // EDGE + 1, second)
    for sign in SIGNS:
        start = 0 if sign == 1 else EDGE - 1
        for yh in range(2):
            slot = 2 * sign_index(sign) + yh
            block = put(block, masks.z == slot, lane_roll(load(items[(2, sign)], yh), start - slot))
    return block


def pack(package, a, fluid, masks):
    def load(item, yh):
        return fluid[yh] if item == FLUID else a[item, yh]

    block = None
    for sign in SIGNS:
        start = 0 if sign == 1 else EDGE - 1
        for item in members(2, sign)[:4]:
            for yh in range(2):
                slot = 2 * Z_NUMBER[item] + yh
                block = put(block, masks.z == slot, lane_roll(load(item, yh), start - slot))
    package[pl.ds(Z_ROWS, EDGE), :] = block
    block = None
    for sign in SIGNS:
        yh, start = (0, 0) if sign == 1 else (1, LANES - EDGE)
        for item in members(1, sign)[:4]:
            number = Y_NUMBER[item]
            block = put(block, masks.yl == number, lane_roll(load(item, yh), start - number * EDGE))
    package[pl.ds(Y_ROWS, EDGE), :] = block
    axis = {(1, 1): 3, (1, -1): 4, (2, 1): 5, (2, -1): 6}
    package[pl.ds(AXIS_ROWS, EDGE), :] = pack_axis(load, axis, masks)
    for sign in SIGNS:
        x_at = 0 if sign == 1 else EDGE - 1
        for item in members(0, sign):
            for yh in range(2):
                package[pl.ds(x_row(item, sign, yh), 1), :] = a[item, yh, pl.ds(x_at, 1), :]
        if fluid is not None:
            for yh in range(2):
                package[pl.ds(x_row(FLUID, sign, yh), 1), :] = fluid[yh, pl.ds(x_at, 1), :]
    if fluid is not None:
        package[pl.ds(YZ_FLUID, EDGE), :] = pack_axis(load, {key: FLUID for key in axis}, masks)


def y_plane(ghost, direction, item, sign, at, masks, only=None):
    if item in Y_NUMBER:
        return lane_roll(ghost(direction, Y_ROWS, EDGE), Y_NUMBER[item] * EDGE - at)
    block = ghost(direction, YZ_FLUID if item == FLUID else AXIS_ROWS, EDGE)
    start = 4 * sign_index(sign) * EDGE + 4
    first = lane_roll(block, start - at) if only is None or only < CUT else None
    second = lane_roll(block, start + EDGE - CUT - at) if only is None or only >= CUT else None
    if first is None or second is None:
        return second if first is None else first
    return jnp.where((masks.lane + (LANES - at)) % LANES < CUT, first, second)


def z_plane(ghost, direction, item, sign, yh, target):
    if item in Z_NUMBER:
        return lane_roll(ghost(direction, Z_ROWS, EDGE), 2 * Z_NUMBER[item] + yh - target)
    block = ghost(direction, YZ_FLUID if item == FLUID else AXIS_ROWS, EDGE)
    return lane_roll(block, 2 * sign_index(sign) + yh - target)


def inside(field, c, masks):
    cx, cy, cz = (int(v) for v in c)
    v0, v1 = field
    if cx:
        v0, v1 = row_roll(v0, cx), row_roll(v1, cx)
    if cy == 1:
        take = masks.lane < EDGE
        v0, v1 = jnp.where(take, v1, v0), v1
    elif cy == -1:
        take = masks.lane >= LANES - EDGE
        v0, v1 = v0, jnp.where(take, v0, v1)
    by = cy * EDGE + cz
    return lane_roll(v0, by), lane_roll(v1, by)


def beyond(c, yh, masks):
    cx, cy, cz = (int(v) for v in c)
    out = None
    if cx:
        out = masks.row == (EDGE - 1 if cx == 1 else 0)
    if cy and yh == (1 if cy == 1 else 0):
        last = masks.yl == (LANES // EDGE - 1 if cy == 1 else 0)
        out = last if out is None else out | last
    if cz:
        last = masks.z == (EDGE - 1 if cz == 1 else 0)
        out = last if out is None else out | last
    return out


HALF = 8


def outside(item, c, ghost, masks):
    cx, cy, cz = (int(v) for v in c)
    both = [(yh, half) for yh in range(2) for half in range(2)]

    def part(value, half):
        return value[HALF * half : HALF * (half + 1)]

    if cx:
        x_half = 1 if cx == 1 else 0
        x_last = masks.row[:HALF] == (HALF - 1 if cx == 1 else 0)
        x_line = [ghost((cx, 0, 0), x_row(item, cx, yh), 1) for yh in range(2)]
    if cy:
        y_half = 1 if cy == 1 else 0
        at, final = (0, LANES - EDGE) if cy == 1 else (LANES - EDGE, 0)
        plane = y_plane(ghost, (0, cy, 0), item, cy, final - cz, masks)
    if cz:
        target = EDGE - 1 if cz == 1 else 0
        source = EDGE - 1 - target
        g = [z_plane(ghost, (0, 0, cz), item, cz, yh, target) for yh in range(2)]
    if cx and not cy and not cz:
        return {(yh, x_half): jnp.broadcast_to(x_line[yh], (HALF, LANES)) for yh in range(2)}
    if cy and not cx and not cz:
        return {(y_half, half): part(plane, half) for half in range(2)}
    if cz and not cx and not cy:
        return {(yh, half): part(g[yh], half) for yh, half in both}
    if cx and cy:
        plane = row_roll(plane, cx)
        line = ghost((cx, cy, 0), x_row(item, cx, 1 - y_half), 1)
        lane = masks.lane[:1]
        take = lane < EDGE if cy == 1 else lane >= LANES - EDGE
        corner, other = (1, 0) if cy == 1 else (0, 1)
        row = [None, None]
        row[corner] = lane_roll(jnp.where(take, line, x_line[corner]), cy * EDGE)
        row[other] = lane_roll(jnp.where(take, x_line[corner], x_line[other]), cy * EDGE)
        return {
            (other, x_half): jnp.broadcast_to(row[other], (HALF, LANES)),
            (corner, x_half): jnp.where(x_last, row[corner], part(plane, x_half)),
            (corner, 1 - x_half): part(plane, 1 - x_half),
        }
    if cx and cz:
        found = {}
        for yh in range(2):
            line = lane_roll(ghost((cx, 0, cz), x_row(item, cx, yh), 1), source - target)
            row = jnp.where(masks.z[:1] == target, line, lane_roll(x_line[yh], cz))
            rolled = row_roll(g[yh], cx)
            found[(yh, x_half)] = jnp.where(x_last, row, part(rolled, x_half))
            found[(yh, 1 - x_half)] = part(rolled, 1 - x_half)
        return found
    line = y_plane(ghost, (0, cy, cz), item, cy, at + target - source, masks, source)
    if cy == 1:
        take = masks.lane < EDGE
        g = [jnp.where(take, g[1], g[0]), jnp.where(take, line, g[1])]
    else:
        take = masks.lane >= LANES - EDGE
        g = [jnp.where(take, line, g[0]), jnp.where(take, g[0], g[1])]
    g = [lane_roll(v, cy * EDGE) for v in g]
    g[y_half] = jnp.where(masks.z == target, g[y_half], plane)
    return {(yh, half): part(g[yh], half) for yh, half in both}


def collide(b, u, k, g, e):
    ux, uy, uz = u
    pairs = [(i, i + 1) for i in range(1, VELS, 2)]
    s = {i: b[i] + b[j] for i, j in pairs}
    d = {i: b[i] - b[j] for i, j in pairs}
    p, q, r = s[7] + s[9], s[11] + s[13], s[15] + s[17]
    sx, sy, sz = s[1] + s[1], s[3] + s[3], s[5] + s[5]
    mxx, myy, mzz = sx + (p + q), sy + (p + r), sz + (q + r)
    mxy, mxz, myz = s[7] - s[9], s[11] - s[13], s[15] - s[17]
    m0 = 12.0 * b[0] + (sx + sy + sz) + (p + q + r)
    m1x = (d[1] + d[1]) + (d[7] + d[9]) + (d[11] + d[13])
    m1y = (d[3] + d[3]) + (d[7] - d[9]) + (d[15] + d[17])
    m1z = (d[5] + d[5]) + (d[11] - d[13]) + (d[15] - d[17])
    nx = mxx * ux + mxy * uy + mxz * uz
    ny = mxy * ux + myy * uy + myz * uz
    nz = mxz * ux + myz * uy + mzz * uz
    vx = g * (m1x + 3.0 * nx - ux * m0)
    vy = g * (m1y + 3.0 * ny - uy * m0)
    vz = g * (m1z + 3.0 * nz - uz * m0)
    o = g * (m0 * e - 1.5 * (ux * nx + uy * ny + uz * nz))
    v = {1: vx, 3: vy, 5: vz, 7: vx + vy, 9: vx - vy, 11: vx + vz, 13: vx - vz, 15: vy + vz, 17: vy - vz}
    out = [k * b[0] + o]
    for i, j in pairs:
        out.append(k * b[i] + (o + v[i]))
        out.append(k * b[j] + (o - v[i]))
    return out


AHEAD, BEHIND, SIBLING, CROSS = OWN + 2, OWN - 2, OWN + 1, OWN - 1


def body(n, inner, *refs):
    (a_hbm, vel_hbm, relax_hbm, words_hbm, nbrs_hbm, ids_hbm, basis_hbm) = refs[:7]
    (a, grad) = refs[7:9]
    (b, vel, relax, basis, fluid, bits, coef, ghost_bits, spread, words, nbrs, ids) = refs[9:21]
    bufs = refs[21 : 21 + STEPS]
    (part1, part2, local_sem, send_sem, recv_sem, sums1, sums2) = refs[21 + STEPS :]
    me = lax.axis_index("blk")
    outer = n // inner
    place = me % inner
    group = me // inner
    way = 1 - 2 * (me % 2)
    ahead, behind, sibling, cross = me + 2 * way, me - 2 * way, me + way, me - way
    has_ahead = (ahead >= 0) & (ahead < n)
    has_behind = (behind >= 0) & (behind < n)
    others = [t + (t >= place).astype(jnp.int32) for t in range(inner - 1)]
    groups = [t + (t >= group).astype(jnp.int32) for t in range(outer - 1)]
    inner_peers = [group * inner + p for p in others]
    outer_peers = [g * inner + place for g in groups]

    barrier = pltpu.get_barrier_semaphore()

    def greet(peer):
        pl.semaphore_signal(barrier, inc=1, device_id=(peer,), device_id_type=pl.DeviceIdType.MESH)

    pl.when(has_ahead)(lambda: greet(ahead))
    pl.when(has_behind)(lambda: greet(behind))
    pl.when(has_behind)(lambda: greet(cross))
    greet(sibling)
    greetings = inner + outer - 1 + has_ahead.astype(jnp.int32) + 2 * has_behind.astype(jnp.int32)

    tables = [
        pltpu.make_async_copy(words_hbm, words, local_sem.at[7]),
        pltpu.make_async_copy(nbrs_hbm, nbrs, local_sem.at[8]),
        pltpu.make_async_copy(ids_hbm, ids, local_sem.at[9]),
    ]
    for table in tables:
        table.start()
    loads = []
    for yh in range(2):
        loads.append(pltpu.make_async_copy(a_hbm.at[:, :, yh, :], a.at[:, yh], local_sem.at[yh]))
        loads.append(pltpu.make_async_copy(vel_hbm.at[:, :, yh, :], vel.at[:, yh], local_sem.at[2 + yh]))
        loads.append(pltpu.make_async_copy(relax_hbm.at[:, yh, :], relax.at[yh], local_sem.at[4 + yh]))
    load_basis = pltpu.make_async_copy(basis_hbm, basis, local_sem.at[6])
    load_basis.start()
    for load in loads:
        load.start()

    for peer in inner_peers + outer_peers:
        greet(peer)

    masks = Masks()
    for table in tables:
        table.wait()
    for yh in range(2):
        word = jnp.zeros((EDGE, LANES), jnp.int32)
        for x in range(EDGE):
            at = x * 8 + yh * 4
            w = [words[0, at + j] for j in range(4)]
            line = jnp.where(
                masks.lane < 64,
                jnp.where(masks.lane < 32, w[0], w[1]),
                jnp.where(masks.lane < 96, w[2], w[3]),
            )
            word = jnp.where(masks.row == x, line, word)
        bit = jnp.bitwise_and(jnp.right_shift(word, masks.lane % 32), 1)
        fluid[yh] = bit.astype(jnp.float32)

    is_inlet = jnp.int32(0)
    for r in range(NIN):
        is_inlet = is_inlet + (ids[r] == me).astype(jnp.int32)
    keep = 1.0 - is_inlet.astype(jnp.float32)
    keep_z = jnp.where(masks.z == 0, keep, 1.0)
    slot_of = []
    present = []
    for k in range(NEIGHBOURS):
        entry = nbrs[0, k]
        there = (entry >= 0).astype(jnp.int32)
        slot = jnp.clip(OWN + (entry - me) * way, 0, 2 * REACH)
        slot_of.append(slot * there + OWN * (1 - there))
        present.append(there.astype(jnp.float32))

    def halo(step, index, source, target, peer):
        rows = pl.ds(0, ROWS if step == 0 else SENT)
        return pltpu.make_async_remote_copy(
            src_ref=bufs[step].at[source, rows],
            dst_ref=bufs[step].at[target, rows],
            send_sem=send_sem.at[step, index],
            recv_sem=recv_sem.at[step, index],
            device_id=(peer,),
            device_id_type=pl.DeviceIdType.MESH,
        )

    def start_sums(part, sems, mine, peers, places):
        for peer, p in zip(peers, places):
            row = 1 + mine - (mine > p).astype(jnp.int32)
            pltpu.make_async_remote_copy(
                src_ref=part.at[pl.ds(0, 1)],
                dst_ref=part.at[pl.ds(row, 1)],
                send_sem=sems.at[0],
                recv_sem=sems.at[1],
                device_id=(peer,),
                device_id_type=pl.DeviceIdType.MESH,
            ).start()

    def wait_sums(part, sems, which):
        rows = part.at[pl.ds(1, part.shape[0] - 1)]
        pltpu.make_async_copy(rows, rows, sems.at[which]).wait()

    layer = [jnp.zeros((EDGE, LANES), jnp.float32) for _ in range(2)]
    for load in loads:
        load.wait()
    exchanges = []
    for step in range(STEPS):
        buf = bufs[step]
        for yh in range(2):
            layer[yh] = layer[yh] + (2.0 * a[5, yh] + ((a[11, yh] + a[14, yh]) + (a[15, yh] + a[18, yh])))
        if step == STEPS - 1:
            mode = lax.broadcasted_iota(jnp.int32, (MODES, LANES), 0)
            total = jnp.zeros((MODES, LANES), jnp.float32)
            for m in range(MODES):
                product = spread[m, 0] * layer[0] + spread[m, 1] * layer[1]
                total = jnp.where(mode == m, jnp.sum(product, axis=0, keepdims=True), total)
            total = jnp.sum(total, axis=1, keepdims=True)
            at_mode = lax.broadcasted_iota(jnp.int32, (MODES, LANES), 1) == mode
            part1[pl.ds(0, 1), :] = jnp.sum(jnp.where(at_mode, total, 0.0), axis=0, keepdims=True)
            start_sums(part1, sums1, place, inner_peers, others)
        pack(buf.at[OWN], a, fluid if step == 0 else None, masks)
        if step == 0:
            pl.semaphore_wait(barrier, greetings)
        to_ahead = halo(step, 0, OWN, BEHIND, ahead)
        to_behind = halo(step, 1, OWN, AHEAD, behind)
        to_sibling = halo(step, 2, OWN, SIBLING, sibling)
        to_cross = halo(step, 3, OWN, CROSS, cross)
        exchanges.append((to_ahead, to_behind, to_sibling, to_cross))
        pl.when(has_behind)(to_behind.start)
        pl.when(has_behind)(to_cross.start)
        pl.when(has_ahead)(to_ahead.start)
        to_sibling.start()
        for yh in range(2):
            if step == 0:
                f = fluid[yh]
                squared = vel[0, yh] * vel[0, yh] + vel[1, yh] * vel[1, yh] + vel[2, yh] * vel[2, yh]
                coef[0, yh] = f * (1.0 - relax[yh])
                coef[1, yh] = f * relax[yh] * (1.0 / 12.0)
                coef[2, yh] = (1.0 / 3.0) + 0.5 * squared
        if step == 0:
            load_basis.wait()
            row = lax.broadcasted_iota(jnp.int32, (EDGE, 2 * LANES), 0)
            flat = lax.broadcasted_iota(jnp.int32, (EDGE, 2 * LANES), 1)
            mine = jnp.zeros((EDGE, 2 * LANES), jnp.float32)
            for r in range(NIN):
                mine = jnp.where(row == r, (ids[r] == me).astype(jnp.float32), mine)
            lines = []
            for m in range(MODES):
                line = jnp.sum(basis[m] * mine, axis=0, keepdims=True)
                lines.append(jnp.where(flat // EDGE == row, line, 0.0))
            lines = jnp.concatenate(lines, axis=0)
            q = lax.broadcasted_iota(jnp.int32, (2 * LANES, LANES), 0)
            site = lax.broadcasted_iota(jnp.int32, (2 * LANES, LANES), 1)
            for yh in range(2):
                pick = ((site % EDGE == 0) & (site // EDGE + 8 * yh == q % EDGE)).astype(jnp.float32)
                placed = jnp.dot(lines, pick, precision=lax.Precision.HIGHEST, preferred_element_type=jnp.float32)
                for m in range(MODES):
                    spread[m, yh] = placed[m * EDGE : (m + 1) * EDGE] * (fluid[yh] * (1.0 / 12.0))
        for yh in range(2):
            b[0, yh] = a[0, yh]
        for i in range(1, VELS):
            if step == 0:
                moved = inside((fluid[0], fluid[1]), C[i], masks)
                for yh in range(2):
                    out = beyond(C[i], yh, masks)
                    bits[i - 1, yh] = moved[yh] if out is None else jnp.where(out, 0.0, moved[yh])
            moved = inside((a[i, 0], a[i, 1]), C[i], masks)
            for yh in range(2):
                back = a[OPP[i], yh]
                if C[i][2] == -1:
                    back = back * keep_z
                b[i, yh] = jnp.where(bits[i - 1, yh] > 0.5, moved[yh], back)
        if step == STEPS - 1:
            wait_sums(part1, sums1, 1)
            part2[pl.ds(0, 1), :] = jnp.sum(part1[...], axis=0, keepdims=True)
            start_sums(part2, sums2, group, outer_peers, groups)
        to_sibling.wait_recv()
        pl.when(has_ahead)(to_behind.wait_recv)

        @pl.when(has_behind)
        def _():
            to_ahead.wait_recv()
            to_cross.wait_recv()


        def ghost(direction, row, rows):
            return buf[slot_of[DIRECTION[direction]], pl.ds(row, rows), :]

        if step == 0:

            def ghost_fluid(direction, row, rows):
                k = DIRECTION[direction]
                return buf[slot_of[k], pl.ds(row, rows), :] * present[k]

            for i in range(1, VELS):
                for (yh, half), value in outside(FLUID, C[i], ghost_fluid, masks).items():
                    rows = slice(HALF * half, HALF * (half + 1))
                    value = jnp.where(beyond(C[i], yh, masks)[rows], value, 0.0)
                    if C[i][2] == -1:
                        value = value * keep_z[rows]
                    ghost_bits[i - 1, yh, pl.ds(HALF * half, HALF), :] = value
        for i in range(1, VELS):
            for (yh, half), value in outside(i, C[i], ghost, masks).items():
                rows = pl.ds(HALF * half, HALF)
                b[i, yh, rows, :] = jnp.where(ghost_bits[i - 1, yh, rows, :] > 0.5, value, b[i, yh, rows, :])
        for yh in range(2):
            for half in range(2):
                rows = pl.ds(HALF * half, HALF)
                new = collide(
                    [b[i, yh, rows, :] for i in range(VELS)],
                    [vel[c, yh, rows, :] for c in range(3)],
                    coef[0, yh, rows, :],
                    coef[1, yh, rows, :],
                    coef[2, yh, rows, :],
                )
                for i in range(VELS):
                    a[i, yh, rows, :] = new[i]

    wait_sums(part2, sums2, 1)
    grad[...] = jnp.sum(part2[...], axis=0, keepdims=True)[:, :MODES]
    for to_ahead, to_behind, to_sibling, to_cross in exchanges:
        pl.when(has_ahead)(to_ahead.wait_send)
        pl.when(has_behind)(to_behind.wait_send)
        to_sibling.wait_send()
        pl.when(has_behind)(to_cross.wait_send)
    wait_sums(part1, sums1, 0)
    wait_sums(part2, sums2, 0)


def hand_over(parts, state, grad_in, out, grad, sem):
    stores = [pltpu.make_async_copy(grad_in, grad, sem.at[2 * parts])]
    bounds = [VELS * j // parts for j in range(parts + 1)]
    for j in range(parts):
        for yh in range(2):
            rows = pl.ds(bounds[j], bounds[j + 1] - bounds[j])
            stores.append(pltpu.make_async_copy(state.at[rows, yh], out.at[rows, :, yh], sem.at[2 * j + yh]))
    for store in stores:
        store.start()
    for store in stores:
        store.wait()


def on_device(adjoint, velocity, relax, fluid_words, neighbours, inlet_ids, basis):
    n = lax.axis_size("blk")
    inner = 8 if n % 64 == 0 else 4
    outer = n // inner
    f32 = jnp.float32
    shape = (EDGE, 2, LANES)
    any_space = pl.BlockSpec(memory_space=pl.ANY)
    dma = pltpu.SemaphoreType.DMA
    out, grad = pl.pallas_call(
        lambda *refs: body(n, inner, *refs),
        out_shape=(
            pltpu.VMEM((VELS, 2, EDGE, LANES), f32),
            jax.ShapeDtypeStruct((1, MODES), f32),
        ),
        in_specs=[any_space] * 7,
        out_specs=(pl.BlockSpec(memory_space=pltpu.VMEM), pl.BlockSpec(memory_space=pltpu.VMEM)),
        scratch_shapes=[
            pltpu.VMEM((VELS, 2, EDGE, LANES), f32),
            pltpu.VMEM((3, 2, EDGE, LANES), f32),
            pltpu.VMEM((2, EDGE, LANES), f32),
            pltpu.VMEM((MODES, NIN, 2 * LANES), f32),
            pltpu.VMEM((2, EDGE, LANES), f32),
            pltpu.VMEM((VELS - 1, 2, EDGE, LANES), f32),
            pltpu.VMEM((3, 2, EDGE, LANES), f32),
            pltpu.VMEM((VELS - 1, 2, EDGE, LANES), f32),
            pltpu.VMEM((MODES, 2, EDGE, LANES), f32),
            pltpu.SMEM((1, EDGE * EDGE * EDGE // 32), jnp.int32),
            pltpu.SMEM((1, NEIGHBOURS), jnp.int32),
            pltpu.SMEM((NIN,), jnp.int32),
        ]
        + [pltpu.VMEM((2 * REACH + 1, ROWS, LANES), f32) for _ in range(STEPS)]
        + [
            pltpu.VMEM((inner, LANES), f32),
            pltpu.VMEM((outer, LANES), f32),
            dma((10,)),
            dma((STEPS, 4)),
            dma((STEPS, 4)),
            dma((2,)),
            dma((2,)),
        ],
        compiler_params=pltpu.CompilerParams(collective_id=0, has_side_effects=True),
        name="adjoint_steps",
    )(
        adjoint.reshape((VELS,) + shape),
        velocity.reshape((3,) + shape),
        relax.reshape(shape),
        fluid_words,
        neighbours,
        inlet_ids,
        basis,
    )
    parts = 4
    out, grad = pl.pallas_call(
        functools.partial(hand_over, parts),
        out_shape=(
            jax.ShapeDtypeStruct((VELS,) + shape, f32),
            jax.ShapeDtypeStruct((1, MODES), f32),
        ),
        in_specs=[pl.BlockSpec(memory_space=pltpu.VMEM), any_space],
        out_specs=(any_space, any_space),
        scratch_shapes=[dma((2 * parts + 1,))],
        name="hand_over",
    )(pltpu.with_memory_space_constraint(out, pltpu.VMEM), grad)
    return (out.reshape(1, VELS, EDGE * EDGE * EDGE), grad.reshape(MODES))


def solution(mesh):
    return jax.shard_map(
        on_device,
        mesh=mesh,
        in_specs=(
            P("blk", None, None),
            P("blk", None, None),
            P("blk", None),
            P("blk", None),
            P("blk", None),
            P(),
            P(),
        ),
        out_specs=(P("blk", None, None), P()),
        check_vma=False,
    )
```

```python
import functools

import jax
import jax.numpy as jnp
import numpy as np
from jax import lax
from jax.experimental import pallas as pl
from jax.experimental.pallas import tpu as pltpu
from jax.sharding import PartitionSpec as P

EDGE = 16
VELS = 19
NEIGHBOURS = 18
REACH = 2
STEPS = 4
LANES = 128
NIN = 16
MODES = 8

C = np.array(
    [
        [0, 0, 0],
        [1, 0, 0],
        [-1, 0, 0],
        [0, 1, 0],
        [0, -1, 0],
        [0, 0, 1],
        [0, 0, -1],
        [1, 1, 0],
        [-1, -1, 0],
        [1, -1, 0],
        [-1, 1, 0],
        [1, 0, 1],
        [-1, 0, -1],
        [1, 0, -1],
        [-1, 0, 1],
        [0, 1, 1],
        [0, -1, -1],
        [0, 1, -1],
        [0, -1, 1],
    ],
    dtype=np.int32,
)
OPP = [0, 2, 1, 4, 3, 6, 5, 8, 7, 10, 9, 12, 11, 14, 13, 16, 15, 18, 17]
DIRECTION = {tuple(int(v) for v in C[k + 1]): k for k in range(NEIGHBOURS)}

FLUID = -1


def members(axis, sign):
    found = [i for i in range(VELS) if C[i][axis] == sign]
    return sorted(found, key=lambda i: int(np.abs(C[i]).sum()), reverse=True)


Z_ROWS, Y_ROWS, AXIS_ROWS, X_ROWS, X_FLUID, YZ_FLUID = 0, 16, 32, 48, 68, 72
SENT, ROWS = 68, 88
SIGNS = (1, -1)
Z_NUMBER = {i: n for n, i in enumerate([i for s in SIGNS for i in members(2, s)[:4]])}
Y_NUMBER = {i: n for n, i in enumerate([i for s in SIGNS for i in members(1, s)[:4]])}
X_NUMBER = {i: n for n, i in enumerate([i for s in SIGNS for i in members(0, s)])}
CUT = 12
OWN = REACH


def sign_index(sign):
    return 0 if sign == 1 else 1


def x_row(item, sign, yh):
    if item == FLUID:
        return X_FLUID + 2 * sign_index(sign) + yh
    return X_ROWS + 2 * X_NUMBER[item] + yh


def lane_roll(value, by):
    by = by % LANES
    return value if by == 0 else pltpu.roll(value, LANES - by, 1)


def row_roll(value, by):
    return pltpu.roll(value, (-by) % EDGE, 0)


class Masks:
    def __init__(self):
        self.lane = lax.broadcasted_iota(jnp.int32, (EDGE, LANES), 1)
        self.row = lax.broadcasted_iota(jnp.int32, (EDGE, LANES), 0)
        self.z = self.lane % EDGE
        self.yl = self.lane // EDGE


def put(block, mask, value):
    return value if block is None else jnp.where(mask, value, block)


def pack_axis(load, items, masks):
    block = None
    for sign in SIGNS:
        yh, start = (0, 0) if sign == 1 else (1, LANES - EDGE)
        plane = load(items[(1, sign)], yh)
        at = 4 * sign_index(sign) * EDGE + 4
        first = lane_roll(plane, start - at)
        second = lane_roll(plane, start + CUT - at - EDGE)
        block = put(block, masks.yl == at // EDGE, first)
        block = put(block, masks.yl == at // EDGE + 1, second)
    for sign in SIGNS:
        start = 0 if sign == 1 else EDGE - 1
        for yh in range(2):
            slot = 2 * sign_index(sign) + yh
            block = put(block, masks.z == slot, lane_roll(load(items[(2, sign)], yh), start - slot))
    return block


def pack(package, a, fluid, masks):
    def load(item, yh):
        return fluid[yh] if item == FLUID else a[item, yh]

    block = None
    for sign in SIGNS:
        start = 0 if sign == 1 else EDGE - 1
        for item in members(2, sign)[:4]:
            for yh in range(2):
                slot = 2 * Z_NUMBER[item] + yh
                block = put(block, masks.z == slot, lane_roll(load(item, yh), start - slot))
    package[pl.ds(Z_ROWS, EDGE), :] = block
    block = None
    for sign in SIGNS:
        yh, start = (0, 0) if sign == 1 else (1, LANES - EDGE)
        for item in members(1, sign)[:4]:
            number = Y_NUMBER[item]
            block = put(block, masks.yl == number, lane_roll(load(item, yh), start - number * EDGE))
    package[pl.ds(Y_ROWS, EDGE), :] = block
    axis = {(1, 1): 3, (1, -1): 4, (2, 1): 5, (2, -1): 6}
    package[pl.ds(AXIS_ROWS, EDGE), :] = pack_axis(load, axis, masks)
    for sign in SIGNS:
        x_at = 0 if sign == 1 else EDGE - 1
        for item in members(0, sign):
            for yh in range(2):
                package[pl.ds(x_row(item, sign, yh), 1), :] = a[item, yh, pl.ds(x_at, 1), :]
        if fluid is not None:
            for yh in range(2):
                package[pl.ds(x_row(FLUID, sign, yh), 1), :] = fluid[yh, pl.ds(x_at, 1), :]
    if fluid is not None:
        package[pl.ds(YZ_FLUID, EDGE), :] = pack_axis(load, {key: FLUID for key in axis}, masks)


def y_plane(ghost, direction, item, sign, at, masks, only=None):
    if item in Y_NUMBER:
        return lane_roll(ghost(direction, Y_ROWS, EDGE), Y_NUMBER[item] * EDGE - at)
    block = ghost(direction, YZ_FLUID if item == FLUID else AXIS_ROWS, EDGE)
    start = 4 * sign_index(sign) * EDGE + 4
    first = lane_roll(block, start - at) if only is None or only < CUT else None
    second = lane_roll(block, start + EDGE - CUT - at) if only is None or only >= CUT else None
    if first is None or second is None:
        return second if first is None else first
    return jnp.where((masks.lane + (LANES - at)) % LANES < CUT, first, second)


def z_plane(ghost, direction, item, sign, yh, target):
    if item in Z_NUMBER:
        return lane_roll(ghost(direction, Z_ROWS, EDGE), 2 * Z_NUMBER[item] + yh - target)
    block = ghost(direction, YZ_FLUID if item == FLUID else AXIS_ROWS, EDGE)
    return lane_roll(block, 2 * sign_index(sign) + yh - target)


def inside(field, c, masks):
    cx, cy, cz = (int(v) for v in c)
    v0, v1 = field
    if cx:
        v0, v1 = row_roll(v0, cx), row_roll(v1, cx)
    if cy == 1:
        take = masks.lane < EDGE
        v0, v1 = jnp.where(take, v1, v0), v1
    elif cy == -1:
        take = masks.lane >= LANES - EDGE
        v0, v1 = v0, jnp.where(take, v0, v1)
    by = cy * EDGE + cz
    return lane_roll(v0, by), lane_roll(v1, by)


def beyond(c, yh, masks):
    cx, cy, cz = (int(v) for v in c)
    out = None
    if cx:
        out = masks.row == (EDGE - 1 if cx == 1 else 0)
    if cy and yh == (1 if cy == 1 else 0):
        last = masks.yl == (LANES // EDGE - 1 if cy == 1 else 0)
        out = last if out is None else out | last
    if cz:
        last = masks.z == (EDGE - 1 if cz == 1 else 0)
        out = last if out is None else out | last
    return out


HALF = 8


def outside(item, c, ghost, masks):
    cx, cy, cz = (int(v) for v in c)
    both = [(yh, half) for yh in range(2) for half in range(2)]

    def part(value, half):
        return value[HALF * half : HALF * (half + 1)]

    if cx:
        x_half = 1 if cx == 1 else 0
        x_last = masks.row[:HALF] == (HALF - 1 if cx == 1 else 0)
        x_line = [ghost((cx, 0, 0), x_row(item, cx, yh), 1) for yh in range(2)]
    if cy:
        y_half = 1 if cy == 1 else 0
        at, final = (0, LANES - EDGE) if cy == 1 else (LANES - EDGE, 0)
        plane = y_plane(ghost, (0, cy, 0), item, cy, final - cz, masks)
    if cz:
        target = EDGE - 1 if cz == 1 else 0
        source = EDGE - 1 - target
        g = [z_plane(ghost, (0, 0, cz), item, cz, yh, target) for yh in range(2)]
    if cx and not cy and not cz:
        return {(yh, x_half): jnp.broadcast_to(x_line[yh], (HALF, LANES)) for yh in range(2)}
    if cy and not cx and not cz:
        return {(y_half, half): part(plane, half) for half in range(2)}
    if cz and not cx and not cy:
        return {(yh, half): part(g[yh], half) for yh, half in both}
    if cx and cy:
        plane = row_roll(plane, cx)
        line = ghost((cx, cy, 0), x_row(item, cx, 1 - y_half), 1)
        lane = masks.lane[:1]
        take = lane < EDGE if cy == 1 else lane >= LANES - EDGE
        corner, other = (1, 0) if cy == 1 else (0, 1)
        row = [None, None]
        row[corner] = lane_roll(jnp.where(take, line, x_line[corner]), cy * EDGE)
        row[other] = lane_roll(jnp.where(take, x_line[corner], x_line[other]), cy * EDGE)
        return {
            (other, x_half): jnp.broadcast_to(row[other], (HALF, LANES)),
            (corner, x_half): jnp.where(x_last, row[corner], part(plane, x_half)),
            (corner, 1 - x_half): part(plane, 1 - x_half),
        }
    if cx and cz:
        found = {}
        for yh in range(2):
            line = lane_roll(ghost((cx, 0, cz), x_row(item, cx, yh), 1), source - target)
            row = jnp.where(masks.z[:1] == target, line, lane_roll(x_line[yh], cz))
            rolled = row_roll(g[yh], cx)
            found[(yh, x_half)] = jnp.where(x_last, row, part(rolled, x_half))
            found[(yh, 1 - x_half)] = part(rolled, 1 - x_half)
        return found
    line = y_plane(ghost, (0, cy, cz), item, cy, at + target - source, masks, source)
    if cy == 1:
        take = masks.lane < EDGE
        g = [jnp.where(take, g[1], g[0]), jnp.where(take, line, g[1])]
    else:
        take = masks.lane >= LANES - EDGE
        g = [jnp.where(take, line, g[0]), jnp.where(take, g[0], g[1])]
    g = [lane_roll(v, cy * EDGE) for v in g]
    g[y_half] = jnp.where(masks.z == target, g[y_half], plane)
    return {(yh, half): part(g[yh], half) for yh, half in both}


def collide(b, u, k, g, e):
    ux, uy, uz = u
    pairs = [(i, i + 1) for i in range(1, VELS, 2)]
    s = {i: b[i] + b[j] for i, j in pairs}
    d = {i: b[i] - b[j] for i, j in pairs}
    p, q, r = s[7] + s[9], s[11] + s[13], s[15] + s[17]
    sx, sy, sz = s[1] + s[1], s[3] + s[3], s[5] + s[5]
    mxx, myy, mzz = sx + (p + q), sy + (p + r), sz + (q + r)
    mxy, mxz, myz = s[7] - s[9], s[11] - s[13], s[15] - s[17]
    m0 = 12.0 * b[0] + (sx + sy + sz) + (p + q + r)
    m1x = (d[1] + d[1]) + (d[7] + d[9]) + (d[11] + d[13])
    m1y = (d[3] + d[3]) + (d[7] - d[9]) + (d[15] + d[17])
    m1z = (d[5] + d[5]) + (d[11] - d[13]) + (d[15] - d[17])
    nx = mxx * ux + mxy * uy + mxz * uz
    ny = mxy * ux + myy * uy + myz * uz
    nz = mxz * ux + myz * uy + mzz * uz
    vx = g * (m1x + 3.0 * nx - ux * m0)
    vy = g * (m1y + 3.0 * ny - uy * m0)
    vz = g * (m1z + 3.0 * nz - uz * m0)
    o = g * (m0 * e - 1.5 * (ux * nx + uy * ny + uz * nz))
    v = {1: vx, 3: vy, 5: vz, 7: vx + vy, 9: vx - vy, 11: vx + vz, 13: vx - vz, 15: vy + vz, 17: vy - vz}
    out = [k * b[0] + o]
    for i, j in pairs:
        out.append(k * b[i] + (o + v[i]))
        out.append(k * b[j] + (o - v[i]))
    return out


AHEAD, BEHIND, SIBLING, CROSS = OWN + 2, OWN - 2, OWN + 1, OWN - 1


def body(n, inner, *refs):
    (a_hbm, vel_hbm, relax_hbm, words_hbm, nbrs_hbm, ids_hbm, basis_hbm) = refs[:7]
    (a, grad) = refs[7:9]
    (b, vel, relax, basis, fluid, bits, coef, ghost_bits, spread, words, nbrs, ids) = refs[9:21]
    bufs = refs[21 : 21 + STEPS]
    (part1, part2, local_sem, send_sem, recv_sem, sums1, sums2) = refs[21 + STEPS :]
    me = lax.axis_index("blk")
    outer = n // inner
    place = me % inner
    group = me // inner
    way = 1 - 2 * (me % 2)
    ahead, behind, sibling, cross = me + 2 * way, me - 2 * way, me + way, me - way
    has_ahead = (ahead >= 0) & (ahead < n)
    has_behind = (behind >= 0) & (behind < n)
    others = [t + (t >= place).astype(jnp.int32) for t in range(inner - 1)]
    groups = [t + (t >= group).astype(jnp.int32) for t in range(outer - 1)]
    inner_peers = [group * inner + p for p in others]
    outer_peers = [g * inner + place for g in groups]

    barrier = pltpu.get_barrier_semaphore()

    def greet(peer):
        pl.semaphore_signal(barrier, inc=1, device_id=(peer,), device_id_type=pl.DeviceIdType.MESH)

    pl.when(has_ahead)(lambda: greet(ahead))
    pl.when(has_behind)(lambda: greet(behind))
    pl.when(has_behind)(lambda: greet(cross))
    greet(sibling)
    greetings = inner + outer - 1 + has_ahead.astype(jnp.int32) + 2 * has_behind.astype(jnp.int32)

    tables = [
        pltpu.make_async_copy(words_hbm, words, local_sem.at[7]),
        pltpu.make_async_copy(nbrs_hbm, nbrs, local_sem.at[8]),
        pltpu.make_async_copy(ids_hbm, ids, local_sem.at[9]),
    ]
    for table in tables:
        table.start()
    loads = []
    for yh in range(2):
        loads.append(pltpu.make_async_copy(a_hbm.at[:, :, yh, :], a.at[:, yh], local_sem.at[yh]))
        loads.append(pltpu.make_async_copy(vel_hbm.at[:, :, yh, :], vel.at[:, yh], local_sem.at[2 + yh]))
        loads.append(pltpu.make_async_copy(relax_hbm.at[:, yh, :], relax.at[yh], local_sem.at[4 + yh]))
    load_basis = pltpu.make_async_copy(basis_hbm, basis, local_sem.at[6])
    load_basis.start()
    for load in loads:
        load.start()

    for peer in inner_peers + outer_peers:
        greet(peer)

    masks = Masks()
    for table in tables:
        table.wait()
    for yh in range(2):
        word = jnp.zeros((EDGE, LANES), jnp.int32)
        for x in range(EDGE):
            at = x * 8 + yh * 4
            w = [words[0, at + j] for j in range(4)]
            line = jnp.where(
                masks.lane < 64,
                jnp.where(masks.lane < 32, w[0], w[1]),
                jnp.where(masks.lane < 96, w[2], w[3]),
            )
            word = jnp.where(masks.row == x, line, word)
        bit = jnp.bitwise_and(jnp.right_shift(word, masks.lane % 32), 1)
        fluid[yh] = bit.astype(jnp.float32)

    is_inlet = jnp.int32(0)
    for r in range(NIN):
        is_inlet = is_inlet + (ids[r] == me).astype(jnp.int32)
    keep = 1.0 - is_inlet.astype(jnp.float32)
    keep_z = jnp.where(masks.z == 0, keep, 1.0)
    slot_of = []
    present = []
    for k in range(NEIGHBOURS):
        entry = nbrs[0, k]
        there = (entry >= 0).astype(jnp.int32)
        slot = jnp.clip(OWN + (entry - me) * way, 0, 2 * REACH)
        slot_of.append(slot * there + OWN * (1 - there))
        present.append(there.astype(jnp.float32))

    def halo(step, index, source, target, peer):
        rows = pl.ds(0, ROWS if step == 0 else SENT)
        return pltpu.make_async_remote_copy(
            src_ref=bufs[step].at[source, rows],
            dst_ref=bufs[step].at[target, rows],
            send_sem=send_sem.at[step, index],
            recv_sem=recv_sem.at[step, index],
            device_id=(peer,),
            device_id_type=pl.DeviceIdType.MESH,
        )

    def start_sums(part, sems, mine, peers, places):
        for peer, p in zip(peers, places):
            row = 1 + mine - (mine > p).astype(jnp.int32)
            pltpu.make_async_remote_copy(
                src_ref=part.at[pl.ds(0, 1)],
                dst_ref=part.at[pl.ds(row, 1)],
                send_sem=sems.at[0],
                recv_sem=sems.at[1],
                device_id=(peer,),
                device_id_type=pl.DeviceIdType.MESH,
            ).start()

    def wait_sums(part, sems, which):
        rows = part.at[pl.ds(1, part.shape[0] - 1)]
        pltpu.make_async_copy(rows, rows, sems.at[which]).wait()

    layer = [jnp.zeros((EDGE, LANES), jnp.float32) for _ in range(2)]
    for load in loads:
        load.wait()
    exchanges = []
    for step in range(STEPS):
        buf = bufs[step]
        for yh in range(2):
            layer[yh] = layer[yh] + (2.0 * a[5, yh] + ((a[11, yh] + a[14, yh]) + (a[15, yh] + a[18, yh])))
        if step == STEPS - 1:
            mode = lax.broadcasted_iota(jnp.int32, (MODES, LANES), 0)
            total = jnp.zeros((MODES, LANES), jnp.float32)
            for m in range(MODES):
                product = spread[m, 0] * layer[0] + spread[m, 1] * layer[1]
                total = jnp.where(mode == m, jnp.sum(product, axis=0, keepdims=True), total)
            total = jnp.sum(total, axis=1, keepdims=True)
            at_mode = lax.broadcasted_iota(jnp.int32, (MODES, LANES), 1) == mode
            part1[pl.ds(0, 1), :] = jnp.sum(jnp.where(at_mode, total, 0.0), axis=0, keepdims=True)
            start_sums(part1, sums1, place, inner_peers, others)
        pack(buf.at[OWN], a, fluid if step == 0 else None, masks)
        if step == 0:
            pl.semaphore_wait(barrier, greetings)
        to_ahead = halo(step, 0, OWN, BEHIND, ahead)
        to_behind = halo(step, 1, OWN, AHEAD, behind)
        to_sibling = halo(step, 2, OWN, SIBLING, sibling)
        to_cross = halo(step, 3, OWN, CROSS, cross)
        exchanges.append((to_ahead, to_behind, to_sibling, to_cross))
        pl.when(has_ahead)(to_ahead.start)
        pl.when(has_behind)(to_behind.start)
        pl.when(has_behind)(to_cross.start)
        to_sibling.start()
        for yh in range(2):
            if step == 0:
                f = fluid[yh]
                squared = vel[0, yh] * vel[0, yh] + vel[1, yh] * vel[1, yh] + vel[2, yh] * vel[2, yh]
                coef[0, yh] = f * (1.0 - relax[yh])
                coef[1, yh] = f * relax[yh] * (1.0 / 12.0)
                coef[2, yh] = (1.0 / 3.0) + 0.5 * squared
        if step == 0:
            load_basis.wait()
            row = lax.broadcasted_iota(jnp.int32, (EDGE, 2 * LANES), 0)
            flat = lax.broadcasted_iota(jnp.int32, (EDGE, 2 * LANES), 1)
            mine = jnp.zeros((EDGE, 2 * LANES), jnp.float32)
            for r in range(NIN):
                mine = jnp.where(row == r, (ids[r] == me).astype(jnp.float32), mine)
            lines = []
            for m in range(MODES):
                line = jnp.sum(basis[m] * mine, axis=0, keepdims=True)
                lines.append(jnp.where(flat // EDGE == row, line, 0.0))
            lines = jnp.concatenate(lines, axis=0)
            q = lax.broadcasted_iota(jnp.int32, (2 * LANES, LANES), 0)
            site = lax.broadcasted_iota(jnp.int32, (2 * LANES, LANES), 1)
            for yh in range(2):
                pick = ((site % EDGE == 0) & (site // EDGE + 8 * yh == q % EDGE)).astype(jnp.float32)
                placed = jnp.dot(lines, pick, precision=lax.Precision.HIGHEST, preferred_element_type=jnp.float32)
                for m in range(MODES):
                    spread[m, yh] = placed[m * EDGE : (m + 1) * EDGE] * (fluid[yh] * (1.0 / 12.0))
        for yh in range(2):
            b[0, yh] = a[0, yh]
        for i in range(1, VELS):
            if step == 0:
                moved = inside((fluid[0], fluid[1]), C[i], masks)
                for yh in range(2):
                    out = beyond(C[i], yh, masks)
                    bits[i - 1, yh] = moved[yh] if out is None else jnp.where(out, 0.0, moved[yh])
            moved = inside((a[i, 0], a[i, 1]), C[i], masks)
            for yh in range(2):
                back = a[OPP[i], yh]
                if C[i][2] == -1:
                    back = back * keep_z
                b[i, yh] = jnp.where(bits[i - 1, yh] > 0.5, moved[yh], back)
        if step == STEPS - 1:
            wait_sums(part1, sums1, 1)
            part2[pl.ds(0, 1), :] = jnp.sum(part1[...], axis=0, keepdims=True)
            start_sums(part2, sums2, group, outer_peers, groups)
        to_sibling.wait_recv()
        pl.when(has_ahead)(to_behind.wait_recv)

        @pl.when(has_behind)
        def _():
            to_ahead.wait_recv()
            to_cross.wait_recv()


        def ghost(direction, row, rows):
            return buf[slot_of[DIRECTION[direction]], pl.ds(row, rows), :]

        if step == 0:

            def ghost_fluid(direction, row, rows):
                k = DIRECTION[direction]
                return buf[slot_of[k], pl.ds(row, rows), :] * present[k]

            for i in range(1, VELS):
                for (yh, half), value in outside(FLUID, C[i], ghost_fluid, masks).items():
                    rows = slice(HALF * half, HALF * (half + 1))
                    value = jnp.where(beyond(C[i], yh, masks)[rows], value, 0.0)
                    if C[i][2] == -1:
                        value = value * keep_z[rows]
                    ghost_bits[i - 1, yh, pl.ds(HALF * half, HALF), :] = value
        for i in range(1, VELS):
            for (yh, half), value in outside(i, C[i], ghost, masks).items():
                rows = pl.ds(HALF * half, HALF)
                b[i, yh, rows, :] = jnp.where(ghost_bits[i - 1, yh, rows, :] > 0.5, value, b[i, yh, rows, :])
        for yh in range(2):
            for half in range(2):
                rows = pl.ds(HALF * half, HALF)
                new = collide(
                    [b[i, yh, rows, :] for i in range(VELS)],
                    [vel[c, yh, rows, :] for c in range(3)],
                    coef[0, yh, rows, :],
                    coef[1, yh, rows, :],
                    coef[2, yh, rows, :],
                )
                for i in range(VELS):
                    a[i, yh, rows, :] = new[i]

    wait_sums(part2, sums2, 1)
    grad[...] = jnp.sum(part2[...], axis=0, keepdims=True)[:, :MODES]
    for to_ahead, to_behind, to_sibling, to_cross in exchanges:
        pl.when(has_ahead)(to_ahead.wait_send)
        pl.when(has_behind)(to_behind.wait_send)
        to_sibling.wait_send()
        pl.when(has_behind)(to_cross.wait_send)
    wait_sums(part1, sums1, 0)
    wait_sums(part2, sums2, 0)


def hand_over(parts, state, grad_in, out, grad, sem):
    stores = [pltpu.make_async_copy(grad_in, grad, sem.at[2 * parts])]
    bounds = [VELS * j // parts for j in range(parts + 1)]
    for j in range(parts):
        for yh in range(2):
            rows = pl.ds(bounds[j], bounds[j + 1] - bounds[j])
            stores.append(pltpu.make_async_copy(state.at[rows, yh], out.at[rows, :, yh], sem.at[2 * j + yh]))
    for store in stores:
        store.start()
    for store in stores:
        store.wait()


def on_device(adjoint, velocity, relax, fluid_words, neighbours, inlet_ids, basis):
    n = lax.axis_size("blk")
    inner = 8 if n % 64 == 0 else 4
    outer = n // inner
    f32 = jnp.float32
    shape = (EDGE, 2, LANES)
    any_space = pl.BlockSpec(memory_space=pl.ANY)
    dma = pltpu.SemaphoreType.DMA
    out, grad = pl.pallas_call(
        lambda *refs: body(n, inner, *refs),
        out_shape=(
            pltpu.VMEM((VELS, 2, EDGE, LANES), f32),
            pltpu.VMEM((1, MODES), f32),
        ),
        in_specs=[any_space] * 7,
        out_specs=(pl.BlockSpec(memory_space=pltpu.VMEM), pl.BlockSpec(memory_space=pltpu.VMEM)),
        scratch_shapes=[
            pltpu.VMEM((VELS, 2, EDGE, LANES), f32),
            pltpu.VMEM((3, 2, EDGE, LANES), f32),
            pltpu.VMEM((2, EDGE, LANES), f32),
            pltpu.VMEM((MODES, NIN, 2 * LANES), f32),
            pltpu.VMEM((2, EDGE, LANES), f32),
            pltpu.VMEM((VELS - 1, 2, EDGE, LANES), f32),
            pltpu.VMEM((3, 2, EDGE, LANES), f32),
            pltpu.VMEM((VELS - 1, 2, EDGE, LANES), f32),
            pltpu.VMEM((MODES, 2, EDGE, LANES), f32),
            pltpu.SMEM((1, EDGE * EDGE * EDGE // 32), jnp.int32),
            pltpu.SMEM((1, NEIGHBOURS), jnp.int32),
            pltpu.SMEM((NIN,), jnp.int32),
        ]
        + [pltpu.VMEM((2 * REACH + 1, ROWS, LANES), f32) for _ in range(STEPS)]
        + [
            pltpu.VMEM((inner, LANES), f32),
            pltpu.VMEM((outer, LANES), f32),
            dma((10,)),
            dma((STEPS, 4)),
            dma((STEPS, 4)),
            dma((2,)),
            dma((2,)),
        ],
        compiler_params=pltpu.CompilerParams(collective_id=0, has_side_effects=True),
        name="adjoint_steps",
    )(
        adjoint.reshape((VELS,) + shape),
        velocity.reshape((3,) + shape),
        relax.reshape(shape),
        fluid_words,
        neighbours,
        inlet_ids,
        basis,
    )
    parts = 1
    out, grad = pl.pallas_call(
        functools.partial(hand_over, parts),
        out_shape=(
            jax.ShapeDtypeStruct((VELS,) + shape, f32),
            jax.ShapeDtypeStruct((1, MODES), f32),
        ),
        in_specs=[pl.BlockSpec(memory_space=pltpu.VMEM)] * 2,
        out_specs=(any_space, any_space),
        scratch_shapes=[dma((2 * parts + 1,))],
        name="hand_over",
    )(pltpu.with_memory_space_constraint(out, pltpu.VMEM), pltpu.with_memory_space_constraint(grad, pltpu.VMEM))
    return (out.reshape(1, VELS, EDGE * EDGE * EDGE), grad.reshape(MODES))


def solution(mesh):
    return jax.shard_map(
        on_device,
        mesh=mesh,
        in_specs=(
            P("blk", None, None),
            P("blk", None, None),
            P("blk", None),
            P("blk", None),
            P("blk", None),
            P(),
            P(),
        ),
        out_specs=(P("blk", None, None), P()),
        check_vma=False,
    )
```

```python
import functools

import jax
import jax.numpy as jnp
import numpy as np
from jax import lax
from jax.experimental import pallas as pl
from jax.experimental.pallas import tpu as pltpu
from jax.sharding import PartitionSpec as P

EDGE = 16
VELS = 19
NEIGHBOURS = 18
REACH = 2
STEPS = 4
LANES = 128
NIN = 16
MODES = 8

C = np.array(
    [
        [0, 0, 0],
        [1, 0, 0],
        [-1, 0, 0],
        [0, 1, 0],
        [0, -1, 0],
        [0, 0, 1],
        [0, 0, -1],
        [1, 1, 0],
        [-1, -1, 0],
        [1, -1, 0],
        [-1, 1, 0],
        [1, 0, 1],
        [-1, 0, -1],
        [1, 0, -1],
        [-1, 0, 1],
        [0, 1, 1],
        [0, -1, -1],
        [0, 1, -1],
        [0, -1, 1],
    ],
    dtype=np.int32,
)
OPP = [0, 2, 1, 4, 3, 6, 5, 8, 7, 10, 9, 12, 11, 14, 13, 16, 15, 18, 17]
DIRECTION = {tuple(int(v) for v in C[k + 1]): k for k in range(NEIGHBOURS)}

FLUID = -1


def members(axis, sign):
    found = [i for i in range(VELS) if C[i][axis] == sign]
    return sorted(found, key=lambda i: int(np.abs(C[i]).sum()), reverse=True)


Z_ROWS, Y_ROWS, AXIS_ROWS, X_ROWS, X_FLUID, YZ_FLUID = 0, 16, 32, 48, 68, 72
SENT, ROWS = 68, 88
SIGNS = (1, -1)
Z_NUMBER = {i: n for n, i in enumerate([i for s in SIGNS for i in members(2, s)[:4]])}
Y_NUMBER = {i: n for n, i in enumerate([i for s in SIGNS for i in members(1, s)[:4]])}
X_NUMBER = {i: n for n, i in enumerate([i for s in SIGNS for i in members(0, s)])}
CUT = 12
OWN = REACH


def sign_index(sign):
    return 0 if sign == 1 else 1


def x_row(item, sign, yh):
    if item == FLUID:
        return X_FLUID + 2 * sign_index(sign) + yh
    return X_ROWS + 2 * X_NUMBER[item] + yh


def lane_roll(value, by):
    by = by % LANES
    return value if by == 0 else pltpu.roll(value, LANES - by, 1)


def row_roll(value, by):
    return pltpu.roll(value, (-by) % EDGE, 0)


class Masks:
    def __init__(self):
        self.lane = lax.broadcasted_iota(jnp.int32, (EDGE, LANES), 1)
        self.row = lax.broadcasted_iota(jnp.int32, (EDGE, LANES), 0)
        self.z = self.lane % EDGE
        self.yl = self.lane // EDGE


def put(block, mask, value):
    return value if block is None else jnp.where(mask, value, block)


def pack_axis(load, items, masks):
    block = None
    for sign in SIGNS:
        yh, start = (0, 0) if sign == 1 else (1, LANES - EDGE)
        plane = load(items[(1, sign)], yh)
        at = 4 * sign_index(sign) * EDGE + 4
        first = lane_roll(plane, start - at)
        second = lane_roll(plane, start + CUT - at - EDGE)
        block = put(block, masks.yl == at // EDGE, first)
        block = put(block, masks.yl == at // EDGE + 1, second)
    for sign in SIGNS:
        start = 0 if sign == 1 else EDGE - 1
        for yh in range(2):
            slot = 2 * sign_index(sign) + yh
            block = put(block, masks.z == slot, lane_roll(load(items[(2, sign)], yh), start - slot))
    return block


def pack(package, a, fluid, masks):
    def load(item, yh):
        return fluid[yh] if item == FLUID else a[item, yh]

    block = None
    for sign in SIGNS:
        start = 0 if sign == 1 else EDGE - 1
        for item in members(2, sign)[:4]:
            for yh in range(2):
                slot = 2 * Z_NUMBER[item] + yh
                block = put(block, masks.z == slot, lane_roll(load(item, yh), start - slot))
    package[pl.ds(Z_ROWS, EDGE), :] = block
    block = None
    for sign in SIGNS:
        yh, start = (0, 0) if sign == 1 else (1, LANES - EDGE)
        for item in members(1, sign)[:4]:
            number = Y_NUMBER[item]
            block = put(block, masks.yl == number, lane_roll(load(item, yh), start - number * EDGE))
    package[pl.ds(Y_ROWS, EDGE), :] = block
    axis = {(1, 1): 3, (1, -1): 4, (2, 1): 5, (2, -1): 6}
    package[pl.ds(AXIS_ROWS, EDGE), :] = pack_axis(load, axis, masks)
    for sign in SIGNS:
        x_at = 0 if sign == 1 else EDGE - 1
        for item in members(0, sign):
            for yh in range(2):
                package[pl.ds(x_row(item, sign, yh), 1), :] = a[item, yh, pl.ds(x_at, 1), :]
        if fluid is not None:
            for yh in range(2):
                package[pl.ds(x_row(FLUID, sign, yh), 1), :] = fluid[yh, pl.ds(x_at, 1), :]
    if fluid is not None:
        package[pl.ds(YZ_FLUID, EDGE), :] = pack_axis(load, {key: FLUID for key in axis}, masks)


def y_plane(ghost, direction, item, sign, at, masks, only=None):
    if item in Y_NUMBER:
        return lane_roll(ghost(direction, Y_ROWS, EDGE), Y_NUMBER[item] * EDGE - at)
    block = ghost(direction, YZ_FLUID if item == FLUID else AXIS_ROWS, EDGE)
    start = 4 * sign_index(sign) * EDGE + 4
    first = lane_roll(block, start - at) if only is None or only < CUT else None
    second = lane_roll(block, start + EDGE - CUT - at) if only is None or only >= CUT else None
    if first is None or second is None:
        return second if first is None else first
    return jnp.where((masks.lane + (LANES - at)) % LANES < CUT, first, second)


def z_plane(ghost, direction, item, sign, yh, target):
    if item in Z_NUMBER:
        return lane_roll(ghost(direction, Z_ROWS, EDGE), 2 * Z_NUMBER[item] + yh - target)
    block = ghost(direction, YZ_FLUID if item == FLUID else AXIS_ROWS, EDGE)
    return lane_roll(block, 2 * sign_index(sign) + yh - target)


def inside(field, c, masks):
    cx, cy, cz = (int(v) for v in c)
    v0, v1 = field
    if cx:
        v0, v1 = row_roll(v0, cx), row_roll(v1, cx)
    if cy == 1:
        take = masks.lane < EDGE
        v0, v1 = jnp.where(take, v1, v0), v1
    elif cy == -1:
        take = masks.lane >= LANES - EDGE
        v0, v1 = v0, jnp.where(take, v0, v1)
    by = cy * EDGE + cz
    return lane_roll(v0, by), lane_roll(v1, by)


def beyond(c, yh, masks):
    cx, cy, cz = (int(v) for v in c)
    out = None
    if cx:
        out = masks.row == (EDGE - 1 if cx == 1 else 0)
    if cy and yh == (1 if cy == 1 else 0):
        last = masks.yl == (LANES // EDGE - 1 if cy == 1 else 0)
        out = last if out is None else out | last
    if cz:
        last = masks.z == (EDGE - 1 if cz == 1 else 0)
        out = last if out is None else out | last
    return out


HALF = 8


def outside(item, c, ghost, masks):
    cx, cy, cz = (int(v) for v in c)
    both = [(yh, half) for yh in range(2) for half in range(2)]

    def part(value, half):
        return value[HALF * half : HALF * (half + 1)]

    if cx:
        x_half = 1 if cx == 1 else 0
        x_last = masks.row[:HALF] == (HALF - 1 if cx == 1 else 0)
        x_line = [ghost((cx, 0, 0), x_row(item, cx, yh), 1) for yh in range(2)]
    if cy:
        y_half = 1 if cy == 1 else 0
        at, final = (0, LANES - EDGE) if cy == 1 else (LANES - EDGE, 0)
        plane = y_plane(ghost, (0, cy, 0), item, cy, final - cz, masks)
    if cz:
        target = EDGE - 1 if cz == 1 else 0
        source = EDGE - 1 - target
        g = [z_plane(ghost, (0, 0, cz), item, cz, yh, target) for yh in range(2)]
    if cx and not cy and not cz:
        return {(yh, x_half): jnp.broadcast_to(x_line[yh], (HALF, LANES)) for yh in range(2)}
    if cy and not cx and not cz:
        return {(y_half, half): part(plane, half) for half in range(2)}
    if cz and not cx and not cy:
        return {(yh, half): part(g[yh], half) for yh, half in both}
    if cx and cy:
        plane = row_roll(plane, cx)
        line = ghost((cx, cy, 0), x_row(item, cx, 1 - y_half), 1)
        lane = masks.lane[:1]
        take = lane < EDGE if cy == 1 else lane >= LANES - EDGE
        corner, other = (1, 0) if cy == 1 else (0, 1)
        row = [None, None]
        row[corner] = lane_roll(jnp.where(take, line, x_line[corner]), cy * EDGE)
        row[other] = lane_roll(jnp.where(take, x_line[corner], x_line[other]), cy * EDGE)
        return {
            (other, x_half): jnp.broadcast_to(row[other], (HALF, LANES)),
            (corner, x_half): jnp.where(x_last, row[corner], part(plane, x_half)),
            (corner, 1 - x_half): part(plane, 1 - x_half),
        }
    if cx and cz:
        found = {}
        for yh in range(2):
            line = lane_roll(ghost((cx, 0, cz), x_row(item, cx, yh), 1), source - target)
            row = jnp.where(masks.z[:1] == target, line, lane_roll(x_line[yh], cz))
            rolled = row_roll(g[yh], cx)
            found[(yh, x_half)] = jnp.where(x_last, row, part(rolled, x_half))
            found[(yh, 1 - x_half)] = part(rolled, 1 - x_half)
        return found
    line = y_plane(ghost, (0, cy, cz), item, cy, at + target - source, masks, source)
    if cy == 1:
        take = masks.lane < EDGE
        g = [jnp.where(take, g[1], g[0]), jnp.where(take, line, g[1])]
    else:
        take = masks.lane >= LANES - EDGE
        g = [jnp.where(take, line, g[0]), jnp.where(take, g[0], g[1])]
    g = [lane_roll(v, cy * EDGE) for v in g]
    g[y_half] = jnp.where(masks.z == target, g[y_half], plane)
    return {(yh, half): part(g[yh], half) for yh, half in both}


def collide(b, u, k, g, e):
    ux, uy, uz = u
    pairs = [(i, i + 1) for i in range(1, VELS, 2)]
    s = {i: b[i] + b[j] for i, j in pairs}
    d = {i: b[i] - b[j] for i, j in pairs}
    p, q, r = s[7] + s[9], s[11] + s[13], s[15] + s[17]
    sx, sy, sz = s[1] + s[1], s[3] + s[3], s[5] + s[5]
    mxx, myy, mzz = sx + (p + q), sy + (p + r), sz + (q + r)
    mxy, mxz, myz = s[7] - s[9], s[11] - s[13], s[15] - s[17]
    m0 = 12.0 * b[0] + (sx + sy + sz) + (p + q + r)
    m1x = (d[1] + d[1]) + (d[7] + d[9]) + (d[11] + d[13])
    m1y = (d[3] + d[3]) + (d[7] - d[9]) + (d[15] + d[17])
    m1z = (d[5] + d[5]) + (d[11] - d[13]) + (d[15] - d[17])
    nx = mxx * ux + mxy * uy + mxz * uz
    ny = mxy * ux + myy * uy + myz * uz
    nz = mxz * ux + myz * uy + mzz * uz
    vx = g * (m1x + 3.0 * nx - ux * m0)
    vy = g * (m1y + 3.0 * ny - uy * m0)
    vz = g * (m1z + 3.0 * nz - uz * m0)
    o = g * (m0 * e - 1.5 * (ux * nx + uy * ny + uz * nz))
    v = {1: vx, 3: vy, 5: vz, 7: vx + vy, 9: vx - vy, 11: vx + vz, 13: vx - vz, 15: vy + vz, 17: vy - vz}
    out = [k * b[0] + o]
    for i, j in pairs:
        out.append(k * b[i] + (o + v[i]))
        out.append(k * b[j] + (o - v[i]))
    return out


AHEAD, BEHIND, SIBLING, CROSS = OWN + 2, OWN - 2, OWN + 1, OWN - 1


def body(n, inner, *refs):
    (a_hbm, vel_hbm, relax_hbm, words_hbm, nbrs_hbm, ids_hbm, basis_hbm) = refs[:7]
    (a, grad) = refs[7:9]
    (b, vel, relax, basis, fluid, bits, coef, ghost_bits, spread, words, nbrs, ids) = refs[9:21]
    bufs = refs[21 : 21 + STEPS]
    (part1, part2, part3, without, local_sem, send_sem, recv_sem, sums1, sums2, direct) = refs[21 + STEPS :]
    me = lax.axis_index("blk")
    outer = n // inner
    place = me % inner
    group = me // inner
    way = 1 - 2 * (me % 2)
    ahead, behind, sibling, cross = me + 2 * way, me - 2 * way, me + way, me - way
    has_ahead = (ahead >= 0) & (ahead < n)
    has_behind = (behind >= 0) & (behind < n)
    others = [t + (t >= place).astype(jnp.int32) for t in range(inner - 1)]
    groups = [t + (t >= group).astype(jnp.int32) for t in range(outer - 1)]
    inner_peers = [group * inner + p for p in others]
    outer_peers = [g * inner + place for g in groups]

    apart = n // 4 // inner
    late_groups = [apart * j - 1 for j in range(1, 4)] if apart > 2 else []
    late = [g * inner + p for g in late_groups for p in (inner - 2, inner - 1)]
    early_groups, early_places = range(2), inner // 2
    early = [g * inner + p for g in early_groups for p in range(early_places)]
    in_late_group = (group % apart == apart - 1) & (group < outer - 1) if late else False
    is_late = in_late_group & (place >= inner - 2)
    is_early = (group < 2) & (place < early_places)
    is_split = in_late_group & (place < early_places)
    is_top = (place >= inner - 2).astype(jnp.int32)

    barrier = pltpu.get_barrier_semaphore()

    def greet(peer):
        pl.semaphore_signal(barrier, inc=1, device_id=(peer,), device_id_type=pl.DeviceIdType.MESH)

    pl.when(has_ahead)(lambda: greet(ahead))
    pl.when(has_behind)(lambda: greet(behind))
    pl.when(has_behind)(lambda: greet(cross))
    greet(sibling)
    if late:

        @pl.when(is_early)
        def _():
            for device in late:
                greet(device)

    greetings = (len(early) * is_late.astype(jnp.int32) if late else 0) + inner + outer - 1 + has_ahead.astype(jnp.int32) + 2 * has_behind.astype(jnp.int32)

    tables = [
        pltpu.make_async_copy(words_hbm, words, local_sem.at[7]),
        pltpu.make_async_copy(nbrs_hbm, nbrs, local_sem.at[8]),
        pltpu.make_async_copy(ids_hbm, ids, local_sem.at[9]),
    ]
    for table in tables:
        table.start()
    loads = []
    for yh in range(2):
        loads.append(pltpu.make_async_copy(a_hbm.at[:, :, yh, :], a.at[:, yh], local_sem.at[yh]))
        loads.append(pltpu.make_async_copy(vel_hbm.at[:, :, yh, :], vel.at[:, yh], local_sem.at[2 + yh]))
        loads.append(pltpu.make_async_copy(relax_hbm.at[:, yh, :], relax.at[yh], local_sem.at[4 + yh]))
    load_basis = pltpu.make_async_copy(basis_hbm, basis, local_sem.at[6])
    load_basis.start()
    for load in loads:
        load.start()

    for peer in inner_peers + outer_peers:
        greet(peer)

    masks = Masks()
    for table in tables:
        table.wait()
    for yh in range(2):
        word = jnp.zeros((EDGE, LANES), jnp.int32)
        for x in range(EDGE):
            at = x * 8 + yh * 4
            w = [words[0, at + j] for j in range(4)]
            line = jnp.where(
                masks.lane < 64,
                jnp.where(masks.lane < 32, w[0], w[1]),
                jnp.where(masks.lane < 96, w[2], w[3]),
            )
            word = jnp.where(masks.row == x, line, word)
        bit = jnp.bitwise_and(jnp.right_shift(word, masks.lane % 32), 1)
        fluid[yh] = bit.astype(jnp.float32)

    is_inlet = jnp.int32(0)
    for r in range(NIN):
        is_inlet = is_inlet + (ids[r] == me).astype(jnp.int32)
    keep = 1.0 - is_inlet.astype(jnp.float32)
    keep_z = jnp.where(masks.z == 0, keep, 1.0)
    slot_of = []
    present = []
    for k in range(NEIGHBOURS):
        entry = nbrs[0, k]
        there = (entry >= 0).astype(jnp.int32)
        slot = jnp.clip(OWN + (entry - me) * way, 0, 2 * REACH)
        slot_of.append(slot * there + OWN * (1 - there))
        present.append(there.astype(jnp.float32))

    def halo(step, index, source, target, peer):
        rows = pl.ds(0, ROWS if step == 0 else SENT)
        return pltpu.make_async_remote_copy(
            src_ref=bufs[step].at[source, rows],
            dst_ref=bufs[step].at[target, rows],
            send_sem=send_sem.at[step, index],
            recv_sem=recv_sem.at[step, index],
            device_id=(peer,),
            device_id_type=pl.DeviceIdType.MESH,
        )

    def row_copy(source, target, row, sems, arrived, peer):
        return pltpu.make_async_remote_copy(
            src_ref=source,
            dst_ref=target.at[pl.ds(row, 1)],
            send_sem=sems.at[0],
            recv_sem=sems.at[arrived],
            device_id=(peer,),
            device_id_type=pl.DeviceIdType.MESH,
        )

    def rank_at(mine, p):
        return 1 + mine - (mine > p).astype(jnp.int32)

    def wait_rows(part, sem, start, count):
        rows = part.at[pl.ds(start, count)]
        pltpu.make_async_copy(rows, rows, sem).wait()

    def wait_first_stage(later):
        for top, cut in ((0, inner - 2), (1, inner - 1)):

            @pl.when(is_top == top)
            def _(cut=cut):
                if later:
                    wait_rows(part1, sums1.at[2], cut, inner - cut)
                else:
                    wait_rows(part1, sums1.at[1], 1, cut - 1)

    layer = [jnp.zeros((EDGE, LANES), jnp.float32) for _ in range(2)]
    for load in loads:
        load.wait()
    exchanges = []
    for step in range(STEPS):
        buf = bufs[step]
        for yh in range(2):
            layer[yh] = layer[yh] + (2.0 * a[5, yh] + ((a[11, yh] + a[14, yh]) + (a[15, yh] + a[18, yh])))
        if step == STEPS - 1:
            mode = lax.broadcasted_iota(jnp.int32, (MODES, LANES), 0)
            total = jnp.zeros((MODES, LANES), jnp.float32)
            for m in range(MODES):
                product = spread[m, 0] * layer[0] + spread[m, 1] * layer[1]
                total = jnp.where(mode == m, jnp.sum(product, axis=0, keepdims=True), total)
            total = jnp.sum(total, axis=1, keepdims=True)
            at_mode = lax.broadcasted_iota(jnp.int32, (MODES, LANES), 1) == mode
            part1[pl.ds(0, 1), :] = jnp.sum(jnp.where(at_mode, total, 0.0), axis=0, keepdims=True)
            if late:

                @pl.when(is_late)
                def _():
                    rank = 2 * (group // apart) + place - (inner - 2)
                    for device in early:
                        row_copy(part1.at[pl.ds(0, 1)], part3, rank, direct, 1, device).start()

            for peer, p in zip(inner_peers, others):
                row_copy(part1.at[pl.ds(0, 1)], part1, rank_at(place, p), sums1, 1 + is_top, peer).start()
        pack(buf.at[OWN], a, fluid if step == 0 else None, masks)
        if step == 0:
            pl.semaphore_wait(barrier, greetings)
        to_ahead = halo(step, 0, OWN, BEHIND, ahead)
        to_behind = halo(step, 1, OWN, AHEAD, behind)
        to_sibling = halo(step, 2, OWN, SIBLING, sibling)
        to_cross = halo(step, 3, OWN, CROSS, cross)
        exchanges.append((to_ahead, to_behind, to_sibling, to_cross))
        pl.when(has_ahead)(to_ahead.start)
        pl.when(has_behind)(to_behind.start)
        pl.when(has_behind)(to_cross.start)
        to_sibling.start()
        for yh in range(2):
            if step == 0:
                f = fluid[yh]
                squared = vel[0, yh] * vel[0, yh] + vel[1, yh] * vel[1, yh] + vel[2, yh] * vel[2, yh]
                coef[0, yh] = f * (1.0 - relax[yh])
                coef[1, yh] = f * relax[yh] * (1.0 / 12.0)
                coef[2, yh] = (1.0 / 3.0) + 0.5 * squared
        if step == 0:
            load_basis.wait()
            row = lax.broadcasted_iota(jnp.int32, (EDGE, 2 * LANES), 0)
            flat = lax.broadcasted_iota(jnp.int32, (EDGE, 2 * LANES), 1)
            mine = jnp.zeros((EDGE, 2 * LANES), jnp.float32)
            for r in range(NIN):
                mine = jnp.where(row == r, (ids[r] == me).astype(jnp.float32), mine)
            lines = []
            for m in range(MODES):
                line = jnp.sum(basis[m] * mine, axis=0, keepdims=True)
                lines.append(jnp.where(flat // EDGE == row, line, 0.0))
            lines = jnp.concatenate(lines, axis=0)
            q = lax.broadcasted_iota(jnp.int32, (2 * LANES, LANES), 0)
            site = lax.broadcasted_iota(jnp.int32, (2 * LANES, LANES), 1)
            for yh in range(2):
                pick = ((site % EDGE == 0) & (site // EDGE + 8 * yh == q % EDGE)).astype(jnp.float32)
                placed = jnp.dot(lines, pick, precision=lax.Precision.HIGHEST, preferred_element_type=jnp.float32)
                for m in range(MODES):
                    spread[m, yh] = placed[m * EDGE : (m + 1) * EDGE] * (fluid[yh] * (1.0 / 12.0))
        for yh in range(2):
            b[0, yh] = a[0, yh]
        for i in range(1, VELS):
            if step == 0:
                moved = inside((fluid[0], fluid[1]), C[i], masks)
                for yh in range(2):
                    out = beyond(C[i], yh, masks)
                    bits[i - 1, yh] = moved[yh] if out is None else jnp.where(out, 0.0, moved[yh])
            moved = inside((a[i, 0], a[i, 1]), C[i], masks)
            for yh in range(2):
                back = a[OPP[i], yh]
                if C[i][2] == -1:
                    back = back * keep_z
                b[i, yh] = jnp.where(bits[i - 1, yh] > 0.5, moved[yh], back)
        if step == STEPS - 1:
            wait_first_stage(False)
            if late:

                @pl.when(is_split)
                def _():
                    without[...] = jnp.sum(part1[pl.ds(0, inner - 2), :], axis=0, keepdims=True)
                    for g in early_groups:
                        row_copy(without, part2, group, sums2, 1, g * inner + place).start()

            wait_first_stage(True)
            part2[pl.ds(0, 1), :] = jnp.sum(part1[...], axis=0, keepdims=True)
            for t, (peer, g) in enumerate(zip(outer_peers, groups)):
                copy = row_copy(part2.at[pl.ds(0, 1)], part2, rank_at(group, g), sums2, 1, peer)
                if late and t < len(early_groups):
                    pl.when(jnp.logical_not(is_split))(copy.start)
                else:
                    copy.start()
        to_sibling.wait_recv()
        pl.when(has_ahead)(to_behind.wait_recv)

        @pl.when(has_behind)
        def _():
            to_ahead.wait_recv()
            to_cross.wait_recv()


        def ghost(direction, row, rows):
            return buf[slot_of[DIRECTION[direction]], pl.ds(row, rows), :]

        if step == 0:

            def ghost_fluid(direction, row, rows):
                k = DIRECTION[direction]
                return buf[slot_of[k], pl.ds(row, rows), :] * present[k]

            for i in range(1, VELS):
                for (yh, half), value in outside(FLUID, C[i], ghost_fluid, masks).items():
                    rows = slice(HALF * half, HALF * (half + 1))
                    value = jnp.where(beyond(C[i], yh, masks)[rows], value, 0.0)
                    if C[i][2] == -1:
                        value = value * keep_z[rows]
                    ghost_bits[i - 1, yh, pl.ds(HALF * half, HALF), :] = value
        for i in range(1, VELS):
            for (yh, half), value in outside(i, C[i], ghost, masks).items():
                rows = pl.ds(HALF * half, HALF)
                b[i, yh, rows, :] = jnp.where(ghost_bits[i - 1, yh, rows, :] > 0.5, value, b[i, yh, rows, :])
        for yh in range(2):
            for half in range(2):
                rows = pl.ds(HALF * half, HALF)
                new = collide(
                    [b[i, yh, rows, :] for i in range(VELS)],
                    [vel[c, yh, rows, :] for c in range(3)],
                    coef[0, yh, rows, :],
                    coef[1, yh, rows, :],
                    coef[2, yh, rows, :],
                )
                for i in range(VELS):
                    a[i, yh, rows, :] = new[i]

    for to_ahead, to_behind, to_sibling, to_cross in exchanges:
        pl.when(has_ahead)(to_ahead.wait_send)
        pl.when(has_behind)(to_behind.wait_send)
        to_sibling.wait_send()
        pl.when(has_behind)(to_cross.wait_send)
    wait_rows(part1, sums1.at[0], 1, inner - 1)
    wait_rows(part2, sums2.at[0], 1, outer - 1)
    if late:
        pl.when(is_late)(lambda: wait_rows(part3, direct.at[0], 0, len(early)))
    wait_rows(part2, sums2.at[1], 1, outer - 1)
    grad[...] = jnp.sum(part2[...], axis=0, keepdims=True)[:, :MODES]
    if late:

        @pl.when(is_early)
        def _():
            wait_rows(part3, direct.at[1], 0, len(late))
            grad[...] += jnp.sum(part3[pl.ds(0, len(late)), :], axis=0, keepdims=True)[:, :MODES]


def hand_over(parts, state, grad_in, out, grad, sem):
    stores = [pltpu.make_async_copy(grad_in, grad, sem.at[2 * parts])]
    bounds = [VELS * j // parts for j in range(parts + 1)]
    for j in range(parts):
        for yh in range(2):
            rows = pl.ds(bounds[j], bounds[j + 1] - bounds[j])
            stores.append(pltpu.make_async_copy(state.at[rows, yh], out.at[rows, :, yh], sem.at[2 * j + yh]))
    for store in stores:
        store.start()
    for store in stores:
        store.wait()


def on_device(adjoint, velocity, relax, fluid_words, neighbours, inlet_ids, basis):
    n = lax.axis_size("blk")
    inner = 8 if n % 64 == 0 else 4
    outer = n // inner
    f32 = jnp.float32
    shape = (EDGE, 2, LANES)
    any_space = pl.BlockSpec(memory_space=pl.ANY)
    dma = pltpu.SemaphoreType.DMA
    out, grad = pl.pallas_call(
        lambda *refs: body(n, inner, *refs),
        out_shape=(
            pltpu.VMEM((VELS, 2, EDGE, LANES), f32),
            pltpu.VMEM((1, MODES), f32),
        ),
        in_specs=[any_space] * 7,
        out_specs=(pl.BlockSpec(memory_space=pltpu.VMEM), pl.BlockSpec(memory_space=pltpu.VMEM)),
        scratch_shapes=[
            pltpu.VMEM((VELS, 2, EDGE, LANES), f32),
            pltpu.VMEM((3, 2, EDGE, LANES), f32),
            pltpu.VMEM((2, EDGE, LANES), f32),
            pltpu.VMEM((MODES, NIN, 2 * LANES), f32),
            pltpu.VMEM((2, EDGE, LANES), f32),
            pltpu.VMEM((VELS - 1, 2, EDGE, LANES), f32),
            pltpu.VMEM((3, 2, EDGE, LANES), f32),
            pltpu.VMEM((VELS - 1, 2, EDGE, LANES), f32),
            pltpu.VMEM((MODES, 2, EDGE, LANES), f32),
            pltpu.SMEM((1, EDGE * EDGE * EDGE // 32), jnp.int32),
            pltpu.SMEM((1, NEIGHBOURS), jnp.int32),
            pltpu.SMEM((NIN,), jnp.int32),
        ]
        + [pltpu.VMEM((2 * REACH + 1, ROWS, LANES), f32) for _ in range(STEPS)]
        + [
            pltpu.VMEM((inner, LANES), f32),
            pltpu.VMEM((outer, LANES), f32),
            pltpu.VMEM((8, LANES), f32),
            pltpu.VMEM((1, LANES), f32),
            dma((10,)),
            dma((STEPS, 4)),
            dma((STEPS, 4)),
            dma((3,)),
            dma((2,)),
            dma((2,)),
        ],
        compiler_params=pltpu.CompilerParams(collective_id=0, has_side_effects=True),
        name="adjoint_steps",
    )(
        adjoint.reshape((VELS,) + shape),
        velocity.reshape((3,) + shape),
        relax.reshape(shape),
        fluid_words,
        neighbours,
        inlet_ids,
        basis,
    )
    parts = 1
    out, grad = pl.pallas_call(
        functools.partial(hand_over, parts),
        out_shape=(
            jax.ShapeDtypeStruct((VELS,) + shape, f32),
            jax.ShapeDtypeStruct((1, MODES), f32),
        ),
        in_specs=[pl.BlockSpec(memory_space=pltpu.VMEM)] * 2,
        out_specs=(any_space, any_space),
        scratch_shapes=[dma((2 * parts + 1,))],
        name="hand_over",
    )(pltpu.with_memory_space_constraint(out, pltpu.VMEM), pltpu.with_memory_space_constraint(grad, pltpu.VMEM))
    return (out.reshape(1, VELS, EDGE * EDGE * EDGE), grad.reshape(MODES))


def solution(mesh):
    return jax.shard_map(
        on_device,
        mesh=mesh,
        in_specs=(
            P("blk", None, None),
            P("blk", None, None),
            P("blk", None),
            P("blk", None),
            P("blk", None),
            P(),
            P(),
        ),
        out_specs=(P("blk", None, None), P()),
        check_vma=False,
    )
```

```python
import functools

import jax
import jax.numpy as jnp
import numpy as np
from jax import lax
from jax.experimental import pallas as pl
from jax.experimental.pallas import tpu as pltpu
from jax.sharding import PartitionSpec as P

EDGE = 16
VELS = 19
NEIGHBOURS = 18
REACH = 2
STEPS = 4
LANES = 128
NIN = 16
MODES = 8

C = np.array(
    [
        [0, 0, 0],
        [1, 0, 0],
        [-1, 0, 0],
        [0, 1, 0],
        [0, -1, 0],
        [0, 0, 1],
        [0, 0, -1],
        [1, 1, 0],
        [-1, -1, 0],
        [1, -1, 0],
        [-1, 1, 0],
        [1, 0, 1],
        [-1, 0, -1],
        [1, 0, -1],
        [-1, 0, 1],
        [0, 1, 1],
        [0, -1, -1],
        [0, 1, -1],
        [0, -1, 1],
    ],
    dtype=np.int32,
)
OPP = [0, 2, 1, 4, 3, 6, 5, 8, 7, 10, 9, 12, 11, 14, 13, 16, 15, 18, 17]
DIRECTION = {tuple(int(v) for v in C[k + 1]): k for k in range(NEIGHBOURS)}

FLUID = -1


def members(axis, sign):
    found = [i for i in range(VELS) if C[i][axis] == sign]
    return sorted(found, key=lambda i: int(np.abs(C[i]).sum()), reverse=True)


Z_ROWS, Y_ROWS, AXIS_ROWS, X_ROWS = 0, 16, 32, 48
YZ_FLUID, X_FLUID = 0, 16
ROWS, FLUID_ROWS = 68, 20
SIGNS = (1, -1)
Z_NUMBER = {i: n for n, i in enumerate([i for s in SIGNS for i in members(2, s)[:4]])}
Y_NUMBER = {i: n for n, i in enumerate([i for s in SIGNS for i in members(1, s)[:4]])}
X_NUMBER = {i: n for n, i in enumerate([i for s in SIGNS for i in members(0, s)])}
CUT = 12
OWN = REACH


def sign_index(sign):
    return 0 if sign == 1 else 1


def x_row(item, sign, yh):
    if item == FLUID:
        return X_FLUID + 2 * sign_index(sign) + yh
    return X_ROWS + 2 * X_NUMBER[item] + yh


def lane_roll(value, by):
    by = by % LANES
    return value if by == 0 else pltpu.roll(value, LANES - by, 1)


def row_roll(value, by):
    return pltpu.roll(value, (-by) % EDGE, 0)


class Masks:
    def __init__(self):
        self.lane = lax.broadcasted_iota(jnp.int32, (EDGE, LANES), 1)
        self.row = lax.broadcasted_iota(jnp.int32, (EDGE, LANES), 0)
        self.z = self.lane % EDGE
        self.yl = self.lane // EDGE


def put(block, mask, value):
    return value if block is None else jnp.where(mask, value, block)


def pack_axis(load, items, masks):
    block = None
    for sign in SIGNS:
        yh, start = (0, 0) if sign == 1 else (1, LANES - EDGE)
        plane = load(items[(1, sign)], yh)
        at = 4 * sign_index(sign) * EDGE + 4
        first = lane_roll(plane, start - at)
        second = lane_roll(plane, start + CUT - at - EDGE)
        block = put(block, masks.yl == at // EDGE, first)
        block = put(block, masks.yl == at // EDGE + 1, second)
    for sign in SIGNS:
        start = 0 if sign == 1 else EDGE - 1
        for yh in range(2):
            slot = 2 * sign_index(sign) + yh
            block = put(block, masks.z == slot, lane_roll(load(items[(2, sign)], yh), start - slot))
    return block


AXIS = {(1, 1): 3, (1, -1): 4, (2, 1): 5, (2, -1): 6}


def pack_fluid(package, fluid, masks):
    package[pl.ds(YZ_FLUID, EDGE), :] = pack_axis(lambda item, yh: fluid[yh], {key: FLUID for key in AXIS}, masks)
    for sign in SIGNS:
        for yh in range(2):
            line = fluid[yh, pl.ds(0 if sign == 1 else EDGE - 1, 1), :]
            package[pl.ds(x_row(FLUID, sign, yh), 1), :] = line


def pack(package, a, masks):
    def load(item, yh):
        return a[item, yh]

    block = None
    for sign in SIGNS:
        start = 0 if sign == 1 else EDGE - 1
        for item in members(2, sign)[:4]:
            for yh in range(2):
                slot = 2 * Z_NUMBER[item] + yh
                block = put(block, masks.z == slot, lane_roll(load(item, yh), start - slot))
    package[pl.ds(Z_ROWS, EDGE), :] = block
    block = None
    for sign in SIGNS:
        yh, start = (0, 0) if sign == 1 else (1, LANES - EDGE)
        for item in members(1, sign)[:4]:
            number = Y_NUMBER[item]
            block = put(block, masks.yl == number, lane_roll(load(item, yh), start - number * EDGE))
    package[pl.ds(Y_ROWS, EDGE), :] = block
    package[pl.ds(AXIS_ROWS, EDGE), :] = pack_axis(load, AXIS, masks)
    for sign in SIGNS:
        x_at = 0 if sign == 1 else EDGE - 1
        for item in members(0, sign):
            for yh in range(2):
                package[pl.ds(x_row(item, sign, yh), 1), :] = a[item, yh, pl.ds(x_at, 1), :]


def y_plane(ghost, direction, item, sign, at, masks, only=None):
    if item in Y_NUMBER:
        return lane_roll(ghost(direction, Y_ROWS, EDGE), Y_NUMBER[item] * EDGE - at)
    block = ghost(direction, YZ_FLUID if item == FLUID else AXIS_ROWS, EDGE)
    start = 4 * sign_index(sign) * EDGE + 4
    first = lane_roll(block, start - at) if only is None or only < CUT else None
    second = lane_roll(block, start + EDGE - CUT - at) if only is None or only >= CUT else None
    if first is None or second is None:
        return second if first is None else first
    return jnp.where((masks.lane + (LANES - at)) % LANES < CUT, first, second)


def z_plane(ghost, direction, item, sign, yh, target):
    if item in Z_NUMBER:
        return lane_roll(ghost(direction, Z_ROWS, EDGE), 2 * Z_NUMBER[item] + yh - target)
    block = ghost(direction, YZ_FLUID if item == FLUID else AXIS_ROWS, EDGE)
    return lane_roll(block, 2 * sign_index(sign) + yh - target)


def inside(field, c, masks):
    cx, cy, cz = (int(v) for v in c)
    v0, v1 = field
    if cx:
        v0, v1 = row_roll(v0, cx), row_roll(v1, cx)
    if cy == 1:
        take = masks.lane < EDGE
        v0, v1 = jnp.where(take, v1, v0), v1
    elif cy == -1:
        take = masks.lane >= LANES - EDGE
        v0, v1 = v0, jnp.where(take, v0, v1)
    by = cy * EDGE + cz
    return lane_roll(v0, by), lane_roll(v1, by)


def beyond(c, yh, masks):
    cx, cy, cz = (int(v) for v in c)
    out = None
    if cx:
        out = masks.row == (EDGE - 1 if cx == 1 else 0)
    if cy and yh == (1 if cy == 1 else 0):
        last = masks.yl == (LANES // EDGE - 1 if cy == 1 else 0)
        out = last if out is None else out | last
    if cz:
        last = masks.z == (EDGE - 1 if cz == 1 else 0)
        out = last if out is None else out | last
    return out


HALF = 8


def outside(item, c, ghost, masks):
    cx, cy, cz = (int(v) for v in c)
    both = [(yh, half) for yh in range(2) for half in range(2)]

    def part(value, half):
        return value[HALF * half : HALF * (half + 1)]

    if cx:
        x_half = 1 if cx == 1 else 0
        x_last = masks.row[:HALF] == (HALF - 1 if cx == 1 else 0)
        x_line = [ghost((cx, 0, 0), x_row(item, cx, yh), 1) for yh in range(2)]
    if cy:
        y_half = 1 if cy == 1 else 0
        at, final = (0, LANES - EDGE) if cy == 1 else (LANES - EDGE, 0)
        plane = y_plane(ghost, (0, cy, 0), item, cy, final - cz, masks)
    if cz:
        target = EDGE - 1 if cz == 1 else 0
        source = EDGE - 1 - target
        g = [z_plane(ghost, (0, 0, cz), item, cz, yh, target) for yh in range(2)]
    if cx and not cy and not cz:
        return {(yh, x_half): jnp.broadcast_to(x_line[yh], (HALF, LANES)) for yh in range(2)}
    if cy and not cx and not cz:
        return {(y_half, half): part(plane, half) for half in range(2)}
    if cz and not cx and not cy:
        return {(yh, half): part(g[yh], half) for yh, half in both}
    if cx and cy:
        plane = row_roll(plane, cx)
        line = ghost((cx, cy, 0), x_row(item, cx, 1 - y_half), 1)
        lane = masks.lane[:1]
        take = lane < EDGE if cy == 1 else lane >= LANES - EDGE
        corner, other = (1, 0) if cy == 1 else (0, 1)
        row = [None, None]
        row[corner] = lane_roll(jnp.where(take, line, x_line[corner]), cy * EDGE)
        row[other] = lane_roll(jnp.where(take, x_line[corner], x_line[other]), cy * EDGE)
        return {
            (other, x_half): jnp.broadcast_to(row[other], (HALF, LANES)),
            (corner, x_half): jnp.where(x_last, row[corner], part(plane, x_half)),
            (corner, 1 - x_half): part(plane, 1 - x_half),
        }
    if cx and cz:
        found = {}
        for yh in range(2):
            line = lane_roll(ghost((cx, 0, cz), x_row(item, cx, yh), 1), source - target)
            row = jnp.where(masks.z[:1] == target, line, lane_roll(x_line[yh], cz))
            rolled = row_roll(g[yh], cx)
            found[(yh, x_half)] = jnp.where(x_last, row, part(rolled, x_half))
            found[(yh, 1 - x_half)] = part(rolled, 1 - x_half)
        return found
    line = y_plane(ghost, (0, cy, cz), item, cy, at + target - source, masks, source)
    if cy == 1:
        take = masks.lane < EDGE
        g = [jnp.where(take, g[1], g[0]), jnp.where(take, line, g[1])]
    else:
        take = masks.lane >= LANES - EDGE
        g = [jnp.where(take, line, g[0]), jnp.where(take, g[0], g[1])]
    g = [lane_roll(v, cy * EDGE) for v in g]
    g[y_half] = jnp.where(masks.z == target, g[y_half], plane)
    return {(yh, half): part(g[yh], half) for yh, half in both}


def collide(b, u, k, g, e):
    ux, uy, uz = u
    pairs = [(i, i + 1) for i in range(1, VELS, 2)]
    s = {i: b[i] + b[j] for i, j in pairs}
    d = {i: b[i] - b[j] for i, j in pairs}
    p, q, r = s[7] + s[9], s[11] + s[13], s[15] + s[17]
    sx, sy, sz = s[1] + s[1], s[3] + s[3], s[5] + s[5]
    mxx, myy, mzz = sx + (p + q), sy + (p + r), sz + (q + r)
    mxy, mxz, myz = s[7] - s[9], s[11] - s[13], s[15] - s[17]
    m0 = 12.0 * b[0] + (sx + sy + sz) + (p + q + r)
    m1x = (d[1] + d[1]) + (d[7] + d[9]) + (d[11] + d[13])
    m1y = (d[3] + d[3]) + (d[7] - d[9]) + (d[15] + d[17])
    m1z = (d[5] + d[5]) + (d[11] - d[13]) + (d[15] - d[17])
    nx = mxx * ux + mxy * uy + mxz * uz
    ny = mxy * ux + myy * uy + myz * uz
    nz = mxz * ux + myz * uy + mzz * uz
    vx = g * (m1x + 3.0 * nx - ux * m0)
    vy = g * (m1y + 3.0 * ny - uy * m0)
    vz = g * (m1z + 3.0 * nz - uz * m0)
    o = g * (m0 * e - 1.5 * (ux * nx + uy * ny + uz * nz))
    v = {1: vx, 3: vy, 5: vz, 7: vx + vy, 9: vx - vy, 11: vx + vz, 13: vx - vz, 15: vy + vz, 17: vy - vz}
    out = [k * b[0] + o]
    for i, j in pairs:
        out.append(k * b[i] + (o + v[i]))
        out.append(k * b[j] + (o - v[i]))
    return out


AHEAD, BEHIND, SIBLING, CROSS = OWN + 2, OWN - 2, OWN + 1, OWN - 1


def body(n, inner, *refs):
    (a_hbm, vel_hbm, relax_hbm, words_hbm, nbrs_hbm, ids_hbm, basis_hbm) = refs[:7]
    (a, grad) = refs[7:9]
    (b, vel, relax, basis, fluid, bits, coef, ghost_bits, spread, words, nbrs, ids) = refs[9:21]
    bufs = refs[21 : 21 + STEPS]
    (fluids, part1, part2, part3, without, local_sem, send_sem, recv_sem, sums1, sums2, direct) = refs[21 + STEPS :]
    me = lax.axis_index("blk")
    outer = n // inner
    place = me % inner
    group = me // inner
    way = 1 - 2 * (me % 2)
    ahead, behind, sibling, cross = me + 2 * way, me - 2 * way, me + way, me - way
    has_ahead = (ahead >= 0) & (ahead < n)
    has_behind = (behind >= 0) & (behind < n)
    others = [t + (t >= place).astype(jnp.int32) for t in range(inner - 1)]
    groups = [t + (t >= group).astype(jnp.int32) for t in range(outer - 1)]
    inner_peers = [group * inner + p for p in others]
    outer_peers = [g * inner + place for g in groups]

    apart = n // 4 // inner
    late_groups = [apart * j - 1 for j in range(1, 4)] if apart > 2 else []
    late = [g * inner + p for g in late_groups for p in (inner - 2, inner - 1)]
    early_groups, early_places = range(3), inner - 2
    early = [g * inner + p for g in early_groups for p in range(early_places)]
    in_late_group = (group % apart == apart - 1) & (group < outer - 1) if late else False
    is_late = in_late_group & (place >= inner - 2)
    is_early = (group < len(early_groups)) & (place < early_places)
    is_split = in_late_group & (place < early_places)
    is_top = (place >= inner - 2).astype(jnp.int32)

    barrier = pltpu.get_barrier_semaphore()

    def greet(peer):
        pl.semaphore_signal(barrier, inc=1, device_id=(peer,), device_id_type=pl.DeviceIdType.MESH)

    pl.when(has_ahead)(lambda: greet(ahead))
    pl.when(has_behind)(lambda: greet(behind))
    pl.when(has_behind)(lambda: greet(cross))
    greet(sibling)
    if late:

        @pl.when(is_early)
        def _():
            for device in late:
                greet(device)

    greetings = (len(early) * is_late.astype(jnp.int32) if late else 0) + inner + outer - 1 + has_ahead.astype(jnp.int32) + 2 * has_behind.astype(jnp.int32)

    tables = [
        pltpu.make_async_copy(words_hbm, words, local_sem.at[7]),
        pltpu.make_async_copy(nbrs_hbm, nbrs, local_sem.at[8]),
        pltpu.make_async_copy(ids_hbm, ids, local_sem.at[9]),
    ]
    for table in tables:
        table.start()
    loads = []
    for yh in range(2):
        loads.append(pltpu.make_async_copy(a_hbm.at[:, :, yh, :], a.at[:, yh], local_sem.at[yh]))
        loads.append(pltpu.make_async_copy(vel_hbm.at[:, :, yh, :], vel.at[:, yh], local_sem.at[2 + yh]))
        loads.append(pltpu.make_async_copy(relax_hbm.at[:, yh, :], relax.at[yh], local_sem.at[4 + yh]))
    load_basis = pltpu.make_async_copy(basis_hbm, basis, local_sem.at[6])
    load_basis.start()
    for load in loads:
        load.start()

    for peer in inner_peers + outer_peers:
        greet(peer)

    masks = Masks()
    for table in tables:
        table.wait()
    for yh in range(2):
        word = jnp.zeros((EDGE, LANES), jnp.int32)
        for x in range(EDGE):
            at = x * 8 + yh * 4
            w = [words[0, at + j] for j in range(4)]
            line = jnp.where(
                masks.lane < 64,
                jnp.where(masks.lane < 32, w[0], w[1]),
                jnp.where(masks.lane < 96, w[2], w[3]),
            )
            word = jnp.where(masks.row == x, line, word)
        bit = jnp.bitwise_and(jnp.right_shift(word, masks.lane % 32), 1)
        fluid[yh] = bit.astype(jnp.float32)

    is_inlet = jnp.int32(0)
    for r in range(NIN):
        is_inlet = is_inlet + (ids[r] == me).astype(jnp.int32)
    keep = 1.0 - is_inlet.astype(jnp.float32)
    keep_z = jnp.where(masks.z == 0, keep, 1.0)
    slot_of = []
    present = []
    for k in range(NEIGHBOURS):
        entry = nbrs[0, k]
        there = (entry >= 0).astype(jnp.int32)
        slot = jnp.clip(OWN + (entry - me) * way, 0, 2 * REACH)
        slot_of.append(slot * there + OWN * (1 - there))
        present.append(there.astype(jnp.float32))

    def halo(step, index, source, target, peer):
        buf = fluids if step == STEPS else bufs[step]
        return pltpu.make_async_remote_copy(
            src_ref=buf.at[source],
            dst_ref=buf.at[target],
            send_sem=send_sem.at[step, index],
            recv_sem=recv_sem.at[step, index],
            device_id=(peer,),
            device_id_type=pl.DeviceIdType.MESH,
        )

    def row_copy(source, target, row, sems, arrived, peer):
        return pltpu.make_async_remote_copy(
            src_ref=source,
            dst_ref=target.at[pl.ds(row, 1)],
            send_sem=sems.at[0],
            recv_sem=sems.at[arrived],
            device_id=(peer,),
            device_id_type=pl.DeviceIdType.MESH,
        )

    def rank_at(mine, p):
        return 1 + mine - (mine > p).astype(jnp.int32)

    def wait_rows(part, sem, start, count):
        rows = part.at[pl.ds(start, count)]
        pltpu.make_async_copy(rows, rows, sem).wait()

    def wait_first_stage(later):
        for top, cut in ((0, inner - 2), (1, inner - 1)):

            @pl.when(is_top == top)
            def _(cut=cut):
                if later:
                    wait_rows(part1, sums1.at[2], cut, inner - cut)
                else:
                    wait_rows(part1, sums1.at[1], 1, cut - 1)

    layer = [jnp.zeros((EDGE, LANES), jnp.float32) for _ in range(2)]
    for load in loads:
        load.wait()
    def exchange(step):
        to_ahead = halo(step, 0, OWN, BEHIND, ahead)
        to_behind = halo(step, 1, OWN, AHEAD, behind)
        to_sibling = halo(step, 2, OWN, SIBLING, sibling)
        to_cross = halo(step, 3, OWN, CROSS, cross)
        pl.when(has_ahead)(to_ahead.start)
        pl.when(has_behind)(to_behind.start)
        pl.when(has_behind)(to_cross.start)
        to_sibling.start()
        return (to_ahead, to_behind, to_sibling, to_cross)

    def arrive(to_ahead, to_behind, to_sibling, to_cross):
        to_sibling.wait_recv()
        pl.when(has_ahead)(to_behind.wait_recv)

        @pl.when(has_behind)
        def _():
            to_ahead.wait_recv()
            to_cross.wait_recv()

    exchanges = []
    for step in range(STEPS):
        buf = bufs[step]
        for yh in range(2):
            layer[yh] = layer[yh] + (2.0 * a[5, yh] + ((a[11, yh] + a[14, yh]) + (a[15, yh] + a[18, yh])))
        if step == STEPS - 1:
            mode = lax.broadcasted_iota(jnp.int32, (MODES, LANES), 0)
            total = jnp.zeros((MODES, LANES), jnp.float32)
            for m in range(MODES):
                product = spread[m, 0] * layer[0] + spread[m, 1] * layer[1]
                total = jnp.where(mode == m, jnp.sum(product, axis=0, keepdims=True), total)
            total = jnp.sum(total, axis=1, keepdims=True)
            at_mode = lax.broadcasted_iota(jnp.int32, (MODES, LANES), 1) == mode
            part1[pl.ds(0, 1), :] = jnp.sum(jnp.where(at_mode, total, 0.0), axis=0, keepdims=True)
            if late:

                @pl.when(is_late)
                def _():
                    rank = 2 * (group // apart) + place - (inner - 2)
                    for device in early:
                        row_copy(part1.at[pl.ds(0, 1)], part3, rank, direct, 1, device).start()

            for peer, p in zip(inner_peers, others):
                row_copy(part1.at[pl.ds(0, 1)], part1, rank_at(place, p), sums1, 1 + is_top, peer).start()
        pack(buf.at[OWN], a, masks)
        if step == 0:
            pack_fluid(fluids.at[OWN], fluid, masks)
            pl.semaphore_wait(barrier, greetings)
            exchanges.append(exchange(STEPS))
        exchanges.append(exchange(step))
        for yh in range(2):
            if step == 0:
                f = fluid[yh]
                squared = vel[0, yh] * vel[0, yh] + vel[1, yh] * vel[1, yh] + vel[2, yh] * vel[2, yh]
                coef[0, yh] = f * (1.0 - relax[yh])
                coef[1, yh] = f * relax[yh] * (1.0 / 12.0)
                coef[2, yh] = (1.0 / 3.0) + 0.5 * squared
        if step == 0:
            load_basis.wait()
            row = lax.broadcasted_iota(jnp.int32, (EDGE, 2 * LANES), 0)
            flat = lax.broadcasted_iota(jnp.int32, (EDGE, 2 * LANES), 1)
            mine = jnp.zeros((EDGE, 2 * LANES), jnp.float32)
            for r in range(NIN):
                mine = jnp.where(row == r, (ids[r] == me).astype(jnp.float32), mine)
            lines = []
            for m in range(MODES):
                line = jnp.sum(basis[m] * mine, axis=0, keepdims=True)
                lines.append(jnp.where(flat // EDGE == row, line, 0.0))
            lines = jnp.concatenate(lines, axis=0)
            q = lax.broadcasted_iota(jnp.int32, (2 * LANES, LANES), 0)
            site = lax.broadcasted_iota(jnp.int32, (2 * LANES, LANES), 1)
            for yh in range(2):
                pick = ((site % EDGE == 0) & (site // EDGE + 8 * yh == q % EDGE)).astype(jnp.float32)
                placed = jnp.dot(lines, pick, precision=lax.Precision.HIGHEST, preferred_element_type=jnp.float32)
                for m in range(MODES):
                    spread[m, yh] = placed[m * EDGE : (m + 1) * EDGE] * (fluid[yh] * (1.0 / 12.0))
        for yh in range(2):
            b[0, yh] = a[0, yh]
        for i in range(1, VELS):
            if step == 0:
                moved = inside((fluid[0], fluid[1]), C[i], masks)
                for yh in range(2):
                    out = beyond(C[i], yh, masks)
                    bits[i - 1, yh] = moved[yh] if out is None else jnp.where(out, 0.0, moved[yh])
            moved = inside((a[i, 0], a[i, 1]), C[i], masks)
            for yh in range(2):
                back = a[OPP[i], yh]
                if C[i][2] == -1:
                    back = back * keep_z
                b[i, yh] = jnp.where(bits[i - 1, yh] > 0.5, moved[yh], back)
        if step == STEPS - 1:
            wait_first_stage(False)
            if late:

                @pl.when(is_split)
                def _():
                    without[...] = jnp.sum(part1[pl.ds(0, inner - 2), :], axis=0, keepdims=True)
                    for g in early_groups:
                        row_copy(without, part2, group, sums2, 1, g * inner + place).start()

            wait_first_stage(True)
            part2[pl.ds(0, 1), :] = jnp.sum(part1[...], axis=0, keepdims=True)
            for t, (peer, g) in enumerate(zip(outer_peers, groups)):
                copy = row_copy(part2.at[pl.ds(0, 1)], part2, rank_at(group, g), sums2, 1, peer)
                if late and t < len(early_groups):
                    pl.when(jnp.logical_not(is_split))(copy.start)
                else:
                    copy.start()
        def ghost(direction, row, rows):
            return buf[slot_of[DIRECTION[direction]], pl.ds(row, rows), :]

        if step == 0:
            arrive(*exchanges[0])

            def ghost_fluid(direction, row, rows):
                k = DIRECTION[direction]
                return fluids[slot_of[k], pl.ds(row, rows), :] * present[k]

            for i in range(1, VELS):
                for (yh, half), value in outside(FLUID, C[i], ghost_fluid, masks).items():
                    rows = slice(HALF * half, HALF * (half + 1))
                    value = jnp.where(beyond(C[i], yh, masks)[rows], value, 0.0)
                    if C[i][2] == -1:
                        value = value * keep_z[rows]
                    ghost_bits[i - 1, yh, pl.ds(HALF * half, HALF), :] = value
        arrive(*exchanges[-1])
        for i in range(1, VELS):
            for (yh, half), value in outside(i, C[i], ghost, masks).items():
                rows = pl.ds(HALF * half, HALF)
                b[i, yh, rows, :] = jnp.where(ghost_bits[i - 1, yh, rows, :] > 0.5, value, b[i, yh, rows, :])
        for yh in range(2):
            for half in range(2):
                rows = pl.ds(HALF * half, HALF)
                new = collide(
                    [b[i, yh, rows, :] for i in range(VELS)],
                    [vel[c, yh, rows, :] for c in range(3)],
                    coef[0, yh, rows, :],
                    coef[1, yh, rows, :],
                    coef[2, yh, rows, :],
                )
                for i in range(VELS):
                    a[i, yh, rows, :] = new[i]

    for to_ahead, to_behind, to_sibling, to_cross in exchanges:
        pl.when(has_ahead)(to_ahead.wait_send)
        pl.when(has_behind)(to_behind.wait_send)
        to_sibling.wait_send()
        pl.when(has_behind)(to_cross.wait_send)
    wait_rows(part1, sums1.at[0], 1, inner - 1)
    wait_rows(part2, sums2.at[0], 1, outer - 1)
    if late:
        pl.when(is_late)(lambda: wait_rows(part3, direct.at[0], 0, len(early)))
    wait_rows(part2, sums2.at[1], 1, outer - 1)
    grad[...] = jnp.sum(part2[...], axis=0, keepdims=True)[:, :MODES]
    if late:

        @pl.when(is_early)
        def _():
            wait_rows(part3, direct.at[1], 0, len(late))
            grad[...] += jnp.sum(part3[pl.ds(0, len(late)), :], axis=0, keepdims=True)[:, :MODES]


def hand_over(parts, state, grad_in, out, grad, sem):
    stores = [pltpu.make_async_copy(grad_in, grad, sem.at[2 * parts])]
    bounds = [VELS * j // parts for j in range(parts + 1)]
    for j in range(parts):
        for yh in range(2):
            rows = pl.ds(bounds[j], bounds[j + 1] - bounds[j])
            stores.append(pltpu.make_async_copy(state.at[rows, yh], out.at[rows, :, yh], sem.at[2 * j + yh]))
    for store in stores:
        store.start()
    for store in stores:
        store.wait()


def on_device(adjoint, velocity, relax, fluid_words, neighbours, inlet_ids, basis):
    n = lax.axis_size("blk")
    inner = 8 if n % 64 == 0 else 4
    outer = n // inner
    f32 = jnp.float32
    shape = (EDGE, 2, LANES)
    any_space = pl.BlockSpec(memory_space=pl.ANY)
    dma = pltpu.SemaphoreType.DMA
    out, grad = pl.pallas_call(
        lambda *refs: body(n, inner, *refs),
        out_shape=(
            pltpu.VMEM((VELS, 2, EDGE, LANES), f32),
            pltpu.VMEM((1, MODES), f32),
        ),
        in_specs=[any_space] * 7,
        out_specs=(pl.BlockSpec(memory_space=pltpu.VMEM), pl.BlockSpec(memory_space=pltpu.VMEM)),
        scratch_shapes=[
            pltpu.VMEM((VELS, 2, EDGE, LANES), f32),
            pltpu.VMEM((3, 2, EDGE, LANES), f32),
            pltpu.VMEM((2, EDGE, LANES), f32),
            pltpu.VMEM((MODES, NIN, 2 * LANES), f32),
            pltpu.VMEM((2, EDGE, LANES), f32),
            pltpu.VMEM((VELS - 1, 2, EDGE, LANES), f32),
            pltpu.VMEM((3, 2, EDGE, LANES), f32),
            pltpu.VMEM((VELS - 1, 2, EDGE, LANES), f32),
            pltpu.VMEM((MODES, 2, EDGE, LANES), f32),
            pltpu.SMEM((1, EDGE * EDGE * EDGE // 32), jnp.int32),
            pltpu.SMEM((1, NEIGHBOURS), jnp.int32),
            pltpu.SMEM((NIN,), jnp.int32),
        ]
        + [pltpu.VMEM((2 * REACH + 1, ROWS, LANES), f32) for _ in range(STEPS)]
        + [
            pltpu.VMEM((2 * REACH + 1, FLUID_ROWS, LANES), f32),
            pltpu.VMEM((inner, LANES), f32),
            pltpu.VMEM((outer, LANES), f32),
            pltpu.VMEM((24, LANES), f32),
            pltpu.VMEM((1, LANES), f32),
            dma((10,)),
            dma((STEPS + 1, 4)),
            dma((STEPS + 1, 4)),
            dma((3,)),
            dma((2,)),
            dma((2,)),
        ],
        compiler_params=pltpu.CompilerParams(collective_id=0, has_side_effects=True),
        name="adjoint_steps",
    )(
        adjoint.reshape((VELS,) + shape),
        velocity.reshape((3,) + shape),
        relax.reshape(shape),
        fluid_words,
        neighbours,
        inlet_ids,
        basis,
    )
    parts = 1
    out, grad = pl.pallas_call(
        functools.partial(hand_over, parts),
        out_shape=(
            jax.ShapeDtypeStruct((VELS,) + shape, f32),
            jax.ShapeDtypeStruct((1, MODES), f32),
        ),
        in_specs=[pl.BlockSpec(memory_space=pltpu.VMEM)] * 2,
        out_specs=(any_space, any_space),
        scratch_shapes=[dma((2 * parts + 1,))],
        name="hand_over",
    )(pltpu.with_memory_space_constraint(out, pltpu.VMEM), pltpu.with_memory_space_constraint(grad, pltpu.VMEM))
    return (out.reshape(1, VELS, EDGE * EDGE * EDGE), grad.reshape(MODES))


def solution(mesh):
    return jax.shard_map(
        on_device,
        mesh=mesh,
        in_specs=(
            P("blk", None, None),
            P("blk", None, None),
            P("blk", None),
            P("blk", None),
            P("blk", None),
            P(),
            P(),
        ),
        out_specs=(P("blk", None, None), P()),
        check_vma=False,
    )
```

```python
import functools

import jax
import jax.numpy as jnp
import numpy as np
from jax import lax
from jax.experimental import pallas as pl
from jax.experimental.pallas import tpu as pltpu
from jax.sharding import PartitionSpec as P

EDGE = 16
VELS = 19
NEIGHBOURS = 18
REACH = 2
STEPS = 4
LANES = 128
NIN = 16
MODES = 8

C = np.array(
    [
        [0, 0, 0],
        [1, 0, 0],
        [-1, 0, 0],
        [0, 1, 0],
        [0, -1, 0],
        [0, 0, 1],
        [0, 0, -1],
        [1, 1, 0],
        [-1, -1, 0],
        [1, -1, 0],
        [-1, 1, 0],
        [1, 0, 1],
        [-1, 0, -1],
        [1, 0, -1],
        [-1, 0, 1],
        [0, 1, 1],
        [0, -1, -1],
        [0, 1, -1],
        [0, -1, 1],
    ],
    dtype=np.int32,
)
OPP = [0, 2, 1, 4, 3, 6, 5, 8, 7, 10, 9, 12, 11, 14, 13, 16, 15, 18, 17]
DIRECTION = {tuple(int(v) for v in C[k + 1]): k for k in range(NEIGHBOURS)}

FLUID = -1


def members(axis, sign):
    found = [i for i in range(VELS) if C[i][axis] == sign]
    return sorted(found, key=lambda i: int(np.abs(C[i]).sum()), reverse=True)


Z_ROWS, Y_ROWS, AXIS_ROWS, X_ROWS = 0, 16, 32, 48
YZ_FLUID, X_FLUID = 0, 16
ROWS, FLUID_ROWS = 68, 20
SIGNS = (1, -1)
Z_NUMBER = {i: n for n, i in enumerate([i for s in SIGNS for i in members(2, s)[:4]])}
Y_NUMBER = {i: n for n, i in enumerate([i for s in SIGNS for i in members(1, s)[:4]])}
X_NUMBER = {i: n for n, i in enumerate([i for s in SIGNS for i in members(0, s)])}
CUT = 12
OWN = REACH


def sign_index(sign):
    return 0 if sign == 1 else 1


def x_row(item, sign, yh):
    if item == FLUID:
        return X_FLUID + 2 * sign_index(sign) + yh
    return X_ROWS + 2 * X_NUMBER[item] + yh


def lane_roll(value, by):
    by = by % LANES
    return value if by == 0 else pltpu.roll(value, LANES - by, 1)


def row_roll(value, by):
    return pltpu.roll(value, (-by) % EDGE, 0)


class Masks:
    def __init__(self):
        self.lane = lax.broadcasted_iota(jnp.int32, (EDGE, LANES), 1)
        self.row = lax.broadcasted_iota(jnp.int32, (EDGE, LANES), 0)
        self.z = self.lane % EDGE
        self.yl = self.lane // EDGE


def put(block, mask, value):
    return value if block is None else jnp.where(mask, value, block)


def pack_axis(load, items, masks):
    block = None
    for sign in SIGNS:
        yh, start = (0, 0) if sign == 1 else (1, LANES - EDGE)
        plane = load(items[(1, sign)], yh)
        at = 4 * sign_index(sign) * EDGE + 4
        first = lane_roll(plane, start - at)
        second = lane_roll(plane, start + CUT - at - EDGE)
        block = put(block, masks.yl == at // EDGE, first)
        block = put(block, masks.yl == at // EDGE + 1, second)
    for sign in SIGNS:
        start = 0 if sign == 1 else EDGE - 1
        for yh in range(2):
            slot = 2 * sign_index(sign) + yh
            block = put(block, masks.z == slot, lane_roll(load(items[(2, sign)], yh), start - slot))
    return block


AXIS = {(1, 1): 3, (1, -1): 4, (2, 1): 5, (2, -1): 6}


def pack_fluid(package, fluid, masks):
    package[pl.ds(YZ_FLUID, EDGE), :] = pack_axis(lambda item, yh: fluid[yh], {key: FLUID for key in AXIS}, masks)
    for sign in SIGNS:
        for yh in range(2):
            line = fluid[yh, pl.ds(0 if sign == 1 else EDGE - 1, 1), :]
            package[pl.ds(x_row(FLUID, sign, yh), 1), :] = line


def pack(package, a, masks):
    def load(item, yh):
        return a[item, yh]

    block = None
    for sign in SIGNS:
        start = 0 if sign == 1 else EDGE - 1
        for item in members(2, sign)[:4]:
            for yh in range(2):
                slot = 2 * Z_NUMBER[item] + yh
                block = put(block, masks.z == slot, lane_roll(load(item, yh), start - slot))
    package[pl.ds(Z_ROWS, EDGE), :] = block
    block = None
    for sign in SIGNS:
        yh, start = (0, 0) if sign == 1 else (1, LANES - EDGE)
        for item in members(1, sign)[:4]:
            number = Y_NUMBER[item]
            block = put(block, masks.yl == number, lane_roll(load(item, yh), start - number * EDGE))
    package[pl.ds(Y_ROWS, EDGE), :] = block
    package[pl.ds(AXIS_ROWS, EDGE), :] = pack_axis(load, AXIS, masks)
    for sign in SIGNS:
        x_at = 0 if sign == 1 else EDGE - 1
        for item in members(0, sign):
            for yh in range(2):
                package[pl.ds(x_row(item, sign, yh), 1), :] = a[item, yh, pl.ds(x_at, 1), :]


def y_plane(ghost, direction, item, sign, at, masks, only=None):
    if item in Y_NUMBER:
        return lane_roll(ghost(direction, Y_ROWS, EDGE), Y_NUMBER[item] * EDGE - at)
    block = ghost(direction, YZ_FLUID if item == FLUID else AXIS_ROWS, EDGE)
    start = 4 * sign_index(sign) * EDGE + 4
    first = lane_roll(block, start - at) if only is None or only < CUT else None
    second = lane_roll(block, start + EDGE - CUT - at) if only is None or only >= CUT else None
    if first is None or second is None:
        return second if first is None else first
    return jnp.where((masks.lane + (LANES - at)) % LANES < CUT, first, second)


def z_plane(ghost, direction, item, sign, yh, target):
    if item in Z_NUMBER:
        return lane_roll(ghost(direction, Z_ROWS, EDGE), 2 * Z_NUMBER[item] + yh - target)
    block = ghost(direction, YZ_FLUID if item == FLUID else AXIS_ROWS, EDGE)
    return lane_roll(block, 2 * sign_index(sign) + yh - target)


def inside(field, c, masks):
    cx, cy, cz = (int(v) for v in c)
    v0, v1 = field
    if cx:
        v0, v1 = row_roll(v0, cx), row_roll(v1, cx)
    if cy == 1:
        take = masks.lane < EDGE
        v0, v1 = jnp.where(take, v1, v0), v1
    elif cy == -1:
        take = masks.lane >= LANES - EDGE
        v0, v1 = v0, jnp.where(take, v0, v1)
    by = cy * EDGE + cz
    return lane_roll(v0, by), lane_roll(v1, by)


def beyond(c, yh, masks):
    cx, cy, cz = (int(v) for v in c)
    out = None
    if cx:
        out = masks.row == (EDGE - 1 if cx == 1 else 0)
    if cy and yh == (1 if cy == 1 else 0):
        last = masks.yl == (LANES // EDGE - 1 if cy == 1 else 0)
        out = last if out is None else out | last
    if cz:
        last = masks.z == (EDGE - 1 if cz == 1 else 0)
        out = last if out is None else out | last
    return out


HALF = 8


def outside(item, c, ghost, masks):
    cx, cy, cz = (int(v) for v in c)
    both = [(yh, half) for yh in range(2) for half in range(2)]

    def part(value, half):
        return value[HALF * half : HALF * (half + 1)]

    if cx:
        x_half = 1 if cx == 1 else 0
        x_last = masks.row[:HALF] == (HALF - 1 if cx == 1 else 0)
        x_line = [ghost((cx, 0, 0), x_row(item, cx, yh), 1) for yh in range(2)]
    if cy:
        y_half = 1 if cy == 1 else 0
        at, final = (0, LANES - EDGE) if cy == 1 else (LANES - EDGE, 0)
        plane = y_plane(ghost, (0, cy, 0), item, cy, final - cz, masks)
    if cz:
        target = EDGE - 1 if cz == 1 else 0
        source = EDGE - 1 - target
        g = [z_plane(ghost, (0, 0, cz), item, cz, yh, target) for yh in range(2)]
    if cx and not cy and not cz:
        return {(yh, x_half): jnp.broadcast_to(x_line[yh], (HALF, LANES)) for yh in range(2)}
    if cy and not cx and not cz:
        return {(y_half, half): part(plane, half) for half in range(2)}
    if cz and not cx and not cy:
        return {(yh, half): part(g[yh], half) for yh, half in both}
    if cx and cy:
        plane = row_roll(plane, cx)
        line = ghost((cx, cy, 0), x_row(item, cx, 1 - y_half), 1)
        lane = masks.lane[:1]
        take = lane < EDGE if cy == 1 else lane >= LANES - EDGE
        corner, other = (1, 0) if cy == 1 else (0, 1)
        row = [None, None]
        row[corner] = lane_roll(jnp.where(take, line, x_line[corner]), cy * EDGE)
        row[other] = lane_roll(jnp.where(take, x_line[corner], x_line[other]), cy * EDGE)
        return {
            (other, x_half): jnp.broadcast_to(row[other], (HALF, LANES)),
            (corner, x_half): jnp.where(x_last, row[corner], part(plane, x_half)),
            (corner, 1 - x_half): part(plane, 1 - x_half),
        }
    if cx and cz:
        found = {}
        for yh in range(2):
            line = lane_roll(ghost((cx, 0, cz), x_row(item, cx, yh), 1), source - target)
            row = jnp.where(masks.z[:1] == target, line, lane_roll(x_line[yh], cz))
            rolled = row_roll(g[yh], cx)
            found[(yh, x_half)] = jnp.where(x_last, row, part(rolled, x_half))
            found[(yh, 1 - x_half)] = part(rolled, 1 - x_half)
        return found
    line = y_plane(ghost, (0, cy, cz), item, cy, at + target - source, masks, source)
    if cy == 1:
        take = masks.lane < EDGE
        g = [jnp.where(take, g[1], g[0]), jnp.where(take, line, g[1])]
    else:
        take = masks.lane >= LANES - EDGE
        g = [jnp.where(take, line, g[0]), jnp.where(take, g[0], g[1])]
    g = [lane_roll(v, cy * EDGE) for v in g]
    g[y_half] = jnp.where(masks.z == target, g[y_half], plane)
    return {(yh, half): part(g[yh], half) for yh, half in both}


def collide(b, u, k, g, e):
    ux, uy, uz = u
    pairs = [(i, i + 1) for i in range(1, VELS, 2)]
    s = {i: b[i] + b[j] for i, j in pairs}
    d = {i: b[i] - b[j] for i, j in pairs}
    p, q, r = s[7] + s[9], s[11] + s[13], s[15] + s[17]
    sx, sy, sz = s[1] + s[1], s[3] + s[3], s[5] + s[5]
    mxx, myy, mzz = sx + (p + q), sy + (p + r), sz + (q + r)
    mxy, mxz, myz = s[7] - s[9], s[11] - s[13], s[15] - s[17]
    m0 = 12.0 * b[0] + (sx + sy + sz) + (p + q + r)
    m1x = (d[1] + d[1]) + (d[7] + d[9]) + (d[11] + d[13])
    m1y = (d[3] + d[3]) + (d[7] - d[9]) + (d[15] + d[17])
    m1z = (d[5] + d[5]) + (d[11] - d[13]) + (d[15] - d[17])
    nx = mxx * ux + mxy * uy + mxz * uz
    ny = mxy * ux + myy * uy + myz * uz
    nz = mxz * ux + myz * uy + mzz * uz
    vx = g * (m1x + 3.0 * nx - ux * m0)
    vy = g * (m1y + 3.0 * ny - uy * m0)
    vz = g * (m1z + 3.0 * nz - uz * m0)
    o = g * (m0 * e - 1.5 * (ux * nx + uy * ny + uz * nz))
    v = {1: vx, 3: vy, 5: vz, 7: vx + vy, 9: vx - vy, 11: vx + vz, 13: vx - vz, 15: vy + vz, 17: vy - vz}
    out = [k * b[0] + o]
    for i, j in pairs:
        out.append(k * b[i] + (o + v[i]))
        out.append(k * b[j] + (o - v[i]))
    return out


AHEAD, BEHIND, SIBLING, CROSS = OWN + 2, OWN - 2, OWN + 1, OWN - 1


def body(n, inner, *refs):
    (a_hbm, vel_hbm, relax_hbm, words_hbm, nbrs_hbm, ids_hbm, basis_hbm) = refs[:7]
    (a, grad) = refs[7:9]
    (b, vel, relax, basis, fluid, bits, coef, ghost_bits, spread, words, nbrs, ids) = refs[9:21]
    bufs = refs[21 : 21 + STEPS]
    (fluids, part1, part2, part3, without, local_sem, send_sem, recv_sem, sums1, sums2, direct) = refs[21 + STEPS :]
    me = lax.axis_index("blk")
    outer = n // inner
    place = me % inner
    group = me // inner
    way = 1 - 2 * (me % 2)
    ahead, behind, sibling, cross = me + 2 * way, me - 2 * way, me + way, me - way
    has_ahead = (ahead >= 0) & (ahead < n)
    has_behind = (behind >= 0) & (behind < n)
    others = [t + (t >= place).astype(jnp.int32) for t in range(inner - 1)]
    groups = [t + (t >= group).astype(jnp.int32) for t in range(outer - 1)]
    inner_peers = [group * inner + p for p in others]
    outer_peers = [g * inner + place for g in groups]

    apart = n // 4 // inner
    late_groups = [apart * j - 1 for j in range(1, 4)] if apart > 2 else []
    late = [g * inner + p for g in late_groups for p in (inner - 2, inner - 1)]
    early_groups, early_places = range(3), inner - 2
    early = [g * inner + p for g in early_groups for p in range(early_places)]
    in_late_group = (group % apart == apart - 1) & (group < outer - 1) if late else False
    is_late = in_late_group & (place >= inner - 2)
    is_early = (group < len(early_groups)) & (place < early_places)
    is_split = in_late_group & (place < early_places)
    is_top = (place >= inner - 2).astype(jnp.int32)

    barrier = pltpu.get_barrier_semaphore()

    def greet(peer):
        pl.semaphore_signal(barrier, inc=1, device_id=(peer,), device_id_type=pl.DeviceIdType.MESH)

    pl.when(has_ahead)(lambda: greet(ahead))
    pl.when(has_behind)(lambda: greet(behind))
    pl.when(has_behind)(lambda: greet(cross))
    greet(sibling)
    if late:

        @pl.when(is_early)
        def _():
            for device in late:
                greet(device)

    greetings = (len(early) * is_late.astype(jnp.int32) if late else 0) + inner + outer - 1 + has_ahead.astype(jnp.int32) + 2 * has_behind.astype(jnp.int32)

    tables = [
        pltpu.make_async_copy(words_hbm, words, local_sem.at[7]),
        pltpu.make_async_copy(nbrs_hbm, nbrs, local_sem.at[8]),
        pltpu.make_async_copy(ids_hbm, ids, local_sem.at[9]),
    ]
    for table in tables:
        table.start()
    loads = []
    for yh in range(2):
        loads.append(pltpu.make_async_copy(a_hbm.at[:, :, yh, :], a.at[:, yh], local_sem.at[yh]))
        loads.append(pltpu.make_async_copy(vel_hbm.at[:, :, yh, :], vel.at[:, yh], local_sem.at[2 + yh]))
        loads.append(pltpu.make_async_copy(relax_hbm.at[:, yh, :], relax.at[yh], local_sem.at[4 + yh]))
    load_basis = pltpu.make_async_copy(basis_hbm, basis, local_sem.at[6])
    load_basis.start()
    for load in loads:
        load.start()

    for peer in outer_peers[::-1] + inner_peers:
        greet(peer)

    masks = Masks()
    for table in tables:
        table.wait()
    for yh in range(2):
        word = jnp.zeros((EDGE, LANES), jnp.int32)
        for x in range(EDGE):
            at = x * 8 + yh * 4
            w = [words[0, at + j] for j in range(4)]
            line = jnp.where(
                masks.lane < 64,
                jnp.where(masks.lane < 32, w[0], w[1]),
                jnp.where(masks.lane < 96, w[2], w[3]),
            )
            word = jnp.where(masks.row == x, line, word)
        bit = jnp.bitwise_and(jnp.right_shift(word, masks.lane % 32), 1)
        fluid[yh] = bit.astype(jnp.float32)

    is_inlet = jnp.int32(0)
    for r in range(NIN):
        is_inlet = is_inlet + (ids[r] == me).astype(jnp.int32)
    keep = 1.0 - is_inlet.astype(jnp.float32)
    keep_z = jnp.where(masks.z == 0, keep, 1.0)
    slot_of = []
    present = []
    for k in range(NEIGHBOURS):
        entry = nbrs[0, k]
        there = (entry >= 0).astype(jnp.int32)
        slot = jnp.clip(OWN + (entry - me) * way, 0, 2 * REACH)
        slot_of.append(slot * there + OWN * (1 - there))
        present.append(there.astype(jnp.float32))

    def halo(step, index, source, target, peer):
        buf = fluids if step == STEPS else bufs[step]
        return pltpu.make_async_remote_copy(
            src_ref=buf.at[source],
            dst_ref=buf.at[target],
            send_sem=send_sem.at[step, index],
            recv_sem=recv_sem.at[step, index],
            device_id=(peer,),
            device_id_type=pl.DeviceIdType.MESH,
        )

    def row_copy(source, target, row, sems, arrived, peer):
        return pltpu.make_async_remote_copy(
            src_ref=source,
            dst_ref=target.at[pl.ds(row, 1)],
            send_sem=sems.at[0],
            recv_sem=sems.at[arrived],
            device_id=(peer,),
            device_id_type=pl.DeviceIdType.MESH,
        )

    def rank_at(mine, p):
        return 1 + mine - (mine > p).astype(jnp.int32)

    def wait_rows(part, sem, start, count):
        rows = part.at[pl.ds(start, count)]
        pltpu.make_async_copy(rows, rows, sem).wait()

    def wait_first_stage(later):
        for top, cut in ((0, inner - 2), (1, inner - 1)):

            @pl.when(is_top == top)
            def _(cut=cut):
                if later:
                    wait_rows(part1, sums1.at[2], cut, inner - cut)
                else:
                    wait_rows(part1, sums1.at[1], 1, cut - 1)

    layer = [jnp.zeros((EDGE, LANES), jnp.float32) for _ in range(2)]
    for load in loads:
        load.wait()
    def exchange(step):
        to_ahead = halo(step, 0, OWN, BEHIND, ahead)
        to_behind = halo(step, 1, OWN, AHEAD, behind)
        to_sibling = halo(step, 2, OWN, SIBLING, sibling)
        to_cross = halo(step, 3, OWN, CROSS, cross)
        pl.when(has_ahead)(to_ahead.start)
        pl.when(has_behind)(to_behind.start)
        pl.when(has_behind)(to_cross.start)
        to_sibling.start()
        return (to_ahead, to_behind, to_sibling, to_cross)

    def arrive(to_ahead, to_behind, to_sibling, to_cross):
        to_sibling.wait_recv()
        pl.when(has_ahead)(to_behind.wait_recv)

        @pl.when(has_behind)
        def _():
            to_ahead.wait_recv()
            to_cross.wait_recv()

    def add_layer():
        for yh in range(2):
            layer[yh] = layer[yh] + (2.0 * a[5, yh] + ((a[11, yh] + a[14, yh]) + (a[15, yh] + a[18, yh])))

    exchanges = []
    for step in range(STEPS):
        buf = bufs[step]
        if step == STEPS - 1:
            add_layer()
        if step == STEPS - 1:
            mode = lax.broadcasted_iota(jnp.int32, (MODES, LANES), 0)
            total = jnp.zeros((MODES, LANES), jnp.float32)
            for m in range(MODES):
                product = spread[m, 0] * layer[0] + spread[m, 1] * layer[1]
                total = jnp.where(mode == m, jnp.sum(product, axis=0, keepdims=True), total)
            total = jnp.sum(total, axis=1, keepdims=True)
            at_mode = lax.broadcasted_iota(jnp.int32, (MODES, LANES), 1) == mode
            part1[pl.ds(0, 1), :] = jnp.sum(jnp.where(at_mode, total, 0.0), axis=0, keepdims=True)
            if late:

                @pl.when(is_late)
                def _():
                    rank = 2 * (group // apart) + place - (inner - 2)
                    for device in early:
                        row_copy(part1.at[pl.ds(0, 1)], part3, rank, direct, 1, device).start()

            for peer, p in zip(inner_peers, others):
                row_copy(part1.at[pl.ds(0, 1)], part1, rank_at(place, p), sums1, 1 + is_top, peer).start()
        pack(buf.at[OWN], a, masks)
        if step == 0:
            pack_fluid(fluids.at[OWN], fluid, masks)
            pl.semaphore_wait(barrier, greetings)
            exchanges.append(exchange(STEPS))
        exchanges.append(exchange(step))
        if step < STEPS - 1:
            add_layer()
        for yh in range(2):
            if step == 0:
                f = fluid[yh]
                squared = vel[0, yh] * vel[0, yh] + vel[1, yh] * vel[1, yh] + vel[2, yh] * vel[2, yh]
                coef[0, yh] = f * (1.0 - relax[yh])
                coef[1, yh] = f * relax[yh] * (1.0 / 12.0)
                coef[2, yh] = (1.0 / 3.0) + 0.5 * squared
        if step == 0:
            load_basis.wait()
            row = lax.broadcasted_iota(jnp.int32, (EDGE, 2 * LANES), 0)
            flat = lax.broadcasted_iota(jnp.int32, (EDGE, 2 * LANES), 1)
            mine = jnp.zeros((EDGE, 2 * LANES), jnp.float32)
            for r in range(NIN):
                mine = jnp.where(row == r, (ids[r] == me).astype(jnp.float32), mine)
            lines = []
            for m in range(MODES):
                line = jnp.sum(basis[m] * mine, axis=0, keepdims=True)
                lines.append(jnp.where(flat // EDGE == row, line, 0.0))
            lines = jnp.concatenate(lines, axis=0)
            q = lax.broadcasted_iota(jnp.int32, (2 * LANES, LANES), 0)
            site = lax.broadcasted_iota(jnp.int32, (2 * LANES, LANES), 1)
            for yh in range(2):
                pick = ((site % EDGE == 0) & (site // EDGE + 8 * yh == q % EDGE)).astype(jnp.float32)
                placed = jnp.dot(lines, pick, precision=lax.Precision.HIGHEST, preferred_element_type=jnp.float32)
                for m in range(MODES):
                    spread[m, yh] = placed[m * EDGE : (m + 1) * EDGE] * (fluid[yh] * (1.0 / 12.0))
        for yh in range(2):
            b[0, yh] = a[0, yh]
        for i in range(1, VELS):
            if step == 0:
                moved = inside((fluid[0], fluid[1]), C[i], masks)
                for yh in range(2):
                    out = beyond(C[i], yh, masks)
                    bits[i - 1, yh] = moved[yh] if out is None else jnp.where(out, 0.0, moved[yh])
            moved = inside((a[i, 0], a[i, 1]), C[i], masks)
            for yh in range(2):
                back = a[OPP[i], yh]
                if C[i][2] == -1:
                    back = back * keep_z
                b[i, yh] = jnp.where(bits[i - 1, yh] > 0.5, moved[yh], back)
        if step == STEPS - 1:
            wait_first_stage(False)
            if late:

                @pl.when(is_split)
                def _():
                    without[...] = jnp.sum(part1[pl.ds(0, inner - 2), :], axis=0, keepdims=True)
                    for g in early_groups:
                        row_copy(without, part2, group, sums2, 1, g * inner + place).start()

            wait_first_stage(True)
            part2[pl.ds(0, 1), :] = jnp.sum(part1[...], axis=0, keepdims=True)
            for t, (peer, g) in enumerate(zip(outer_peers, groups)):
                copy = row_copy(part2.at[pl.ds(0, 1)], part2, rank_at(group, g), sums2, 1, peer)
                if late and t < len(early_groups):
                    pl.when(jnp.logical_not(is_split))(copy.start)
                else:
                    copy.start()
        def ghost(direction, row, rows):
            return buf[slot_of[DIRECTION[direction]], pl.ds(row, rows), :]

        if step == 0:
            arrive(*exchanges[0])

            def ghost_fluid(direction, row, rows):
                k = DIRECTION[direction]
                return fluids[slot_of[k], pl.ds(row, rows), :] * present[k]

            for i in range(1, VELS):
                for (yh, half), value in outside(FLUID, C[i], ghost_fluid, masks).items():
                    rows = slice(HALF * half, HALF * (half + 1))
                    value = jnp.where(beyond(C[i], yh, masks)[rows], value, 0.0)
                    if C[i][2] == -1:
                        value = value * keep_z[rows]
                    ghost_bits[i - 1, yh, pl.ds(HALF * half, HALF), :] = value
        arrive(*exchanges[-1])
        for i in range(1, VELS):
            for (yh, half), value in outside(i, C[i], ghost, masks).items():
                rows = pl.ds(HALF * half, HALF)
                b[i, yh, rows, :] = jnp.where(ghost_bits[i - 1, yh, rows, :] > 0.5, value, b[i, yh, rows, :])
        for yh in range(2):
            for half in range(2):
                rows = pl.ds(HALF * half, HALF)
                new = collide(
                    [b[i, yh, rows, :] for i in range(VELS)],
                    [vel[c, yh, rows, :] for c in range(3)],
                    coef[0, yh, rows, :],
                    coef[1, yh, rows, :],
                    coef[2, yh, rows, :],
                )
                for i in range(VELS):
                    a[i, yh, rows, :] = new[i]

    for to_ahead, to_behind, to_sibling, to_cross in exchanges:
        pl.when(has_ahead)(to_ahead.wait_send)
        pl.when(has_behind)(to_behind.wait_send)
        to_sibling.wait_send()
        pl.when(has_behind)(to_cross.wait_send)
    wait_rows(part1, sums1.at[0], 1, inner - 1)
    wait_rows(part2, sums2.at[0], 1, outer - 1)
    if late:
        pl.when(is_late)(lambda: wait_rows(part3, direct.at[0], 0, len(early)))
    wait_rows(part2, sums2.at[1], 1, outer - 1)
    grad[...] = jnp.sum(part2[...], axis=0, keepdims=True)[:, :MODES]
    if late:

        @pl.when(is_early)
        def _():
            wait_rows(part3, direct.at[1], 0, len(late))
            grad[...] += jnp.sum(part3[pl.ds(0, len(late)), :], axis=0, keepdims=True)[:, :MODES]


def hand_over(parts, state, grad_in, out, grad, sem):
    stores = [pltpu.make_async_copy(grad_in, grad, sem.at[2 * parts])]
    bounds = [VELS * j // parts for j in range(parts + 1)]
    for j in range(parts):
        for yh in range(2):
            rows = pl.ds(bounds[j], bounds[j + 1] - bounds[j])
            stores.append(pltpu.make_async_copy(state.at[rows, yh], out.at[rows, :, yh], sem.at[2 * j + yh]))
    for store in stores:
        store.start()
    for store in stores:
        store.wait()


def on_device(adjoint, velocity, relax, fluid_words, neighbours, inlet_ids, basis):
    n = lax.axis_size("blk")
    inner = 8 if n % 64 == 0 else 4
    outer = n // inner
    f32 = jnp.float32
    shape = (EDGE, 2, LANES)
    any_space = pl.BlockSpec(memory_space=pl.ANY)
    dma = pltpu.SemaphoreType.DMA
    out, grad = pl.pallas_call(
        lambda *refs: body(n, inner, *refs),
        out_shape=(
            pltpu.VMEM((VELS, 2, EDGE, LANES), f32),
            pltpu.VMEM((1, MODES), f32),
        ),
        in_specs=[any_space] * 7,
        out_specs=(pl.BlockSpec(memory_space=pltpu.VMEM), pl.BlockSpec(memory_space=pltpu.VMEM)),
        scratch_shapes=[
            pltpu.VMEM((VELS, 2, EDGE, LANES), f32),
            pltpu.VMEM((3, 2, EDGE, LANES), f32),
            pltpu.VMEM((2, EDGE, LANES), f32),
            pltpu.VMEM((MODES, NIN, 2 * LANES), f32),
            pltpu.VMEM((2, EDGE, LANES), f32),
            pltpu.VMEM((VELS - 1, 2, EDGE, LANES), f32),
            pltpu.VMEM((3, 2, EDGE, LANES), f32),
            pltpu.VMEM((VELS - 1, 2, EDGE, LANES), f32),
            pltpu.VMEM((MODES, 2, EDGE, LANES), f32),
            pltpu.SMEM((1, EDGE * EDGE * EDGE // 32), jnp.int32),
            pltpu.SMEM((1, NEIGHBOURS), jnp.int32),
            pltpu.SMEM((NIN,), jnp.int32),
        ]
        + [pltpu.VMEM((2 * REACH + 1, ROWS, LANES), f32) for _ in range(STEPS)]
        + [
            pltpu.VMEM((2 * REACH + 1, FLUID_ROWS, LANES), f32),
            pltpu.VMEM((inner, LANES), f32),
            pltpu.VMEM((outer, LANES), f32),
            pltpu.VMEM((24, LANES), f32),
            pltpu.VMEM((1, LANES), f32),
            dma((10,)),
            dma((STEPS + 1, 4)),
            dma((STEPS + 1, 4)),
            dma((3,)),
            dma((2,)),
            dma((2,)),
        ],
        compiler_params=pltpu.CompilerParams(collective_id=0, has_side_effects=True),
        name="adjoint_steps",
    )(
        adjoint.reshape((VELS,) + shape),
        velocity.reshape((3,) + shape),
        relax.reshape(shape),
        fluid_words,
        neighbours,
        inlet_ids,
        basis,
    )
    parts = 1
    out, grad = pl.pallas_call(
        functools.partial(hand_over, parts),
        out_shape=(
            jax.ShapeDtypeStruct((VELS,) + shape, f32),
            jax.ShapeDtypeStruct((1, MODES), f32),
        ),
        in_specs=[pl.BlockSpec(memory_space=pltpu.VMEM)] * 2,
        out_specs=(any_space, any_space),
        scratch_shapes=[dma((2 * parts + 1,))],
        name="hand_over",
    )(pltpu.with_memory_space_constraint(out, pltpu.VMEM), pltpu.with_memory_space_constraint(grad, pltpu.VMEM))
    return (out.reshape(1, VELS, EDGE * EDGE * EDGE), grad.reshape(MODES))


def solution(mesh):
    return jax.shard_map(
        on_device,
        mesh=mesh,
        in_specs=(
            P("blk", None, None),
            P("blk", None, None),
            P("blk", None),
            P("blk", None),
            P("blk", None),
            P(),
            P(),
        ),
        out_specs=(P("blk", None, None), P()),
        check_vma=False,
    )
```

```python
import functools

import jax
import jax.numpy as jnp
import numpy as np
from jax import lax
from jax.experimental import pallas as pl
from jax.experimental.pallas import tpu as pltpu
from jax.sharding import PartitionSpec as P

EDGE = 16
VELS = 19
NEIGHBOURS = 18
REACH = 2
STEPS = 4
LANES = 128
NIN = 16
MODES = 8

C = np.array(
    [
        [0, 0, 0],
        [1, 0, 0],
        [-1, 0, 0],
        [0, 1, 0],
        [0, -1, 0],
        [0, 0, 1],
        [0, 0, -1],
        [1, 1, 0],
        [-1, -1, 0],
        [1, -1, 0],
        [-1, 1, 0],
        [1, 0, 1],
        [-1, 0, -1],
        [1, 0, -1],
        [-1, 0, 1],
        [0, 1, 1],
        [0, -1, -1],
        [0, 1, -1],
        [0, -1, 1],
    ],
    dtype=np.int32,
)
OPP = [0, 2, 1, 4, 3, 6, 5, 8, 7, 10, 9, 12, 11, 14, 13, 16, 15, 18, 17]
DIRECTION = {tuple(int(v) for v in C[k + 1]): k for k in range(NEIGHBOURS)}

FLUID = -1


def members(axis, sign):
    found = [i for i in range(VELS) if C[i][axis] == sign]
    return sorted(found, key=lambda i: int(np.abs(C[i]).sum()), reverse=True)


Z_ROWS, Y_ROWS, AXIS_ROWS, X_ROWS = 0, 16, 32, 48
YZ_FLUID, X_FLUID = 0, 16
ROWS, FLUID_ROWS = 68, 20
SIGNS = (1, -1)
Z_NUMBER = {i: n for n, i in enumerate([i for s in SIGNS for i in members(2, s)[:4]])}
Y_NUMBER = {i: n for n, i in enumerate([i for s in SIGNS for i in members(1, s)[:4]])}
X_NUMBER = {i: n for n, i in enumerate([i for s in SIGNS for i in members(0, s)])}
CUT = 12
OWN = REACH


def sign_index(sign):
    return 0 if sign == 1 else 1


def x_row(item, sign, yh):
    if item == FLUID:
        return X_FLUID + 2 * sign_index(sign) + yh
    return X_ROWS + 2 * X_NUMBER[item] + yh


def lane_roll(value, by):
    by = by % LANES
    return value if by == 0 else pltpu.roll(value, LANES - by, 1)


def row_roll(value, by):
    return pltpu.roll(value, (-by) % EDGE, 0)


class Masks:
    def __init__(self):
        self.lane = lax.broadcasted_iota(jnp.int32, (EDGE, LANES), 1)
        self.row = lax.broadcasted_iota(jnp.int32, (EDGE, LANES), 0)
        self.z = self.lane % EDGE
        self.yl = self.lane // EDGE


def put(block, mask, value):
    return value if block is None else jnp.where(mask, value, block)


def pack_axis(load, items, masks):
    block = None
    for sign in SIGNS:
        yh, start = (0, 0) if sign == 1 else (1, LANES - EDGE)
        plane = load(items[(1, sign)], yh)
        at = 4 * sign_index(sign) * EDGE + 4
        first = lane_roll(plane, start - at)
        second = lane_roll(plane, start + CUT - at - EDGE)
        block = put(block, masks.yl == at // EDGE, first)
        block = put(block, masks.yl == at // EDGE + 1, second)
    for sign in SIGNS:
        start = 0 if sign == 1 else EDGE - 1
        for yh in range(2):
            slot = 2 * sign_index(sign) + yh
            block = put(block, masks.z == slot, lane_roll(load(items[(2, sign)], yh), start - slot))
    return block


AXIS = {(1, 1): 3, (1, -1): 4, (2, 1): 5, (2, -1): 6}


def pack_fluid(package, fluid, masks):
    package[pl.ds(YZ_FLUID, EDGE), :] = pack_axis(lambda item, yh: fluid[yh], {key: FLUID for key in AXIS}, masks)
    for sign in SIGNS:
        for yh in range(2):
            line = fluid[yh, pl.ds(0 if sign == 1 else EDGE - 1, 1), :]
            package[pl.ds(x_row(FLUID, sign, yh), 1), :] = line


def pack(package, a, masks):
    def load(item, yh):
        return a[item, yh]

    block = None
    for sign in SIGNS:
        start = 0 if sign == 1 else EDGE - 1
        for item in members(2, sign)[:4]:
            for yh in range(2):
                slot = 2 * Z_NUMBER[item] + yh
                block = put(block, masks.z == slot, lane_roll(load(item, yh), start - slot))
    package[pl.ds(Z_ROWS, EDGE), :] = block
    block = None
    for sign in SIGNS:
        yh, start = (0, 0) if sign == 1 else (1, LANES - EDGE)
        for item in members(1, sign)[:4]:
            number = Y_NUMBER[item]
            block = put(block, masks.yl == number, lane_roll(load(item, yh), start - number * EDGE))
    package[pl.ds(Y_ROWS, EDGE), :] = block
    package[pl.ds(AXIS_ROWS, EDGE), :] = pack_axis(load, AXIS, masks)
    for sign in SIGNS:
        x_at = 0 if sign == 1 else EDGE - 1
        for item in members(0, sign):
            for yh in range(2):
                package[pl.ds(x_row(item, sign, yh), 1), :] = a[item, yh, pl.ds(x_at, 1), :]


def y_plane(ghost, direction, item, sign, at, masks, only=None):
    if item in Y_NUMBER:
        return lane_roll(ghost(direction, Y_ROWS, EDGE), Y_NUMBER[item] * EDGE - at)
    block = ghost(direction, YZ_FLUID if item == FLUID else AXIS_ROWS, EDGE)
    start = 4 * sign_index(sign) * EDGE + 4
    first = lane_roll(block, start - at) if only is None or only < CUT else None
    second = lane_roll(block, start + EDGE - CUT - at) if only is None or only >= CUT else None
    if first is None or second is None:
        return second if first is None else first
    return jnp.where((masks.lane + (LANES - at)) % LANES < CUT, first, second)


def z_plane(ghost, direction, item, sign, yh, target):
    if item in Z_NUMBER:
        return lane_roll(ghost(direction, Z_ROWS, EDGE), 2 * Z_NUMBER[item] + yh - target)
    block = ghost(direction, YZ_FLUID if item == FLUID else AXIS_ROWS, EDGE)
    return lane_roll(block, 2 * sign_index(sign) + yh - target)


def inside(field, c, masks):
    cx, cy, cz = (int(v) for v in c)
    v0, v1 = field
    if cx:
        v0, v1 = row_roll(v0, cx), row_roll(v1, cx)
    if cy == 1:
        take = masks.lane < EDGE
        v0, v1 = jnp.where(take, v1, v0), v1
    elif cy == -1:
        take = masks.lane >= LANES - EDGE
        v0, v1 = v0, jnp.where(take, v0, v1)
    by = cy * EDGE + cz
    return lane_roll(v0, by), lane_roll(v1, by)


def beyond(c, yh, masks):
    cx, cy, cz = (int(v) for v in c)
    out = None
    if cx:
        out = masks.row == (EDGE - 1 if cx == 1 else 0)
    if cy and yh == (1 if cy == 1 else 0):
        last = masks.yl == (LANES // EDGE - 1 if cy == 1 else 0)
        out = last if out is None else out | last
    if cz:
        last = masks.z == (EDGE - 1 if cz == 1 else 0)
        out = last if out is None else out | last
    return out


HALF = 8


def outside(item, c, ghost, masks):
    cx, cy, cz = (int(v) for v in c)
    both = [(yh, half) for yh in range(2) for half in range(2)]

    def part(value, half):
        return value[HALF * half : HALF * (half + 1)]

    if cx:
        x_half = 1 if cx == 1 else 0
        x_last = masks.row[:HALF] == (HALF - 1 if cx == 1 else 0)
        x_line = [ghost((cx, 0, 0), x_row(item, cx, yh), 1) for yh in range(2)]
    if cy:
        y_half = 1 if cy == 1 else 0
        at, final = (0, LANES - EDGE) if cy == 1 else (LANES - EDGE, 0)
        plane = y_plane(ghost, (0, cy, 0), item, cy, final - cz, masks)
    if cz:
        target = EDGE - 1 if cz == 1 else 0
        source = EDGE - 1 - target
        g = [z_plane(ghost, (0, 0, cz), item, cz, yh, target) for yh in range(2)]
    if cx and not cy and not cz:
        return {(yh, x_half): jnp.broadcast_to(x_line[yh], (HALF, LANES)) for yh in range(2)}
    if cy and not cx and not cz:
        return {(y_half, half): part(plane, half) for half in range(2)}
    if cz and not cx and not cy:
        return {(yh, half): part(g[yh], half) for yh, half in both}
    if cx and cy:
        plane = row_roll(plane, cx)
        line = ghost((cx, cy, 0), x_row(item, cx, 1 - y_half), 1)
        lane = masks.lane[:1]
        take = lane < EDGE if cy == 1 else lane >= LANES - EDGE
        corner, other = (1, 0) if cy == 1 else (0, 1)
        row = [None, None]
        row[corner] = lane_roll(jnp.where(take, line, x_line[corner]), cy * EDGE)
        row[other] = lane_roll(jnp.where(take, x_line[corner], x_line[other]), cy * EDGE)
        return {
            (other, x_half): jnp.broadcast_to(row[other], (HALF, LANES)),
            (corner, x_half): jnp.where(x_last, row[corner], part(plane, x_half)),
            (corner, 1 - x_half): part(plane, 1 - x_half),
        }
    if cx and cz:
        found = {}
        for yh in range(2):
            line = lane_roll(ghost((cx, 0, cz), x_row(item, cx, yh), 1), source - target)
            row = jnp.where(masks.z[:1] == target, line, lane_roll(x_line[yh], cz))
            rolled = row_roll(g[yh], cx)
            found[(yh, x_half)] = jnp.where(x_last, row, part(rolled, x_half))
            found[(yh, 1 - x_half)] = part(rolled, 1 - x_half)
        return found
    line = y_plane(ghost, (0, cy, cz), item, cy, at + target - source, masks, source)
    if cy == 1:
        take = masks.lane < EDGE
        g = [jnp.where(take, g[1], g[0]), jnp.where(take, line, g[1])]
    else:
        take = masks.lane >= LANES - EDGE
        g = [jnp.where(take, line, g[0]), jnp.where(take, g[0], g[1])]
    g = [lane_roll(v, cy * EDGE) for v in g]
    g[y_half] = jnp.where(masks.z == target, g[y_half], plane)
    return {(yh, half): part(g[yh], half) for yh, half in both}


def collide(b, u, k, g, e):
    ux, uy, uz = u
    pairs = [(i, i + 1) for i in range(1, VELS, 2)]
    s = {i: b[i] + b[j] for i, j in pairs}
    d = {i: b[i] - b[j] for i, j in pairs}
    p, q, r = s[7] + s[9], s[11] + s[13], s[15] + s[17]
    sx, sy, sz = s[1] + s[1], s[3] + s[3], s[5] + s[5]
    mxx, myy, mzz = sx + (p + q), sy + (p + r), sz + (q + r)
    mxy, mxz, myz = s[7] - s[9], s[11] - s[13], s[15] - s[17]
    m0 = 12.0 * b[0] + (sx + sy + sz) + (p + q + r)
    m1x = (d[1] + d[1]) + (d[7] + d[9]) + (d[11] + d[13])
    m1y = (d[3] + d[3]) + (d[7] - d[9]) + (d[15] + d[17])
    m1z = (d[5] + d[5]) + (d[11] - d[13]) + (d[15] - d[17])
    nx = mxx * ux + mxy * uy + mxz * uz
    ny = mxy * ux + myy * uy + myz * uz
    nz = mxz * ux + myz * uy + mzz * uz
    vx = g * (m1x + 3.0 * nx - ux * m0)
    vy = g * (m1y + 3.0 * ny - uy * m0)
    vz = g * (m1z + 3.0 * nz - uz * m0)
    o = g * (m0 * e - 1.5 * (ux * nx + uy * ny + uz * nz))
    v = {1: vx, 3: vy, 5: vz, 7: vx + vy, 9: vx - vy, 11: vx + vz, 13: vx - vz, 15: vy + vz, 17: vy - vz}
    out = [k * b[0] + o]
    for i, j in pairs:
        out.append(k * b[i] + (o + v[i]))
        out.append(k * b[j] + (o - v[i]))
    return out


AHEAD, BEHIND, SIBLING, CROSS = OWN + 2, OWN - 2, OWN + 1, OWN - 1


def body(n, inner, *refs):
    (a_hbm, vel_hbm, relax_hbm, words_hbm, nbrs_hbm, ids_hbm, basis_hbm) = refs[:7]
    (a, grad) = refs[7:9]
    (b, vel, relax, basis, fluid, bits, coef, ghost_bits, spread, words, nbrs, ids) = refs[9:21]
    bufs = refs[21 : 21 + STEPS]
    (fluids, part1, part2, part3, without, local_sem, send_sem, recv_sem, sums1, sums2, direct) = refs[21 + STEPS :]
    me = lax.axis_index("blk")
    outer = n // inner
    place = me % inner
    group = me // inner
    way = 1 - 2 * (me % 2)
    ahead, behind, sibling, cross = me + 2 * way, me - 2 * way, me + way, me - way
    has_ahead = (ahead >= 0) & (ahead < n)
    has_behind = (behind >= 0) & (behind < n)
    others = [t + (t >= place).astype(jnp.int32) for t in range(inner - 1)]
    groups = [t + (t >= group).astype(jnp.int32) for t in range(outer - 1)]
    inner_peers = [group * inner + p for p in others]
    outer_peers = [g * inner + place for g in groups]

    apart = n // 4 // inner
    late_groups = [apart * j - 1 for j in range(1, 4)] if apart > 2 else []
    late = [g * inner + p for g in late_groups for p in (inner - 2, inner - 1)]
    early_groups, early_places = range(3), inner - 2
    early = [g * inner + p for g in early_groups for p in range(early_places)]
    in_late_group = (group % apart == apart - 1) & (group < outer - 1) if late else False
    is_late = in_late_group & (place >= inner - 2)
    is_early = (group < len(early_groups)) & (place < early_places)
    is_split = in_late_group & (place < early_places)
    is_top = (place >= inner - 2).astype(jnp.int32)

    barrier = pltpu.get_barrier_semaphore()

    def greet(peer):
        pl.semaphore_signal(barrier, inc=1, device_id=(peer,), device_id_type=pl.DeviceIdType.MESH)

    pl.when(has_ahead)(lambda: greet(ahead))
    pl.when(has_behind)(lambda: greet(behind))
    pl.when(has_behind)(lambda: greet(cross))
    greet(sibling)
    if late:

        @pl.when(is_early)
        def _():
            for device in late:
                greet(device)

    greetings = (len(early) * is_late.astype(jnp.int32) if late else 0) + inner + outer - 1 + has_ahead.astype(jnp.int32) + 2 * has_behind.astype(jnp.int32)

    tables = [
        pltpu.make_async_copy(words_hbm, words, local_sem.at[7]),
        pltpu.make_async_copy(nbrs_hbm, nbrs, local_sem.at[8]),
        pltpu.make_async_copy(ids_hbm, ids, local_sem.at[9]),
    ]
    for table in tables:
        table.start()
    loads = []
    for yh in range(2):
        loads.append(pltpu.make_async_copy(a_hbm.at[:, :, yh, :], a.at[:, yh], local_sem.at[yh]))
        loads.append(pltpu.make_async_copy(vel_hbm.at[:, :, yh, :], vel.at[:, yh], local_sem.at[2 + yh]))
        loads.append(pltpu.make_async_copy(relax_hbm.at[:, yh, :], relax.at[yh], local_sem.at[4 + yh]))
    load_basis = pltpu.make_async_copy(basis_hbm, basis, local_sem.at[6])
    load_basis.start()
    for load in loads:
        load.start()

    for peer in outer_peers[::-1] + inner_peers:
        greet(peer)

    masks = Masks()
    for table in tables:
        table.wait()
    for yh in range(2):
        word = jnp.zeros((EDGE, LANES), jnp.int32)
        for x in range(EDGE):
            at = x * 8 + yh * 4
            w = [words[0, at + j] for j in range(4)]
            line = jnp.where(
                masks.lane < 64,
                jnp.where(masks.lane < 32, w[0], w[1]),
                jnp.where(masks.lane < 96, w[2], w[3]),
            )
            word = jnp.where(masks.row == x, line, word)
        bit = jnp.bitwise_and(jnp.right_shift(word, masks.lane % 32), 1)
        fluid[yh] = bit.astype(jnp.float32)

    is_inlet = jnp.int32(0)
    for r in range(NIN):
        is_inlet = is_inlet + (ids[r] == me).astype(jnp.int32)
    keep = 1.0 - is_inlet.astype(jnp.float32)
    keep_z = jnp.where(masks.z == 0, keep, 1.0)
    slot_of = []
    present = []
    for k in range(NEIGHBOURS):
        entry = nbrs[0, k]
        there = (entry >= 0).astype(jnp.int32)
        slot = jnp.clip(OWN + (entry - me) * way, 0, 2 * REACH)
        slot_of.append(slot * there + OWN * (1 - there))
        present.append(there.astype(jnp.float32))

    def halo(step, index, source, target, peer):
        buf = fluids if step == STEPS else bufs[step]
        return pltpu.make_async_remote_copy(
            src_ref=buf.at[source],
            dst_ref=buf.at[target],
            send_sem=send_sem.at[step, index],
            recv_sem=recv_sem.at[step, index],
            device_id=(peer,),
            device_id_type=pl.DeviceIdType.MESH,
        )

    def row_copy(source, target, row, sems, arrived, peer):
        return pltpu.make_async_remote_copy(
            src_ref=source,
            dst_ref=target.at[pl.ds(row, 1)],
            send_sem=sems.at[0],
            recv_sem=sems.at[arrived],
            device_id=(peer,),
            device_id_type=pl.DeviceIdType.MESH,
        )

    def rank_at(mine, p):
        return 1 + mine - (mine > p).astype(jnp.int32)

    def wait_rows(part, sem, start, count):
        rows = part.at[pl.ds(start, count)]
        pltpu.make_async_copy(rows, rows, sem).wait()

    def wait_first_stage(later):
        for top, cut in ((0, inner - 2), (1, inner - 1)):

            @pl.when(is_top == top)
            def _(cut=cut):
                if later:
                    wait_rows(part1, sums1.at[2], cut, inner - cut)
                else:
                    wait_rows(part1, sums1.at[1], 1, cut - 1)

    layer = [jnp.zeros((EDGE, LANES), jnp.float32) for _ in range(2)]
    for load in loads:
        load.wait()
    def exchange(step):
        to_ahead = halo(step, 0, OWN, BEHIND, ahead)
        to_behind = halo(step, 1, OWN, AHEAD, behind)
        to_sibling = halo(step, 2, OWN, SIBLING, sibling)
        to_cross = halo(step, 3, OWN, CROSS, cross)
        pl.when(has_ahead)(to_ahead.start)
        pl.when(has_behind)(to_behind.start)
        pl.when(has_behind)(to_cross.start)
        to_sibling.start()
        return (to_ahead, to_behind, to_sibling, to_cross)

    def arrive(to_ahead, to_behind, to_sibling, to_cross):
        to_sibling.wait_recv()
        pl.when(has_ahead)(to_behind.wait_recv)

        @pl.when(has_behind)
        def _():
            to_ahead.wait_recv()
            to_cross.wait_recv()

    def add_layer():
        for yh in range(2):
            layer[yh] = layer[yh] + (2.0 * a[5, yh] + ((a[11, yh] + a[14, yh]) + (a[15, yh] + a[18, yh])))

    exchanges = []
    for step in range(STEPS):
        buf = bufs[step]
        if step == STEPS - 1:
            add_layer()
        if step == STEPS - 1:
            mode = lax.broadcasted_iota(jnp.int32, (MODES, LANES), 0)
            total = jnp.zeros((MODES, LANES), jnp.float32)
            for m in range(MODES):
                product = spread[m, 0] * layer[0] + spread[m, 1] * layer[1]
                total = jnp.where(mode == m, jnp.sum(product, axis=0, keepdims=True), total)
            total = jnp.sum(total, axis=1, keepdims=True)
            at_mode = lax.broadcasted_iota(jnp.int32, (MODES, LANES), 1) == mode
            part1[pl.ds(0, 1), :] = jnp.sum(jnp.where(at_mode, total, 0.0), axis=0, keepdims=True)
            if late:

                @pl.when(is_late)
                def _():
                    rank = 2 * (group // apart) + place - (inner - 2)
                    for device in early:
                        row_copy(part1.at[pl.ds(0, 1)], part3, rank, direct, 1, device).start()

        pack(buf.at[OWN], a, masks)
        if step == 0:
            pack_fluid(fluids.at[OWN], fluid, masks)
            pl.semaphore_wait(barrier, greetings)
            exchanges.append(exchange(STEPS))
        exchanges.append(exchange(step))
        if step < STEPS - 1:
            add_layer()
        else:
            for peer, p in zip(inner_peers, others):
                row_copy(part1.at[pl.ds(0, 1)], part1, rank_at(place, p), sums1, 1 + is_top, peer).start()
        for yh in range(2):
            if step == 0:
                f = fluid[yh]
                squared = vel[0, yh] * vel[0, yh] + vel[1, yh] * vel[1, yh] + vel[2, yh] * vel[2, yh]
                coef[0, yh] = f * (1.0 - relax[yh])
                coef[1, yh] = f * relax[yh] * (1.0 / 12.0)
                coef[2, yh] = (1.0 / 3.0) + 0.5 * squared
        if step == 0:
            load_basis.wait()
            row = lax.broadcasted_iota(jnp.int32, (EDGE, 2 * LANES), 0)
            flat = lax.broadcasted_iota(jnp.int32, (EDGE, 2 * LANES), 1)
            mine = jnp.zeros((EDGE, 2 * LANES), jnp.float32)
            for r in range(NIN):
                mine = jnp.where(row == r, (ids[r] == me).astype(jnp.float32), mine)
            lines = []
            for m in range(MODES):
                line = jnp.sum(basis[m] * mine, axis=0, keepdims=True)
                lines.append(jnp.where(flat // EDGE == row, line, 0.0))
            lines = jnp.concatenate(lines, axis=0)
            q = lax.broadcasted_iota(jnp.int32, (2 * LANES, LANES), 0)
            site = lax.broadcasted_iota(jnp.int32, (2 * LANES, LANES), 1)
            for yh in range(2):
                pick = ((site % EDGE == 0) & (site // EDGE + 8 * yh == q % EDGE)).astype(jnp.float32)
                placed = jnp.dot(lines, pick, precision=lax.Precision.HIGHEST, preferred_element_type=jnp.float32)
                for m in range(MODES):
                    spread[m, yh] = placed[m * EDGE : (m + 1) * EDGE] * (fluid[yh] * (1.0 / 12.0))
        for yh in range(2):
            b[0, yh] = a[0, yh]
        for i in range(1, VELS):
            if step == 0:
                moved = inside((fluid[0], fluid[1]), C[i], masks)
                for yh in range(2):
                    out = beyond(C[i], yh, masks)
                    bits[i - 1, yh] = moved[yh] if out is None else jnp.where(out, 0.0, moved[yh])
            moved = inside((a[i, 0], a[i, 1]), C[i], masks)
            for yh in range(2):
                back = a[OPP[i], yh]
                if C[i][2] == -1:
                    back = back * keep_z
                b[i, yh] = jnp.where(bits[i - 1, yh] > 0.5, moved[yh], back)
        if step == STEPS - 1:
            wait_first_stage(False)
            if late:

                @pl.when(is_split)
                def _():
                    without[...] = jnp.sum(part1[pl.ds(0, inner - 2), :], axis=0, keepdims=True)
                    for g in early_groups:
                        row_copy(without, part2, group, sums2, 1, g * inner + place).start()

            wait_first_stage(True)
            part2[pl.ds(0, 1), :] = jnp.sum(part1[...], axis=0, keepdims=True)
            for t, (peer, g) in enumerate(zip(outer_peers, groups)):
                copy = row_copy(part2.at[pl.ds(0, 1)], part2, rank_at(group, g), sums2, 1, peer)
                if late and t < len(early_groups):
                    pl.when(jnp.logical_not(is_split))(copy.start)
                else:
                    copy.start()
        def ghost(direction, row, rows):
            return buf[slot_of[DIRECTION[direction]], pl.ds(row, rows), :]

        if step == 0:
            arrive(*exchanges[0])

            def ghost_fluid(direction, row, rows):
                k = DIRECTION[direction]
                return fluids[slot_of[k], pl.ds(row, rows), :] * present[k]

            for i in range(1, VELS):
                for (yh, half), value in outside(FLUID, C[i], ghost_fluid, masks).items():
                    rows = slice(HALF * half, HALF * (half + 1))
                    value = jnp.where(beyond(C[i], yh, masks)[rows], value, 0.0)
                    if C[i][2] == -1:
                        value = value * keep_z[rows]
                    ghost_bits[i - 1, yh, pl.ds(HALF * half, HALF), :] = value
        arrive(*exchanges[-1])
        for i in range(1, VELS):
            for (yh, half), value in outside(i, C[i], ghost, masks).items():
                rows = pl.ds(HALF * half, HALF)
                b[i, yh, rows, :] = jnp.where(ghost_bits[i - 1, yh, rows, :] > 0.5, value, b[i, yh, rows, :])
        for yh in range(2):
            for half in range(2):
                rows = pl.ds(HALF * half, HALF)
                new = collide(
                    [b[i, yh, rows, :] for i in range(VELS)],
                    [vel[c, yh, rows, :] for c in range(3)],
                    coef[0, yh, rows, :],
                    coef[1, yh, rows, :],
                    coef[2, yh, rows, :],
                )
                for i in range(VELS):
                    a[i, yh, rows, :] = new[i]

    for to_ahead, to_behind, to_sibling, to_cross in exchanges:
        pl.when(has_ahead)(to_ahead.wait_send)
        pl.when(has_behind)(to_behind.wait_send)
        to_sibling.wait_send()
        pl.when(has_behind)(to_cross.wait_send)
    wait_rows(part1, sums1.at[0], 1, inner - 1)
    wait_rows(part2, sums2.at[0], 1, outer - 1)
    if late:
        pl.when(is_late)(lambda: wait_rows(part3, direct.at[0], 0, len(early)))
    wait_rows(part2, sums2.at[1], 1, outer - 1)
    grad[...] = jnp.sum(part2[...], axis=0, keepdims=True)[:, :MODES]
    if late:

        @pl.when(is_early)
        def _():
            wait_rows(part3, direct.at[1], 0, len(late))
            grad[...] += jnp.sum(part3[pl.ds(0, len(late)), :], axis=0, keepdims=True)[:, :MODES]


def hand_over(parts, state, grad_in, out, grad, sem):
    stores = [pltpu.make_async_copy(grad_in, grad, sem.at[2 * parts])]
    bounds = [VELS * j // parts for j in range(parts + 1)]
    for j in range(parts):
        for yh in range(2):
            rows = pl.ds(bounds[j], bounds[j + 1] - bounds[j])
            stores.append(pltpu.make_async_copy(state.at[rows, yh], out.at[rows, :, yh], sem.at[2 * j + yh]))
    for store in stores:
        store.start()
    for store in stores:
        store.wait()


def on_device(adjoint, velocity, relax, fluid_words, neighbours, inlet_ids, basis):
    n = lax.axis_size("blk")
    inner = 8 if n % 64 == 0 else 4
    outer = n // inner
    f32 = jnp.float32
    shape = (EDGE, 2, LANES)
    any_space = pl.BlockSpec(memory_space=pl.ANY)
    dma = pltpu.SemaphoreType.DMA
    out, grad = pl.pallas_call(
        lambda *refs: body(n, inner, *refs),
        out_shape=(
            pltpu.VMEM((VELS, 2, EDGE, LANES), f32),
            pltpu.VMEM((1, MODES), f32),
        ),
        in_specs=[any_space] * 7,
        out_specs=(pl.BlockSpec(memory_space=pltpu.VMEM), pl.BlockSpec(memory_space=pltpu.VMEM)),
        scratch_shapes=[
            pltpu.VMEM((VELS, 2, EDGE, LANES), f32),
            pltpu.VMEM((3, 2, EDGE, LANES), f32),
            pltpu.VMEM((2, EDGE, LANES), f32),
            pltpu.VMEM((MODES, NIN, 2 * LANES), f32),
            pltpu.VMEM((2, EDGE, LANES), f32),
            pltpu.VMEM((VELS - 1, 2, EDGE, LANES), f32),
            pltpu.VMEM((3, 2, EDGE, LANES), f32),
            pltpu.VMEM((VELS - 1, 2, EDGE, LANES), f32),
            pltpu.VMEM((MODES, 2, EDGE, LANES), f32),
            pltpu.SMEM((1, EDGE * EDGE * EDGE // 32), jnp.int32),
            pltpu.SMEM((1, NEIGHBOURS), jnp.int32),
            pltpu.SMEM((NIN,), jnp.int32),
        ]
        + [pltpu.VMEM((2 * REACH + 1, ROWS, LANES), f32) for _ in range(STEPS)]
        + [
            pltpu.VMEM((2 * REACH + 1, FLUID_ROWS, LANES), f32),
            pltpu.VMEM((inner, LANES), f32),
            pltpu.VMEM((outer, LANES), f32),
            pltpu.VMEM((24, LANES), f32),
            pltpu.VMEM((1, LANES), f32),
            dma((10,)),
            dma((STEPS + 1, 4)),
            dma((STEPS + 1, 4)),
            dma((3,)),
            dma((2,)),
            dma((2,)),
        ],
        compiler_params=pltpu.CompilerParams(collective_id=0, has_side_effects=True),
        name="adjoint_steps",
    )(
        adjoint.reshape((VELS,) + shape),
        velocity.reshape((3,) + shape),
        relax.reshape(shape),
        fluid_words,
        neighbours,
        inlet_ids,
        basis,
    )
    parts = 1
    out, grad = pl.pallas_call(
        functools.partial(hand_over, parts),
        out_shape=(
            jax.ShapeDtypeStruct((VELS,) + shape, f32),
            jax.ShapeDtypeStruct((1, MODES), f32),
        ),
        in_specs=[pl.BlockSpec(memory_space=pltpu.VMEM)] * 2,
        out_specs=(any_space, any_space),
        scratch_shapes=[dma((2 * parts + 1,))],
        name="hand_over",
    )(pltpu.with_memory_space_constraint(out, pltpu.VMEM), pltpu.with_memory_space_constraint(grad, pltpu.VMEM))
    return (out.reshape(1, VELS, EDGE * EDGE * EDGE), grad.reshape(MODES))


def solution(mesh):
    return jax.shard_map(
        on_device,
        mesh=mesh,
        in_specs=(
            P("blk", None, None),
            P("blk", None, None),
            P("blk", None),
            P("blk", None),
            P("blk", None),
            P(),
            P(),
        ),
        out_specs=(P("blk", None, None), P()),
        check_vma=False,
    )
```
